256 devices in a mesh: dom: 16 (over x_hi, y, core), blk: 16 (over z, x_lo).
Axes of the slice: x: 4 (x_hi: 2, x_lo: 2; x = x_hi * 2 + x_lo), y: 4, z: 8, core: 2. Of those that a mesh axis runs over, the one named last changes fastest.
Arguments:
- particles: bfloat16 [32768, 4096], P(('dom', 'blk')), may hold values from -52 to 52
- references: bfloat16 [48, 12, 4096], P('blk'), may hold values from -0.09375 to 0.09375
- noise_weight: float32 [2048], replicated, may hold values from 0.5 to 2
- offsets: int32 [4, 2], replicated, may hold values from -6 to 6
- candidates: int32 [32768, 8], P(('dom', 'blk')), may hold values from 0 to 47, all different within a row
- class_owner: int32 [48], replicated, may hold values from 0 to 15, as said below
Outputs:
- class_means: float32 [128, 4096], P('dom', 'blk')
- class_mass: float32 [128], P('dom')
- log_evidence: float32 [32768], P(('dom', 'blk'))
The draws below stay inside these ranges and needn't reach their ends.
Inputs may be any that keep to these rules, and one draw needn't show every extreme that they name: `class_owner`: each class is owned by one index; no index owns more than 8 classes and one owns exactly 8.
All inputs are finite; a program needn't handle non-finite values.
Results may differ from the reference program's by a relative error of at most 0.004.
Values may be sent and summed in bfloat16 or wider, within the bound.
No kernel may reach another device: no remote copies, remote signals or barrier semaphores. Data moves between devices by JAX's collectives and lax.ppermute only.
A program may use at most 128 MiB of HBM per device.

```python
import math
import jax
import jax.numpy as jnp
from jax import lax

ROT = 12
NSHIFT = 4
KROW = 64
KCOL = 32
BOX = 256
TOPK = 8
SLOTS = 8
K = 2048
CLASSES = 48
PARTICLES = 32768
N_DOM = 16


def draw_particles(key, part):
    first_key = jax.random.fold_in(jax.random.fold_in(key, 11), 0)
    values = jnp.clip(jax.random.normal(first_key, (PARTICLES, 2 * K), jnp.float32), -6.0, 6.0)
    return values.astype(jnp.bfloat16)


def draw_class_owner(key, part):
    first_key, second_key = jax.random.split(jax.random.fold_in(key, 23))
    busiest = jax.random.randint(first_key, (), 0, N_DOM)
    order = jax.random.permutation(second_key, CLASSES)
    index = jnp.arange(CLASSES, dtype=jnp.int32)
    others = (busiest + 1 + (index - SLOTS) % (N_DOM - 1)) % N_DOM
    owners = jnp.where(index < SLOTS, busiest, others).astype(jnp.int32)
    return jnp.zeros((CLASSES,), jnp.int32).at[order].set(owners)


def plant(values, key, smallest, high):
    longest = values.shape.index(max(values.shape))
    spots = []
    for shift in (0, 1):
        where = [jax.random.randint(jax.random.fold_in(key, axis), (), 0, length) for axis, length in enumerate(values.shape)]
        where[longest] = (where[longest] + shift) % values.shape[longest]
        spots.append(tuple(where))
    return values.at[spots[0]].set(smallest).at[spots[1]].set(high)


def levels(key, extent, pieces, smallest, high):
    loudness = 1.0
    for dim, shards_of in pieces:
        steps = jax.random.uniform(jax.random.fold_in(jax.random.fold_in(key, 6), dim), (shards_of,), jnp.float32, smallest / len(pieces), high / len(pieces))
        loudness = loudness * jnp.repeat(jnp.exp(steps), extent[dim] // shards_of).reshape((-1,) + (1,) * (len(extent) - 1 - dim))
    return loudness


def distinct(own_key, rows, count, top, lift):
    sequence = jax.random.permutation(jax.random.fold_in(own_key, 1), count)
    boost = sequence
    for power in range(3):
        boost = boost * boost // count
    boost = boost * lift // count
    lots = jax.random.randint(jax.random.fold_in(own_key, 2), (rows, count), 0, 4096) + boost
    fixed_rows = jax.random.permutation(jax.random.fold_in(own_key, 3), rows)[jnp.arange(count) % rows]
    lots = jnp.where(jnp.arange(rows)[:, None] == fixed_rows[None, :], 1 << 14, lots)
    priority = lots * count + jnp.arange(count)
    return lax.top_k(priority.astype(jnp.int32), top)[1].astype(jnp.int32)


def noise(key, extent, deviation, most, cuts=(), kind=jnp.bfloat16):
    values = jax.random.normal(key, extent, jnp.float32) * deviation
    if len(cuts) > 0:
        values = levels(key, extent, cuts, -0.22, 0.18) * values
    return jnp.clip(values, min=-most, max=most).astype(kind)


def setup_inputs(seed: int = 0) -> dict:
    arg_keys = jax.random.split(jax.random.key(seed), 7)
    return {
        "particles": draw_particles(jax.random.fold_in(arg_keys[6], 71), 0),
        "references": noise(arg_keys[1], (CLASSES, ROT, 2 * K), (2 * K) ** -0.5, 0.09375, ((0, 16),)),
        "noise_weight": jnp.clip(jnp.exp(jax.random.uniform(arg_keys[2], (K,), jnp.float32, math.log(0.5), math.log(2.0))), 0.5, 2.0),
        "offsets": plant(jax.random.randint(arg_keys[3], (NSHIFT, 2), -6, 7), jax.random.fold_in(arg_keys[3], 1), -6, 6).astype(jnp.int32),
        "candidates": distinct(arg_keys[4], PARTICLES, CLASSES, TOPK, 1365),
        "class_owner": draw_class_owner(jax.random.fold_in(arg_keys[6], 71), 0),
    }


INV_TEMP = 4.0


def phase_tables(offsets):
    index = jnp.arange(KROW * KCOL, dtype=jnp.int32)
    column = index % KCOL
    rowpos = index // KCOL - KROW // 2
    turns = (offsets[:, 0:1] * column[None, :] + offsets[:, 1:2] * rowpos[None, :]).astype(jnp.float32)
    angle = turns * (2.0 * math.pi / BOX)
    return jnp.cos(angle), jnp.sin(angle)


def reference(particles, references, noise_weight, offsets, candidates, class_owner):
    half_width = K
    cosine, sine = phase_tables(offsets)
    flat = references.reshape(CLASSES * ROT, 2 * K).astype(jnp.float32)
    ref_real = flat[:, :half_width]
    ref_imag = flat[:, half_width:]
    energy = jnp.sum(noise_weight * (ref_real * ref_real + ref_imag * ref_imag), axis=1).reshape(CLASSES, ROT)
    cos_full = cosine[:, None, :]
    sin_full = sine[:, None, :]
    shifted_real = noise_weight * (cos_full * ref_real - sin_full * ref_imag)
    shifted_imag = noise_weight * (sin_full * ref_real + cos_full * ref_imag)
    table = jnp.concatenate([shifted_real, shifted_imag], axis=2).astype(jnp.bfloat16)
    table = table.astype(jnp.float32).reshape(NSHIFT * CLASSES * ROT, 2 * K)
    allowed = jnp.any(candidates[:, :, None] == jnp.arange(CLASSES, dtype=jnp.int32)[None, None, :], axis=1)
    block_rows = min(512, PARTICLES)
    count_blocks = PARTICLES // block_rows

    def one_block(inputs):
        rows_x, rows_allow = inputs
        values = rows_x.astype(jnp.float32)
        scores = jnp.dot(values, table.T, precision=lax.Precision.HIGHEST)
        scores = scores.reshape(block_rows, NSHIFT, CLASSES, ROT)
        loglik = INV_TEMP * (scores - 0.5 * energy[None, None])
        wanted = rows_allow[:, None, :, None]
        peak = jnp.max(jnp.where(wanted, loglik, -jnp.inf), axis=(1, 2, 3))
        terms = jnp.sum(jnp.where(wanted, jnp.exp(loglik - peak[:, None, None, None]), 0.0), axis=3)
        evidence = jnp.sum(terms, axis=(1, 2))
        log_ev = peak + jnp.log(evidence)
        probs = terms / evidence[:, None, None]
        mass = jnp.sum(probs, axis=(0, 1))
        probs_low = probs.astype(jnp.bfloat16).astype(jnp.float32)
        gathered = jnp.einsum('psc,pk->sck', probs_low, values, precision=lax.Precision.HIGHEST)
        g_real = gathered[:, :, :half_width]
        g_imag = gathered[:, :, half_width:]
        part_real = jnp.sum(cos_full * g_real + sin_full * g_imag, axis=0)
        part_imag = jnp.sum(cos_full * g_imag - sin_full * g_real, axis=0)
        return log_ev, jnp.concatenate([part_real, part_imag], axis=1), mass

    log_ev, parts, masses = lax.map(one_block, (particles.reshape(count_blocks, block_rows, 2 * K),
                                                 allowed.reshape(count_blocks, block_rows, CLASSES)))
    class_part = jnp.sum(parts, axis=0)
    mass = jnp.sum(masses, axis=0)
    class_ids = jnp.arange(CLASSES, dtype=jnp.int32)
    shared_owner = class_owner[:, None] == class_owner[None, :]
    earlier = class_ids[:, None] < class_ids[None, :]
    position = jnp.sum((shared_owner & earlier).astype(jnp.int32), axis=0)
    target = class_owner * SLOTS + position
    placement = (jnp.arange(N_DOM * SLOTS, dtype=jnp.int32)[:, None] == target[None, :]).astype(jnp.float32)
    owned = jnp.dot(placement, class_part, precision=lax.Precision.HIGHEST)
    owned_mass = jnp.dot(placement, mass, precision=lax.Precision.HIGHEST)
    means = owned / (owned_mass[:, None] + 1.0)
    return means, owned_mass, log_ev.reshape(PARTICLES)
```

```python
import math

import jax
import jax.numpy as jnp
import numpy as np
from jax import lax
from jax.experimental import pallas as pl
from jax.experimental.pallas import tpu as pltpu
from jax.sharding import Mesh, PartitionSpec as P

KROW = 64
KCOL = 32
BOX = 256
SLOTS = 8
INV_TEMP = 4.0
FLOOR = -1e30

FINE = (("xh", 2), ("yh", 2), ("yl", 2), ("core", 2), ("z", 8), ("xl", 2))
DOM = ("xh", "yh", "yl", "core")
BLK = ("z", "xl")
POOL = ("yl", "core")

K = 2048
CLASSES = 48
ROT = 12
NSHIFT = 4
ROWS = 128
NPOOL = 4
QROT = ROT // NPOOL
QCLS = CLASSES // NPOOL
NBLK = 16
NDOM = 16
LOCAL = 3
COLS = 256
F32 = jnp.float32
BF16 = jnp.bfloat16
VMEM = pltpu.VMEM
SMEM_SPEC = pl.BlockSpec(memory_space=pltpu.SMEM)
VMEM_SPEC = pl.BlockSpec(memory_space=pltpu.VMEM)
ANY_SPEC = pl.BlockSpec(memory_space=pl.ANY)


def params(mib):
    return pltpu.CompilerParams(vmem_limit_bytes=mib << 20)


def pack_kernel(q_ref, refs_ref, out_ref, wide, rows):
    q = q_ref[0]
    wide[...] = refs_ref[...].astype(F32)
    for c in range(LOCAL):
        for r in range(QROT):
            row = wide[c, pl.ds(QROT * q + r, 1), :]
            for a in range(32):
                at = (c * QROT + r) * 32 + a
                rows[at : at + 1, :] = row[:, a * 128 : (a + 1) * 128]
    packed = rows[...].astype(BF16)
    for d in range(NBLK):
        out_ref[d] = packed


def pool_copies(q, parts, pool, sem):
    copies = []
    for j, part in enumerate(parts):
        start = pl.multiple_of((q ^ j) * ROWS, ROWS)
        copies.append(pltpu.make_async_copy(part, pool.at[pl.ds(start, ROWS), :], sem.at[j]))
    return copies


def score_kernel(
    q_ref, refs_ref, p0, p1, p2, p3, wc_ref, ws_ref, w_ref, cand_ref, out_ref, wide, table, pool, sem
):
    q = q_ref[0]
    copies = pool_copies(q, (p0, p1, p2, p3), pool, sem)
    for copy in copies:
        copy.start()
    wide[...] = refs_ref[...].astype(F32)
    energy = [jnp.zeros((CLASSES, 128), F32) for _ in range(QROT)]
    stride = QROT * 32
    for a in range(16):
        weight = w_ref[a : a + 1, :]
        for r in range(QROT):
            real = wide[pl.ds(r * 32 + a, CLASSES, stride=stride), :]
            imag = wide[pl.ds(r * 32 + 16 + a, CLASSES, stride=stride), :]
            energy[r] = energy[r] + weight * (real * real + imag * imag)
            for s in range(NSHIFT):
                wc = wc_ref[s * 16 + a : s * 16 + a + 1, :]
                ws = ws_ref[s * 16 + a : s * 16 + a + 1, :]
                row = (s * QROT + r) * CLASSES
                table[row : row + CLASSES, a * 128 : (a + 1) * 128] = (wc * real - ws * imag).astype(BF16)
                table[row : row + CLASSES, K + a * 128 : K + (a + 1) * 128] = (ws * real + wc * imag).astype(BF16)
    half_energy = [0.5 * jnp.sum(e, axis=1, keepdims=True) for e in energy]
    for copy in copies:
        copy.wait()
    class_id = lax.broadcasted_iota(jnp.int32, (CLASSES, 256), 0)
    for n in range(2):
        lanes = slice(n * 256, (n + 1) * 256)
        scores = lax.dot_general(
            table[...], pool[lanes, :], (((1,), (1,)), ((), ())), preferred_element_type=F32
        )
        cand = jnp.concatenate([cand_ref[2 * n], cand_ref[2 * n + 1]], axis=1)
        allowed = class_id == cand[0:1, :]
        for k in range(1, 8):
            allowed = allowed | (class_id == cand[k : k + 1, :])
        loglik = []
        for s in range(NSHIFT):
            for r in range(QROT):
                row = (s * QROT + r) * CLASSES
                value = INV_TEMP * (scores[row : row + CLASSES] - half_energy[r])
                loglik.append(jnp.where(allowed, value, FLOOR))
        top = loglik[0]
        for value in loglik[1:]:
            top = jnp.maximum(top, value)
        peak = jnp.max(top, axis=0, keepdims=True)
        evidence = jnp.zeros((1, 256), F32)
        for s in range(NSHIFT):
            terms = jnp.zeros((CLASSES, 256), F32)
            for r in range(QROT):
                value = loglik[s * QROT + r]
                terms = terms + jnp.where(allowed, jnp.exp(value - peak), 0.0)
            evidence = evidence + jnp.sum(terms, axis=0, keepdims=True)
            for d in range(NPOOL):
                out_ref[d, s * QCLS : (s + 1) * QCLS, lanes] = terms[d * QCLS : (d + 1) * QCLS]
        for d in range(NPOOL):
            out_ref[d, 48:49, lanes] = peak
            out_ref[d, 49:50, lanes] = evidence
            out_ref[d, 50:56, lanes] = jnp.zeros((6, 256), F32)


def class_kernel(
    q_ref, x_ref, p0, p1, p2, p3, cos_ref, sin_ref, out_ref, log_ref, pool, slots, line, sem
):
    q = q_ref[0]
    copies = pool_copies(q, (p0, p1, p2, p3), pool, sem)
    for copy in copies:
        copy.start()
    peak = x_ref[0, 48:49, :]
    for j in range(1, NPOOL):
        peak = jnp.maximum(peak, x_ref[j, 48:49, :])
    evidence = jnp.zeros_like(peak)
    terms = jnp.zeros((NSHIFT * QCLS, NPOOL * ROWS), F32)
    for j in range(NPOOL):
        scale = jnp.exp(x_ref[j, 48:49, :] - peak)
        evidence = evidence + scale * x_ref[j, 49:50, :]
        terms = terms + scale * x_ref[j, 0:48, :]
    line[...] = peak + jnp.log(evidence)
    log_ref[...] = line[:, pl.ds(pl.multiple_of(q * ROWS, ROWS), ROWS)]
    probs = terms / evidence
    for s in range(NSHIFT):
        slots[s * 16 : s * 16 + QCLS, :] = probs[s * QCLS : (s + 1) * QCLS]
        slots[s * 16 + QCLS : (s + 1) * 16, :] = jnp.zeros((4, NPOOL * ROWS), F32)
    padded = slots[...]
    mass = jnp.sum(padded, axis=1, keepdims=True)
    mass = mass[0:16] + mass[16:32] + mass[32:48] + mass[48:64]
    low = padded.astype(BF16)
    row_id = lax.broadcasted_iota(jnp.int32, (16, COLS), 0)
    lane_id = lax.broadcasted_iota(jnp.int32, (16, COLS), 1)
    mass_row = jnp.sum(jnp.where(row_id == lane_id, mass, 0.0), axis=0, keepdims=True)
    mass_high = mass_row.astype(BF16).astype(F32)
    mass_low = mass_row - mass_high
    for copy in copies:
        copy.wait()
    for b in range(NBLK // 2):
        cols = slice(b * COLS, (b + 1) * COLS)
        cols_im = slice(K + b * COLS, K + (b + 1) * COLS)
        g_re = jnp.dot(low, pool[:, cols], preferred_element_type=F32)
        g_im = jnp.dot(low, pool[:, cols_im], preferred_element_type=F32)
        sum_re = jnp.zeros((16, COLS), F32)
        sum_im = jnp.zeros((16, COLS), F32)
        for s in range(NSHIFT):
            c = cos_ref[s : s + 1, cols]
            z = sin_ref[s : s + 1, cols]
            re = g_re[s * 16 : (s + 1) * 16]
            im = g_im[s * 16 : (s + 1) * 16]
            sum_re = sum_re + (c * re + z * im)
            sum_im = sum_im + (c * im - z * re)
        for dest, value in ((b, sum_re), (NBLK // 2 + b, sum_im)):
            value = jnp.where(row_id == QCLS, mass_high, value)
            value = jnp.where(row_id == QCLS + 1, mass_low, value)
            out_ref[dest] = value.astype(BF16)


def place_kernel(target_ref, y_ref, out_ref):
    total = y_ref[0].astype(F32)
    for b in range(1, NBLK):
        total = total + y_ref[b].astype(F32)
    mass = total[QCLS : QCLS + 1, 0:128] + total[QCLS + 1 : QCLS + 2, 0:128]
    row = lax.broadcasted_iota(jnp.int32, (NDOM * 16, 128), 0)
    slot = row % 16
    wanted = (row // 16) * SLOTS + slot % 8
    hit = target_ref[...] == wanted
    pick = jnp.where(hit & (slot < 8), 1.0, 0.0).astype(BF16)
    placed = jnp.dot(pick[:, 0:16], total.astype(BF16), preferred_element_type=F32)
    placed_mass = jnp.sum(jnp.where(hit & (slot >= 8), mass, 0.0), axis=1, keepdims=True)
    high = placed_mass.astype(BF16).astype(F32)
    lane = lax.broadcasted_iota(jnp.int32, (NDOM * 16, COLS), 1)
    extra = jnp.where(lane == 0, high, jnp.where(lane == 1, placed_mass - high, 0.0))
    out = (placed + extra).astype(BF16)
    out_ref[...] = out.reshape(NDOM, 16, COLS)


def mean_kernel(z_ref, mean_ref, mass_ref):
    total = z_ref[0].astype(F32)
    for d in range(1, NDOM):
        total = total + z_ref[d].astype(F32)
    mass = total[8:16, 0:1] + total[8:16, 1:2]
    mean_ref[...] = total[0:8] / (mass + 1.0)
    mass_ref[...] = jnp.broadcast_to(mass, (SLOTS, 128))


def phase_tables(offsets):
    index = jnp.arange(KROW * KCOL, dtype=jnp.int32)
    column = index % KCOL
    rowpos = index // KCOL - KROW // 2
    turns = (offsets[:, 0:1] * column[None, :] + offsets[:, 1:2] * rowpos[None, :]).astype(F32)
    angle = turns * (2.0 * math.pi / BOX)
    return (jnp.cos(angle), jnp.sin(angle))


def swap(x, axis):
    return lax.ppermute(x, axis, [(0, 1), (1, 0)])


def on_device(particles, references, noise_weight, offsets, candidates, class_owner):
    pool_index = (lax.axis_index("yl") * 2 + lax.axis_index("core")).astype(jnp.int32)
    q = pool_index.reshape(1)

    far = swap(particles, "yl")
    packed = pl.pallas_call(
        pack_kernel,
        out_shape=jax.ShapeDtypeStruct((NBLK, LOCAL * QROT * 32, 128), BF16),
        in_specs=[SMEM_SPEC, VMEM_SPEC],
        out_specs=VMEM_SPEC,
        scratch_shapes=[VMEM((LOCAL, ROT, 2 * K), F32), VMEM((LOCAL * QROT * 32, 128), F32)],
        compiler_params=params(16),
        name="pack",
    )(q, references)
    gathered = lax.all_to_all(packed, BLK, 0, 0, tiled=True)
    near = swap(particles, "core")
    far_near = swap(far, "core")
    pool = (particles, near, far, far_near)

    cand = lax.all_gather(candidates.T, POOL, axis=0, tiled=False)
    cosine, sine = phase_tables(offsets)
    wc = (noise_weight * cosine).reshape(NSHIFT * 16, 128)
    ws = (noise_weight * sine).reshape(NSHIFT * 16, 128)
    weight = noise_weight.reshape(16, 128)

    copies = pltpu.SemaphoreType.DMA((NPOOL,))
    pool_shape = VMEM((NPOOL * ROWS, 2 * K), BF16)
    terms = pl.pallas_call(
        score_kernel,
        out_shape=jax.ShapeDtypeStruct((NPOOL, 56, NPOOL * ROWS), F32),
        in_specs=[SMEM_SPEC, VMEM_SPEC] + [ANY_SPEC] * 4 + [VMEM_SPEC] * 4,
        out_specs=VMEM_SPEC,
        scratch_shapes=[
            VMEM((NBLK * LOCAL * QROT * 32, 128), F32),
            VMEM((NSHIFT * QROT * CLASSES, 2 * K), BF16),
            pool_shape,
            copies,
        ],
        compiler_params=params(40),
        name="score",
    )(q, gathered.reshape(NBLK * LOCAL * QROT * 32, 128), *pool, wc, ws, weight, cand)
    terms = lax.all_to_all(terms, POOL, 0, 0, tiled=True)

    sums, log_evidence = pl.pallas_call(
        class_kernel,
        out_shape=(
            jax.ShapeDtypeStruct((NBLK, 16, COLS), BF16),
            jax.ShapeDtypeStruct((1, ROWS), F32),
        ),
        in_specs=[SMEM_SPEC, VMEM_SPEC] + [ANY_SPEC] * 4 + [VMEM_SPEC] * 2,
        out_specs=(VMEM_SPEC, VMEM_SPEC),
        scratch_shapes=[
            pool_shape,
            VMEM((NSHIFT * 16, NPOOL * ROWS), F32),
            VMEM((1, NPOOL * ROWS), F32),
            copies,
        ],
        compiler_params=params(24),
        name="classes",
    )(q, terms, *pool, cosine, sine)
    sums = lax.all_to_all(sums, BLK, 0, 0, tiled=True)

    class_ids = jnp.arange(CLASSES, dtype=jnp.int32)
    shared_owner = class_owner[:, None] == class_owner[None, :]
    earlier = class_ids[:, None] < class_ids[None, :]
    position = jnp.sum((shared_owner & earlier).astype(jnp.int32), axis=0)
    target = class_owner * SLOTS + position
    mine = lax.dynamic_slice(target, (pool_index * QCLS,), (QCLS,))
    mine = jnp.pad(mine, (0, 128 - QCLS), constant_values=-1).reshape(1, 128)
    placed = pl.pallas_call(
        place_kernel,
        out_shape=jax.ShapeDtypeStruct((NDOM, 16, COLS), BF16),
        in_specs=[VMEM_SPEC, VMEM_SPEC],
        out_specs=VMEM_SPEC,
        name="place",
    )(mine, sums)
    placed = lax.all_to_all(placed, DOM, 0, 0, tiled=True)
    means, mass = pl.pallas_call(
        mean_kernel,
        out_shape=(
            jax.ShapeDtypeStruct((SLOTS, COLS), F32),
            jax.ShapeDtypeStruct((SLOTS, 128), F32),
        ),
        in_specs=[VMEM_SPEC],
        out_specs=(VMEM_SPEC, VMEM_SPEC),
        name="means",
    )(placed)
    return (means, mass[:, 0], log_evidence.reshape(ROWS))


def solution(mesh):
    fine = Mesh(
        np.asarray(mesh.devices).reshape([size for _, size in FINE]), [name for name, _ in FINE]
    )
    every = DOM + BLK
    return jax.shard_map(
        on_device,
        mesh=fine,
        in_specs=(P(every, None), P(BLK, None, None), P(), P(), P(every, None), P()),
        out_specs=(P(DOM, BLK), P(DOM), P(every)),
        check_vma=False,
    )
```

```python
import math

import jax
import jax.numpy as jnp
import numpy as np
from jax import lax
from jax.experimental import pallas as pl
from jax.experimental.pallas import tpu as pltpu
from jax.sharding import Mesh, PartitionSpec as P

KROW = 64
KCOL = 32
BOX = 256
SLOTS = 8
INV_TEMP = 4.0
FLOOR = -1e30

FINE = (("xh", 2), ("yh", 2), ("yl", 2), ("core", 2), ("z", 8), ("xl", 2))
DOM = ("xh", "yh", "yl", "core")
BLK = ("z", "xl")
POOL = ("yl", "core")

K = 2048
CLASSES = 48
ROT = 12
NSHIFT = 4
ROWS = 128
NPOOL = 4
QROT = ROT // NPOOL
QCLS = CLASSES // NPOOL
NBLK = 16
NDOM = 16
LOCAL = 3
COLS = 256
F32 = jnp.float32
BF16 = jnp.bfloat16
VMEM = pltpu.VMEM
SMEM_SPEC = pl.BlockSpec(memory_space=pltpu.SMEM)
VMEM_SPEC = pl.BlockSpec(memory_space=pltpu.VMEM)
ANY_SPEC = pl.BlockSpec(memory_space=pl.ANY)


def params(mib):
    return pltpu.CompilerParams(vmem_limit_bytes=mib << 20)


def pack_kernel(q_ref, refs_ref, out_ref, wide, rows):
    q = q_ref[0]
    wide[...] = refs_ref[...].astype(F32)
    for c in range(LOCAL):
        for r in range(QROT):
            row = wide[c, pl.ds(QROT * q + r, 1), :]
            for a in range(32):
                at = (c * QROT + r) * 32 + a
                rows[at : at + 1, :] = row[:, a * 128 : (a + 1) * 128]
    packed = rows[...].astype(BF16)
    for d in range(NBLK):
        out_ref[d] = packed


def pool_copies(q, parts, pool, sem):
    copies = []
    for j, part in enumerate(parts):
        start = pl.multiple_of((q ^ j) * ROWS, ROWS)
        copies.append(pltpu.make_async_copy(part, pool.at[pl.ds(start, ROWS), :], sem.at[j]))
    return copies


def score_kernel(
    q_ref, refs_ref, p0, p1, p2, p3, wc_ref, ws_ref, w_ref, c0_ref, c1_ref, c23_ref, out_hbm,
    wide, table, pool, cands, out_ref, sem, out_sem
):
    q = q_ref[0]
    copies = pool_copies(q, (p0, p1, p2, p3), pool, sem)
    for copy in copies:
        copy.start()
    for j, cand in enumerate((c0_ref[...], c23_ref[0], c1_ref[...], c23_ref[1])):
        cands[:, pl.ds(pl.multiple_of((q ^ j) * ROWS, ROWS), ROWS)] = cand
    wide[...] = refs_ref[...].astype(F32)
    energy = [jnp.zeros((CLASSES, 128), F32) for _ in range(QROT)]
    stride = QROT * 32
    for a in range(16):
        weight = w_ref[a : a + 1, :]
        for r in range(QROT):
            real = wide[pl.ds(r * 32 + a, CLASSES, stride=stride), :]
            imag = wide[pl.ds(r * 32 + 16 + a, CLASSES, stride=stride), :]
            energy[r] = energy[r] + weight * (real * real + imag * imag)
            for s in range(NSHIFT):
                wc = wc_ref[s * 16 + a : s * 16 + a + 1, :]
                ws = ws_ref[s * 16 + a : s * 16 + a + 1, :]
                row = (s * QROT + r) * CLASSES
                table[row : row + CLASSES, a * 128 : (a + 1) * 128] = (wc * real - ws * imag).astype(BF16)
                table[row : row + CLASSES, K + a * 128 : K + (a + 1) * 128] = (ws * real + wc * imag).astype(BF16)
    half_energy = [0.5 * jnp.sum(e, axis=1, keepdims=True) for e in energy]
    for copy in copies:
        copy.wait()
    class_id = lax.broadcasted_iota(jnp.int32, (CLASSES, 256), 0)
    sends = []
    for n in range(2):
        lanes = slice(n * 256, (n + 1) * 256)
        scores = lax.dot_general(
            table[...], pool[lanes, :], (((1,), (1,)), ((), ())), preferred_element_type=F32
        )
        cand = cands[:, lanes]
        allowed = class_id == cand[0:1, :]
        for k in range(1, 8):
            allowed = allowed | (class_id == cand[k : k + 1, :])
        loglik = []
        for s in range(NSHIFT):
            for r in range(QROT):
                row = (s * QROT + r) * CLASSES
                value = INV_TEMP * (scores[row : row + CLASSES] - half_energy[r])
                loglik.append(jnp.where(allowed, value, FLOOR))
        top = loglik[0]
        for value in loglik[1:]:
            top = jnp.maximum(top, value)
        peak = jnp.max(top, axis=0, keepdims=True)
        evidence = jnp.zeros((1, 256), F32)
        for s in range(NSHIFT):
            terms = jnp.zeros((CLASSES, 256), F32)
            for r in range(QROT):
                value = loglik[s * QROT + r]
                terms = terms + jnp.where(allowed, jnp.exp(value - peak), 0.0)
            evidence = evidence + jnp.sum(terms, axis=0, keepdims=True)
            for d in range(NPOOL):
                out_ref[d, s * QCLS : (s + 1) * QCLS, lanes] = terms[d * QCLS : (d + 1) * QCLS]
        for d in range(NPOOL):
            out_ref[d, 48:49, lanes] = peak
            out_ref[d, 49:50, lanes] = evidence
            out_ref[d, 50:56, lanes] = jnp.zeros((6, 256), F32)
        send = pltpu.make_async_copy(out_ref.at[:, :, lanes], out_hbm.at[:, :, lanes], out_sem.at[n])
        send.start()
        sends.append(send)
    for send in sends:
        send.wait()


def class_kernel(
    q_ref, x_ref, p0, p1, p2, p3, cos_ref, sin_ref, out_ref, log_ref, pool, slots, line, sem
):
    q = q_ref[0]
    copies = pool_copies(q, (p0, p1, p2, p3), pool, sem)
    for copy in copies:
        copy.start()
    peak = x_ref[0, 48:49, :]
    for j in range(1, NPOOL):
        peak = jnp.maximum(peak, x_ref[j, 48:49, :])
    evidence = jnp.zeros_like(peak)
    terms = jnp.zeros((NSHIFT * QCLS, NPOOL * ROWS), F32)
    for j in range(NPOOL):
        scale = jnp.exp(x_ref[j, 48:49, :] - peak)
        evidence = evidence + scale * x_ref[j, 49:50, :]
        terms = terms + scale * x_ref[j, 0:48, :]
    line[...] = peak + jnp.log(evidence)
    log_ref[...] = line[:, pl.ds(pl.multiple_of(q * ROWS, ROWS), ROWS)]
    probs = terms / evidence
    for s in range(NSHIFT):
        slots[s * 16 : s * 16 + QCLS, :] = probs[s * QCLS : (s + 1) * QCLS]
        slots[s * 16 + QCLS : (s + 1) * 16, :] = jnp.zeros((4, NPOOL * ROWS), F32)
    padded = slots[...]
    mass = jnp.sum(padded, axis=1, keepdims=True)
    mass = mass[0:16] + mass[16:32] + mass[32:48] + mass[48:64]
    low = padded.astype(BF16)
    row_id = lax.broadcasted_iota(jnp.int32, (16, COLS), 0)
    lane_id = lax.broadcasted_iota(jnp.int32, (16, COLS), 1)
    mass_row = jnp.sum(jnp.where(row_id == lane_id, mass, 0.0), axis=0, keepdims=True)
    mass_high = mass_row.astype(BF16).astype(F32)
    mass_low = mass_row - mass_high
    for copy in copies:
        copy.wait()
    for b in range(NBLK // 2):
        cols = slice(b * COLS, (b + 1) * COLS)
        cols_im = slice(K + b * COLS, K + (b + 1) * COLS)
        g_re = jnp.dot(low, pool[:, cols], preferred_element_type=F32)
        g_im = jnp.dot(low, pool[:, cols_im], preferred_element_type=F32)
        sum_re = jnp.zeros((16, COLS), F32)
        sum_im = jnp.zeros((16, COLS), F32)
        for s in range(NSHIFT):
            c = cos_ref[s : s + 1, cols]
            z = sin_ref[s : s + 1, cols]
            re = g_re[s * 16 : (s + 1) * 16]
            im = g_im[s * 16 : (s + 1) * 16]
            sum_re = sum_re + (c * re + z * im)
            sum_im = sum_im + (c * im - z * re)
        for dest, value in ((b, sum_re), (NBLK // 2 + b, sum_im)):
            value = jnp.where(row_id == QCLS, mass_high, value)
            value = jnp.where(row_id == QCLS + 1, mass_low, value)
            out_ref[dest] = value.astype(BF16)


def place_kernel(target_ref, y_ref, out_hbm, out_ref, sem):
    total = y_ref[0].astype(F32)
    for b in range(1, NBLK):
        total = total + y_ref[b].astype(F32)
    mass = total[QCLS : QCLS + 1, 0:128] + total[QCLS + 1 : QCLS + 2, 0:128]
    row = lax.broadcasted_iota(jnp.int32, (NDOM * SLOTS, 128), 0)
    hit = target_ref[...] == row
    pick = jnp.where(hit, 1.0, 0.0).astype(BF16)
    placed = jnp.dot(pick[:, 0:16], total.astype(BF16), preferred_element_type=F32)
    placed_mass = jnp.sum(jnp.where(hit, mass, 0.0), axis=1, keepdims=True)
    high = placed_mass.astype(BF16).astype(F32)
    lane = lax.broadcasted_iota(jnp.int32, (NDOM * SLOTS, 128), 1)
    extra = jnp.where(lane == 0, high, jnp.where(lane == 1, placed_mass - high, 0.0))
    out_ref[:, :, 0:COLS] = placed.reshape(NDOM, SLOTS, COLS).astype(BF16)
    out_ref[:, :, COLS:] = extra.reshape(NDOM, SLOTS, 128).astype(BF16)
    send = pltpu.make_async_copy(out_ref, out_hbm, sem)
    send.start()
    send.wait()


def mean_kernel(z_ref, mean_ref, mass_ref):
    total = z_ref[0].astype(F32)
    for d in range(1, NDOM):
        total = total + z_ref[d].astype(F32)
    mass = total[:, COLS : COLS + 1] + total[:, COLS + 1 : COLS + 2]
    mean_ref[...] = total[:, 0:COLS] / (mass + 1.0)
    row = lax.broadcasted_iota(jnp.int32, (SLOTS, 128), 0)
    lane = lax.broadcasted_iota(jnp.int32, (SLOTS, 128), 1)
    mass_ref[...] = jnp.sum(jnp.where(row == lane, mass, 0.0), axis=0)[0:SLOTS]


def phase_tables(offsets):
    index = jnp.arange(KROW * KCOL, dtype=jnp.int32)
    column = index % KCOL
    rowpos = index // KCOL - KROW // 2
    turns = (offsets[:, 0:1] * column[None, :] + offsets[:, 1:2] * rowpos[None, :]).astype(F32)
    angle = turns * (2.0 * math.pi / BOX)
    return (jnp.cos(angle), jnp.sin(angle))


def swap(x, axis):
    return lax.ppermute(x, axis, [(0, 1), (1, 0)])


def on_device(particles, references, noise_weight, offsets, candidates, class_owner):
    pool_index = (lax.axis_index("yl") * 2 + lax.axis_index("core")).astype(jnp.int32)
    q = pool_index.reshape(1)

    far = swap(particles, "yl")
    packed = pl.pallas_call(
        pack_kernel,
        out_shape=jax.ShapeDtypeStruct((NBLK, LOCAL * QROT * 32, 128), BF16),
        in_specs=[SMEM_SPEC, VMEM_SPEC],
        out_specs=VMEM_SPEC,
        scratch_shapes=[VMEM((LOCAL, ROT, 2 * K), F32), VMEM((LOCAL * QROT * 32, 128), F32)],
        compiler_params=params(16),
        name="pack",
    )(q, references)
    gathered = lax.all_to_all(packed, BLK, 0, 0, tiled=True)
    near = swap(particles, "core")
    cand = candidates.T
    cand_far = swap(cand, "yl")
    cand_near = swap(jnp.stack([cand, cand_far]), "core")
    far, cand_near = lax.optimization_barrier((far, cand_near))
    far_near = swap(far, "core")
    pool = (particles, near, far, far_near)

    cosine, sine = phase_tables(offsets)
    wc = (noise_weight * cosine).reshape(NSHIFT * 16, 128)
    ws = (noise_weight * sine).reshape(NSHIFT * 16, 128)
    weight = noise_weight.reshape(16, 128)

    copies = pltpu.SemaphoreType.DMA((NPOOL,))
    pool_shape = VMEM((NPOOL * ROWS, 2 * K), BF16)
    terms = pl.pallas_call(
        score_kernel,
        out_shape=pltpu.HBM((NPOOL, 56, NPOOL * ROWS), F32),
        in_specs=[SMEM_SPEC, VMEM_SPEC] + [ANY_SPEC] * 4 + [VMEM_SPEC] * 6,
        out_specs=pl.BlockSpec(memory_space=pltpu.HBM),
        scratch_shapes=[
            VMEM((NBLK * LOCAL * QROT * 32, 128), F32),
            VMEM((NSHIFT * QROT * CLASSES, 2 * K), BF16),
            pool_shape,
            VMEM((8, NPOOL * ROWS), jnp.int32),
            VMEM((NPOOL, 56, NPOOL * ROWS), F32),
            copies,
            pltpu.SemaphoreType.DMA((2,)),
        ],
        compiler_params=params(40),
        name="score",
    )(q, gathered.reshape(NBLK * LOCAL * QROT * 32, 128), *pool, wc, ws, weight, cand, cand_far, cand_near)
    terms = lax.all_to_all(terms, POOL, 0, 0, tiled=True)

    sums, log_evidence = pl.pallas_call(
        class_kernel,
        out_shape=(
            jax.ShapeDtypeStruct((NBLK, 16, COLS), BF16),
            jax.ShapeDtypeStruct((1, ROWS), F32),
        ),
        in_specs=[SMEM_SPEC, VMEM_SPEC] + [ANY_SPEC] * 4 + [VMEM_SPEC] * 2,
        out_specs=(VMEM_SPEC, VMEM_SPEC),
        scratch_shapes=[
            pool_shape,
            VMEM((NSHIFT * 16, NPOOL * ROWS), F32),
            VMEM((1, NPOOL * ROWS), F32),
            copies,
        ],
        compiler_params=params(24),
        name="classes",
    )(q, terms, *pool, cosine, sine)
    sums = lax.all_to_all(sums, BLK, 0, 0, tiled=True)

    class_ids = jnp.arange(CLASSES, dtype=jnp.int32)
    shared_owner = class_owner[:, None] == class_owner[None, :]
    earlier = class_ids[:, None] < class_ids[None, :]
    position = jnp.sum((shared_owner & earlier).astype(jnp.int32), axis=0)
    target = class_owner * SLOTS + position
    mine = lax.dynamic_slice(target, (pool_index * QCLS,), (QCLS,))
    mine = jnp.pad(mine, (0, 128 - QCLS), constant_values=-1).reshape(1, 128)
    placed = pl.pallas_call(
        place_kernel,
        out_shape=pltpu.HBM((NDOM, SLOTS, COLS + 128), BF16),
        in_specs=[VMEM_SPEC, VMEM_SPEC],
        out_specs=pl.BlockSpec(memory_space=pltpu.HBM),
        scratch_shapes=[VMEM((NDOM, SLOTS, COLS + 128), BF16), pltpu.SemaphoreType.DMA],
        compiler_params=params(4),
        name="place",
    )(mine, sums)
    placed = lax.all_to_all(placed, DOM, 0, 0, tiled=True)
    means, mass = pl.pallas_call(
        mean_kernel,
        out_shape=(
            jax.ShapeDtypeStruct((SLOTS, COLS), F32),
            jax.ShapeDtypeStruct((SLOTS,), F32),
        ),
        in_specs=[VMEM_SPEC],
        out_specs=(VMEM_SPEC, VMEM_SPEC),
        compiler_params=params(4),
        name="means",
    )(placed)
    return (means, mass, log_evidence.reshape(ROWS))


def solution(mesh):
    fine = Mesh(
        np.asarray(mesh.devices).reshape([size for _, size in FINE]), [name for name, _ in FINE]
    )
    every = DOM + BLK
    return jax.shard_map(
        on_device,
        mesh=fine,
        in_specs=(P(every, None), P(BLK, None, None), P(), P(), P(every, None), P()),
        out_specs=(P(DOM, BLK), P(DOM), P(every)),
        check_vma=False,
    )
```

```python
import math

import jax
import jax.numpy as jnp
import numpy as np
from jax import lax
from jax.experimental import pallas as pl
from jax.experimental.pallas import tpu as pltpu
from jax.sharding import Mesh, PartitionSpec as P

KROW = 64
KCOL = 32
BOX = 256
SLOTS = 8
INV_TEMP = 4.0
FLOOR = -1e30

FINE = (("xh", 2), ("yh", 2), ("yl", 2), ("core", 2), ("z", 8), ("xl", 2))
DOM = ("xh", "yh", "yl", "core")
BLK = ("z", "xl")
POOL = ("yl", "core")

K = 2048
CLASSES = 48
ROT = 12
NSHIFT = 4
ROWS = 128
HALF = ROWS // 2
NPOOL = 4
QROT = ROT // NPOOL
QCLS = CLASSES // NPOOL
NBLK = 16
NDOM = 16
LOCAL = 3
COLS = 256
STEP_TILES = 4
F32 = jnp.float32
BF16 = jnp.bfloat16
VMEM = pltpu.VMEM
SMEM_SPEC = pl.BlockSpec(memory_space=pltpu.SMEM)
VMEM_SPEC = pl.BlockSpec(memory_space=pltpu.VMEM)
ANY_SPEC = pl.BlockSpec(memory_space=pl.ANY)


def params(mib):
    return pltpu.CompilerParams(vmem_limit_bytes=mib << 20)


def pack_kernel(q_ref, refs_ref, out_ref, wide, rows):
    q = q_ref[0]
    wide[...] = refs_ref[...].astype(F32)
    for c in range(LOCAL):
        for r in range(QROT):
            row = wide[c, pl.ds(QROT * q + r, 1), :]
            for a in range(32):
                at = (c * QROT + r) * 32 + a
                rows[at : at + 1, :] = row[:, a * 128 : (a + 1) * 128]
    packed = rows[...].astype(BF16)
    for d in range(NBLK):
        out_ref[d] = packed


def pool_copies(q, parts, pool, sem):
    copies = []
    for i, (part, j, offset) in enumerate(zip(parts, (0, 1, 2, 3, 3), (0, 0, 0, 0, HALF))):
        start = pl.multiple_of((q ^ j) * ROWS + offset, HALF)
        rows = pl.ds(start, part.shape[0])
        copies.append(pltpu.make_async_copy(part, pool.at[rows, :], sem.at[i]))
    return copies


def split(x):
    high = x.astype(BF16).astype(F32)
    middle = (x - high).astype(BF16).astype(F32)
    return (high, middle, x - high - middle)


def score_kernel(
    q_ref, refs_ref, p0, p1, p2, p3, p4, wc_ref, ws_ref, w_ref, c0_ref, c1_ref, c23_ref,
    own_ref, near_ref, far_ref, cross_ref,
    wide, table0, table1, pool, cands, scores, groups, sem
):
    q = q_ref[0]
    copies = pool_copies(q, (p0, p1, p2, p3, p4), pool, sem)
    for copy in copies:
        copy.start()
    for j, cand in enumerate((c0_ref[...], c23_ref[0], c1_ref[...], c23_ref[1])):
        cands[:, pl.ds(pl.multiple_of((q ^ j) * ROWS, ROWS), ROWS)] = cand
    wide[...] = refs_ref[...].astype(F32)
    energy = [jnp.zeros((CLASSES, 128), F32) for _ in range(QROT)]
    stride = QROT * 32
    tables = (table0, table1)
    wide_cols = 128 * STEP_TILES

    def build(step):
        table = tables[step % 2]
        for t in range(STEP_TILES):
            a = step * STEP_TILES + t
            weight = w_ref[a : a + 1, :]
            for r in range(QROT):
                real = wide[pl.ds(r * 32 + a, CLASSES, stride=stride), :]
                imag = wide[pl.ds(r * 32 + 16 + a, CLASSES, stride=stride), :]
                energy[r] = energy[r] + weight * (real * real + imag * imag)
                for s in range(NSHIFT):
                    wc = wc_ref[s * 16 + a : s * 16 + a + 1, :]
                    ws = ws_ref[s * 16 + a : s * 16 + a + 1, :]
                    row = (s * QROT + r) * CLASSES
                    at = slice(t * 128, (t + 1) * 128)
                    at_im = slice(wide_cols + t * 128, wide_cols + (t + 1) * 128)
                    table[row : row + CLASSES, at] = (wc * real - ws * imag).astype(BF16)
                    table[row : row + CLASSES, at_im] = (ws * real + wc * imag).astype(BF16)

    build(0)
    for copy in copies:
        copy.wait()
    steps = 16 // STEP_TILES
    for step in range(steps):
        if step + 1 < steps:
            build(step + 1)
        table = tables[step % 2]
        cols = slice(step * wide_cols, (step + 1) * wide_cols)
        cols_im = slice(K + step * wide_cols, K + (step + 1) * wide_cols)
        for n in range(2):
            lanes = slice(n * 256, (n + 1) * 256)
            part = lax.dot_general(
                table[:, 0:wide_cols], pool[lanes, cols], (((1,), (1,)), ((), ())),
                preferred_element_type=F32,
            ) + lax.dot_general(
                table[:, wide_cols:], pool[lanes, cols_im], (((1,), (1,)), ((), ())),
                preferred_element_type=F32,
            )
            if step == 0:
                scores[:, lanes] = part
            else:
                scores[:, lanes] += part

    half_energy = [0.5 * jnp.sum(e, axis=1, keepdims=True) for e in energy]
    class_id = lax.broadcasted_iota(jnp.int32, (CLASSES, 256), 0)
    for n in range(2):
        lanes = slice(n * 256, (n + 1) * 256)
        cand = cands[:, lanes]
        allowed = class_id == cand[0:1, :]
        for k in range(1, 8):
            allowed = allowed | (class_id == cand[k : k + 1, :])
        loglik = []
        for s in range(NSHIFT):
            for r in range(QROT):
                row = (s * QROT + r) * CLASSES
                value = INV_TEMP * (scores[row : row + CLASSES, lanes] - half_energy[r])
                loglik.append(jnp.where(allowed, value, FLOOR))
        top = loglik[0]
        for value in loglik[1:]:
            top = jnp.maximum(top, value)
        peak = jnp.max(top, axis=0, keepdims=True)
        evidence = jnp.zeros((1, 256), F32)
        for s in range(NSHIFT):
            terms = jnp.zeros((CLASSES, 256), F32)
            for r in range(QROT):
                value = loglik[s * QROT + r]
                terms = terms + jnp.where(allowed, jnp.exp(value - peak), 0.0)
            evidence = evidence + jnp.sum(terms, axis=0, keepdims=True)
            for d in range(NPOOL):
                groups[d, s * QCLS : (s + 1) * QCLS, lanes] = terms[d * QCLS : (d + 1) * QCLS]
        pieces = split(peak) + split(evidence)
        for d in range(NPOOL):
            for i, piece in enumerate(pieces):
                groups[d, 48 + i : 49 + i, lanes] = piece
            groups[d, 54:56, lanes] = jnp.zeros((2, 256), F32)
    own_ref[...] = groups[q]
    for j, ref in enumerate((near_ref, far_ref, cross_ref)):
        ref[...] = groups[q ^ (j + 1)].astype(BF16)


def class_kernel(
    q_ref, x0, x1, x2, x3, p0, p1, p2, p3, p4, cos_ref, sin_ref, out_ref, log_ref, pool, slots, line, sem
):
    q = q_ref[0]
    copies = pool_copies(q, (p0, p1, p2, p3, p4), pool, sem)
    for copy in copies:
        copy.start()
    parts = [x[...].astype(F32) for x in (x0, x1, x2, x3)]
    peaks = [x[48:49] + x[49:50] + x[50:51] for x in parts]
    peak = peaks[0]
    for value in peaks[1:]:
        peak = jnp.maximum(peak, value)
    evidence = jnp.zeros_like(peak)
    terms = jnp.zeros((NSHIFT * QCLS, NPOOL * ROWS), F32)
    for x, value in zip(parts, peaks):
        scale = jnp.exp(value - peak)
        evidence = evidence + scale * (x[51:52] + x[52:53] + x[53:54])
        terms = terms + scale * x[0:48]
    line[...] = peak + jnp.log(evidence)
    log_ref[...] = line[:, pl.ds(pl.multiple_of(q * ROWS, ROWS), ROWS)]
    probs = terms / evidence
    for s in range(NSHIFT):
        slots[s * 16 : s * 16 + QCLS, :] = probs[s * QCLS : (s + 1) * QCLS]
        slots[s * 16 + QCLS : (s + 1) * 16, :] = jnp.zeros((4, NPOOL * ROWS), F32)
    padded = slots[...]
    mass = jnp.sum(padded, axis=1, keepdims=True)
    mass = mass[0:16] + mass[16:32] + mass[32:48] + mass[48:64]
    low = padded.astype(BF16)
    row_id = lax.broadcasted_iota(jnp.int32, (16, COLS), 0)
    lane_id = lax.broadcasted_iota(jnp.int32, (16, COLS), 1)
    mass_row = jnp.sum(jnp.where(row_id == lane_id, mass, 0.0), axis=0, keepdims=True)
    mass_high = mass_row.astype(BF16).astype(F32)
    mass_low = mass_row - mass_high
    for copy in copies:
        copy.wait()
    for b in range(NBLK // 2):
        cols = slice(b * COLS, (b + 1) * COLS)
        cols_im = slice(K + b * COLS, K + (b + 1) * COLS)
        g_re = jnp.dot(low, pool[:, cols], preferred_element_type=F32)
        g_im = jnp.dot(low, pool[:, cols_im], preferred_element_type=F32)
        sum_re = jnp.zeros((16, COLS), F32)
        sum_im = jnp.zeros((16, COLS), F32)
        for s in range(NSHIFT):
            c = cos_ref[s : s + 1, cols]
            z = sin_ref[s : s + 1, cols]
            re = g_re[s * 16 : (s + 1) * 16]
            im = g_im[s * 16 : (s + 1) * 16]
            sum_re = sum_re + (c * re + z * im)
            sum_im = sum_im + (c * im - z * re)
        for dest, value in ((b, sum_re), (NBLK // 2 + b, sum_im)):
            value = jnp.where(row_id == QCLS, mass_high, value)
            value = jnp.where(row_id == QCLS + 1, mass_low, value)
            out_ref[dest] = value.astype(BF16)


def place_kernel(target_ref, y_ref, out_hbm, out_ref, sem):
    total = y_ref[0].astype(F32)
    for b in range(1, NBLK):
        total = total + y_ref[b].astype(F32)
    mass = total[QCLS : QCLS + 1, 0:128] + total[QCLS + 1 : QCLS + 2, 0:128]
    row = lax.broadcasted_iota(jnp.int32, (NDOM * SLOTS, 128), 0)
    hit = target_ref[...] == row
    pick = jnp.where(hit, 1.0, 0.0).astype(BF16)
    placed = jnp.dot(pick[:, 0:16], total.astype(BF16), preferred_element_type=F32)
    placed_mass = jnp.sum(jnp.where(hit, mass, 0.0), axis=1, keepdims=True)
    high = placed_mass.astype(BF16).astype(F32)
    lane = lax.broadcasted_iota(jnp.int32, (NDOM * SLOTS, 128), 1)
    extra = jnp.where(lane == 0, high, jnp.where(lane == 1, placed_mass - high, 0.0))
    out_ref[:, :, 0:COLS] = placed.reshape(NDOM, SLOTS, COLS).astype(BF16)
    out_ref[:, :, COLS:] = extra.reshape(NDOM, SLOTS, 128).astype(BF16)
    send = pltpu.make_async_copy(out_ref, out_hbm, sem)
    send.start()
    send.wait()


def mean_kernel(z_ref, mean_ref, mass_ref):
    total = z_ref[0].astype(F32)
    for d in range(1, NDOM):
        total = total + z_ref[d].astype(F32)
    mass = total[:, COLS : COLS + 1] + total[:, COLS + 1 : COLS + 2]
    mean_ref[...] = total[:, 0:COLS] / (mass + 1.0)
    row = lax.broadcasted_iota(jnp.int32, (SLOTS, 128), 0)
    lane = lax.broadcasted_iota(jnp.int32, (SLOTS, 128), 1)
    mass_ref[...] = jnp.sum(jnp.where(row == lane, mass, 0.0), axis=0)[0:SLOTS]


def phase_tables(offsets):
    index = jnp.arange(KROW * KCOL, dtype=jnp.int32)
    column = index % KCOL
    rowpos = index // KCOL - KROW // 2
    turns = (offsets[:, 0:1] * column[None, :] + offsets[:, 1:2] * rowpos[None, :]).astype(F32)
    angle = turns * (2.0 * math.pi / BOX)
    return (jnp.cos(angle), jnp.sin(angle))


def swap(x, axis):
    return lax.ppermute(x, axis, [(0, 1), (1, 0)])


def trade(parts, axes):
    own, near, far, cross = parts
    return (
        own,
        swap(near, axes[1]),
        swap(far, axes[0]),
        lax.ppermute(cross, axes, [(i, 3 - i) for i in range(4)]),
    )


def on_device(particles, references, noise_weight, offsets, candidates, class_owner):
    pool_index = (lax.axis_index("yl") * 2 + lax.axis_index("core")).astype(jnp.int32)
    q = pool_index.reshape(1)

    cand = candidates.T
    cand_far = swap(cand, "yl")
    far = swap(particles, "yl")
    packed = pl.pallas_call(
        pack_kernel,
        out_shape=jax.ShapeDtypeStruct((NBLK, LOCAL * QROT * 32, 128), BF16),
        in_specs=[SMEM_SPEC, VMEM_SPEC],
        out_specs=VMEM_SPEC,
        scratch_shapes=[VMEM((LOCAL, ROT, 2 * K), F32), VMEM((LOCAL * QROT * 32, 128), F32)],
        compiler_params=params(16),
        name="pack",
    )(q, references)
    gathered = lax.all_to_all(packed, BLK, 0, 0, tiled=True)
    near = swap(particles, "core")
    cand_far, far = lax.optimization_barrier((cand_far, far))
    cand_near = swap(jnp.stack([cand, cand_far]), "core")
    first = swap(far[:HALF], "core")
    rest, first = lax.optimization_barrier((far[HALF:], first))
    second = swap(rest, "core")
    pool = (particles, near, far, first, second)

    cosine, sine = phase_tables(offsets)
    wc = (noise_weight * cosine).reshape(NSHIFT * 16, 128)
    ws = (noise_weight * sine).reshape(NSHIFT * 16, 128)
    weight = noise_weight.reshape(16, 128)

    copies = pltpu.SemaphoreType.DMA((5,))
    pool_shape = VMEM((NPOOL * ROWS, 2 * K), BF16)
    table_rows = NSHIFT * QROT * CLASSES
    terms = pl.pallas_call(
        score_kernel,
        out_shape=[
            jax.ShapeDtypeStruct((56, NPOOL * ROWS), F32 if j == 0 else BF16) for j in range(NPOOL)
        ],
        in_specs=[SMEM_SPEC, VMEM_SPEC] + [ANY_SPEC] * 5 + [VMEM_SPEC] * 6,
        out_specs=[VMEM_SPEC] * NPOOL,
        scratch_shapes=[
            VMEM((NBLK * LOCAL * QROT * 32, 128), F32),
            VMEM((table_rows, 256 * STEP_TILES), BF16),
            VMEM((table_rows, 256 * STEP_TILES), BF16),
            pool_shape,
            VMEM((8, NPOOL * ROWS), jnp.int32),
            VMEM((table_rows, NPOOL * ROWS), F32),
            VMEM((NPOOL, 56, NPOOL * ROWS), F32),
            copies,
        ],
        compiler_params=params(40),
        name="score",
    )(
        q, gathered.reshape(NBLK * LOCAL * QROT * 32, 128), *pool,
        wc, ws, weight, cand, cand_far, cand_near,
    )
    terms = trade(terms, POOL)

    sums, log_evidence = pl.pallas_call(
        class_kernel,
        out_shape=(
            jax.ShapeDtypeStruct((NBLK, 16, COLS), BF16),
            jax.ShapeDtypeStruct((1, ROWS), F32),
        ),
        in_specs=[SMEM_SPEC] + [VMEM_SPEC] * 4 + [ANY_SPEC] * 5 + [VMEM_SPEC] * 2,
        out_specs=(VMEM_SPEC, VMEM_SPEC),
        scratch_shapes=[
            pool_shape,
            VMEM((NSHIFT * 16, NPOOL * ROWS), F32),
            VMEM((1, NPOOL * ROWS), F32),
            copies,
        ],
        compiler_params=params(24),
        name="classes",
    )(q, *terms, *pool, cosine, sine)
    sums = lax.all_to_all(sums, BLK, 0, 0, tiled=True)

    class_ids = jnp.arange(CLASSES, dtype=jnp.int32)
    shared_owner = class_owner[:, None] == class_owner[None, :]
    earlier = class_ids[:, None] < class_ids[None, :]
    position = jnp.sum((shared_owner & earlier).astype(jnp.int32), axis=0)
    target = class_owner * SLOTS + position
    mine = lax.dynamic_slice(target, (pool_index * QCLS,), (QCLS,))
    mine = jnp.pad(mine, (0, 128 - QCLS), constant_values=-1).reshape(1, 128)
    placed = pl.pallas_call(
        place_kernel,
        out_shape=pltpu.HBM((NDOM, SLOTS, COLS + 128), BF16),
        in_specs=[VMEM_SPEC, VMEM_SPEC],
        out_specs=pl.BlockSpec(memory_space=pltpu.HBM),
        scratch_shapes=[VMEM((NDOM, SLOTS, COLS + 128), BF16), pltpu.SemaphoreType.DMA],
        compiler_params=params(4),
        name="place",
    )(mine, sums)
    placed = lax.all_to_all(placed, DOM, 0, 0, tiled=True)
    means, mass = pl.pallas_call(
        mean_kernel,
        out_shape=(
            jax.ShapeDtypeStruct((SLOTS, COLS), F32),
            jax.ShapeDtypeStruct((SLOTS,), F32),
        ),
        in_specs=[VMEM_SPEC],
        out_specs=(VMEM_SPEC, VMEM_SPEC),
        compiler_params=params(4),
        name="means",
    )(placed)
    return (means, mass, log_evidence.reshape(ROWS))


def solution(mesh):
    fine = Mesh(
        np.asarray(mesh.devices).reshape([size for _, size in FINE]), [name for name, _ in FINE]
    )
    every = DOM + BLK
    return jax.shard_map(
        on_device,
        mesh=fine,
        in_specs=(P(every, None), P(BLK, None, None), P(), P(), P(every, None), P()),
        out_specs=(P(DOM, BLK), P(DOM), P(every)),
        check_vma=False,
    )
```

```python
import math

import jax
import jax.numpy as jnp
import numpy as np
from jax import lax
from jax.experimental import pallas as pl
from jax.experimental.pallas import tpu as pltpu
from jax.sharding import Mesh, PartitionSpec as P

KROW = 64
KCOL = 32
BOX = 256
SLOTS = 8
INV_TEMP = 4.0
FLOOR = -1e30

FINE = (("xh", 2), ("yh", 2), ("yl", 2), ("core", 2), ("z", 8), ("xl", 2))
DOM = ("xh", "yh", "yl", "core")
BLK = ("z", "xl")
POOL = ("yl", "core")

K = 2048
CLASSES = 48
ROT = 12
NSHIFT = 4
ROWS = 128
HALF = ROWS // 2
NPOOL = 4
QROT = ROT // NPOOL
QCLS = CLASSES // NPOOL
NBLK = 16
NDOM = 16
LOCAL = 3
COLS = 256
STEP_TILES = 4
F32 = jnp.float32
BF16 = jnp.bfloat16
VMEM = pltpu.VMEM
SMEM_SPEC = pl.BlockSpec(memory_space=pltpu.SMEM)
VMEM_SPEC = pl.BlockSpec(memory_space=pltpu.VMEM)
ANY_SPEC = pl.BlockSpec(memory_space=pl.ANY)
HBM_SPEC = pl.BlockSpec(memory_space=pltpu.HBM)


def params(mib):
    return pltpu.CompilerParams(vmem_limit_bytes=mib << 20)


def pack_kernel(q_ref, refs_ref, out_ref, wide, rows):
    q = q_ref[0]
    wide[...] = refs_ref[...].astype(F32)
    for c in range(LOCAL):
        for r in range(QROT):
            row = wide[c, pl.ds(QROT * q + r, 1), :]
            for a in range(32):
                at = (c * QROT + r) * 32 + a
                rows[at : at + 1, :] = row[:, a * 128 : (a + 1) * 128]
    packed = rows[...].astype(BF16)
    for d in range(NBLK):
        out_ref[d] = packed


def pool_kernel(q_ref, p0, p1, p2, p3, p4, p5, c0_ref, c1_ref, c23_ref, pool, cands, sem):
    q = q_ref[0]
    copies = []
    places = ((0, 0), (1, 0), (2, 0), (2, HALF), (3, 0), (3, HALF))
    for i, (part, (j, offset)) in enumerate(zip((p0, p1, p2, p3, p4, p5), places)):
        rows = pl.ds(pl.multiple_of((q ^ j) * ROWS + offset, HALF), part.shape[0])
        copies.append(pltpu.make_async_copy(part, pool.at[rows, :], sem.at[i]))
    for copy in copies:
        copy.start()
    for j, cand in enumerate((c0_ref[...], c23_ref[0], c1_ref[...], c23_ref[1])):
        cands[:, pl.ds(pl.multiple_of((q ^ j) * ROWS, ROWS), ROWS)] = cand
    for copy in copies:
        copy.wait()


def split(x):
    high = x.astype(BF16).astype(F32)
    middle = (x - high).astype(BF16).astype(F32)
    return (high, middle, x - high - middle)


def score_kernel(
    q_ref, refs_ref, pool_hbm, wc_ref, ws_ref, w_ref, cands,
    own_ref, near_ref, far_ref, cross_ref,
    wide, table0, table1, scores, groups, pool, sem
):
    q = q_ref[0]
    steps = 16 // STEP_TILES
    wide_cols = 128 * STEP_TILES
    copies = []
    for step in range(steps):
        for part in range(2):
            cols = pl.ds(part * K + step * wide_cols, wide_cols)
            copies.append(
                pltpu.make_async_copy(pool_hbm.at[:, cols], pool.at[:, cols], sem.at[step, part])
            )
    for copy in copies:
        copy.start()
    wide[...] = refs_ref[...].astype(F32)
    energy = [jnp.zeros((CLASSES, 128), F32) for _ in range(QROT)]
    stride = QROT * 32
    tables = (table0, table1)

    def build(step):
        table = tables[step % 2]
        for t in range(STEP_TILES):
            a = step * STEP_TILES + t
            weight = w_ref[a : a + 1, :]
            for r in range(QROT):
                real = wide[pl.ds(r * 32 + a, CLASSES, stride=stride), :]
                imag = wide[pl.ds(r * 32 + 16 + a, CLASSES, stride=stride), :]
                energy[r] = energy[r] + weight * (real * real + imag * imag)
                for s in range(NSHIFT):
                    wc = wc_ref[s * 16 + a : s * 16 + a + 1, :]
                    ws = ws_ref[s * 16 + a : s * 16 + a + 1, :]
                    row = (s * QROT + r) * CLASSES
                    at = slice(t * 128, (t + 1) * 128)
                    at_im = slice(wide_cols + t * 128, wide_cols + (t + 1) * 128)
                    table[row : row + CLASSES, at] = (wc * real - ws * imag).astype(BF16)
                    table[row : row + CLASSES, at_im] = (ws * real + wc * imag).astype(BF16)

    build(0)
    for step in range(steps):
        copies[2 * step].wait()
        copies[2 * step + 1].wait()
        if step + 1 < steps:
            build(step + 1)
        table = tables[step % 2]
        cols = slice(step * wide_cols, (step + 1) * wide_cols)
        cols_im = slice(K + step * wide_cols, K + (step + 1) * wide_cols)
        for n in range(2):
            lanes = slice(n * 256, (n + 1) * 256)
            part = lax.dot_general(
                table[:, 0:wide_cols], pool[lanes, cols], (((1,), (1,)), ((), ())),
                preferred_element_type=F32,
            ) + lax.dot_general(
                table[:, wide_cols:], pool[lanes, cols_im], (((1,), (1,)), ((), ())),
                preferred_element_type=F32,
            )
            if step == 0:
                scores[:, lanes] = part
            else:
                scores[:, lanes] += part

    half_energy = [0.5 * jnp.sum(e, axis=1, keepdims=True) for e in energy]
    class_id = lax.broadcasted_iota(jnp.int32, (CLASSES, 256), 0)
    for n in range(2):
        lanes = slice(n * 256, (n + 1) * 256)
        cand = cands[:, lanes]
        allowed = class_id == cand[0:1, :]
        for k in range(1, 8):
            allowed = allowed | (class_id == cand[k : k + 1, :])
        loglik = []
        for s in range(NSHIFT):
            for r in range(QROT):
                row = (s * QROT + r) * CLASSES
                value = INV_TEMP * (scores[row : row + CLASSES, lanes] - half_energy[r])
                loglik.append(jnp.where(allowed, value, FLOOR))
        top = loglik[0]
        for value in loglik[1:]:
            top = jnp.maximum(top, value)
        peak = jnp.max(top, axis=0, keepdims=True)
        evidence = jnp.zeros((1, 256), F32)
        for s in range(NSHIFT):
            terms = jnp.zeros((CLASSES, 256), F32)
            for r in range(QROT):
                value = loglik[s * QROT + r]
                terms = terms + jnp.where(allowed, jnp.exp(value - peak), 0.0)
            evidence = evidence + jnp.sum(terms, axis=0, keepdims=True)
            for d in range(NPOOL):
                groups[d, s * QCLS : (s + 1) * QCLS, lanes] = terms[d * QCLS : (d + 1) * QCLS]
        pieces = split(peak) + split(evidence)
        for d in range(NPOOL):
            for i, piece in enumerate(pieces):
                groups[d, 48 + i : 49 + i, lanes] = piece
            groups[d, 54:56, lanes] = jnp.zeros((2, 256), F32)
    own_ref[...] = groups[q]
    for j, ref in enumerate((near_ref, far_ref, cross_ref)):
        ref[...] = groups[q ^ (j + 1)].astype(BF16)


def class_kernel(
    q_ref, x0, x1, x2, x3, pool, cos_ref, sin_ref, out_ref, log_ref, slots, line
):
    q = q_ref[0]
    parts = [x[...].astype(F32) for x in (x0, x1, x2, x3)]
    peaks = [x[48:49] + x[49:50] + x[50:51] for x in parts]
    peak = peaks[0]
    for value in peaks[1:]:
        peak = jnp.maximum(peak, value)
    evidence = jnp.zeros_like(peak)
    terms = jnp.zeros((NSHIFT * QCLS, NPOOL * ROWS), F32)
    for x, value in zip(parts, peaks):
        scale = jnp.exp(value - peak)
        evidence = evidence + scale * (x[51:52] + x[52:53] + x[53:54])
        terms = terms + scale * x[0:48]
    line[...] = peak + jnp.log(evidence)
    log_ref[...] = line[:, pl.ds(pl.multiple_of(q * ROWS, ROWS), ROWS)]
    probs = terms / evidence
    for s in range(NSHIFT):
        slots[s * 16 : s * 16 + QCLS, :] = probs[s * QCLS : (s + 1) * QCLS]
        slots[s * 16 + QCLS : (s + 1) * 16, :] = jnp.zeros((4, NPOOL * ROWS), F32)
    padded = slots[...]
    mass = jnp.sum(padded, axis=1, keepdims=True)
    mass = mass[0:16] + mass[16:32] + mass[32:48] + mass[48:64]
    low = padded.astype(BF16)
    row_id = lax.broadcasted_iota(jnp.int32, (16, COLS), 0)
    lane_id = lax.broadcasted_iota(jnp.int32, (16, COLS), 1)
    mass_row = jnp.sum(jnp.where(row_id == lane_id, mass, 0.0), axis=0, keepdims=True)
    mass_high = mass_row.astype(BF16).astype(F32)
    mass_low = mass_row - mass_high
    for b in range(NBLK // 2):
        cols = slice(b * COLS, (b + 1) * COLS)
        cols_im = slice(K + b * COLS, K + (b + 1) * COLS)
        g_re = jnp.dot(low, pool[:, cols], preferred_element_type=F32)
        g_im = jnp.dot(low, pool[:, cols_im], preferred_element_type=F32)
        sum_re = jnp.zeros((16, COLS), F32)
        sum_im = jnp.zeros((16, COLS), F32)
        for s in range(NSHIFT):
            c = cos_ref[s : s + 1, cols]
            z = sin_ref[s : s + 1, cols]
            re = g_re[s * 16 : (s + 1) * 16]
            im = g_im[s * 16 : (s + 1) * 16]
            sum_re = sum_re + (c * re + z * im)
            sum_im = sum_im + (c * im - z * re)
        for dest, value in ((b, sum_re), (NBLK // 2 + b, sum_im)):
            value = jnp.where(row_id == QCLS, mass_high, value)
            value = jnp.where(row_id == QCLS + 1, mass_low, value)
            out_ref[dest] = value.astype(BF16)


def place_kernel(target_ref, y_ref, out_hbm, out_ref, sem):
    total = y_ref[0].astype(F32)
    for b in range(1, NBLK):
        total = total + y_ref[b].astype(F32)
    mass = total[QCLS : QCLS + 1, 0:128] + total[QCLS + 1 : QCLS + 2, 0:128]
    row = lax.broadcasted_iota(jnp.int32, (NDOM * SLOTS, 128), 0)
    hit = target_ref[...] == row
    pick = jnp.where(hit, 1.0, 0.0).astype(BF16)
    placed = jnp.dot(pick[:, 0:16], total.astype(BF16), preferred_element_type=F32)
    placed_mass = jnp.sum(jnp.where(hit, mass, 0.0), axis=1, keepdims=True)
    high = placed_mass.astype(BF16).astype(F32)
    lane = lax.broadcasted_iota(jnp.int32, (NDOM * SLOTS, 128), 1)
    extra = jnp.where(lane == 0, high, jnp.where(lane == 1, placed_mass - high, 0.0))
    out_ref[:, :, 0:COLS] = placed.reshape(NDOM, SLOTS, COLS).astype(BF16)
    out_ref[:, :, COLS:] = extra.reshape(NDOM, SLOTS, 128).astype(BF16)
    send = pltpu.make_async_copy(out_ref, out_hbm, sem)
    send.start()
    send.wait()


def mean_kernel(z_ref, mean_ref, mass_ref):
    total = z_ref[0].astype(F32)
    for d in range(1, NDOM):
        total = total + z_ref[d].astype(F32)
    mass = total[:, COLS : COLS + 1] + total[:, COLS + 1 : COLS + 2]
    mean_ref[...] = total[:, 0:COLS] / (mass + 1.0)
    row = lax.broadcasted_iota(jnp.int32, (SLOTS, 128), 0)
    lane = lax.broadcasted_iota(jnp.int32, (SLOTS, 128), 1)
    mass_ref[...] = jnp.sum(jnp.where(row == lane, mass, 0.0), axis=0)[0:SLOTS]


def phase_tables(offsets):
    index = jnp.arange(KROW * KCOL, dtype=jnp.int32)
    column = index % KCOL
    rowpos = index // KCOL - KROW // 2
    turns = (offsets[:, 0:1] * column[None, :] + offsets[:, 1:2] * rowpos[None, :]).astype(F32)
    angle = turns * (2.0 * math.pi / BOX)
    return (jnp.cos(angle), jnp.sin(angle))


def in_hbm(x):
    return pltpu.with_memory_space_constraint(x, pltpu.HBM)


def swap(x, axis):
    return lax.ppermute(x, axis, [(0, 1), (1, 0)])


def trade(parts, axes):
    own, near, far, cross = parts
    return (
        own,
        swap(near, axes[1]),
        swap(far, axes[0]),
        lax.ppermute(cross, axes, [(i, 3 - i) for i in range(4)]),
    )


def on_device(particles, references, noise_weight, offsets, candidates, class_owner):
    pool_index = (lax.axis_index("yl") * 2 + lax.axis_index("core")).astype(jnp.int32)
    q = pool_index.reshape(1)

    cand = candidates.T
    far0 = swap(particles[:HALF], "yl")
    cand_far = swap(cand, "yl")
    rest, far0, cand_far = lax.optimization_barrier((particles[HALF:], far0, cand_far))
    far1 = swap(rest, "yl")
    packed = pl.pallas_call(
        pack_kernel,
        out_shape=jax.ShapeDtypeStruct((NBLK, LOCAL * QROT * 32, 128), BF16),
        in_specs=[SMEM_SPEC, VMEM_SPEC],
        out_specs=VMEM_SPEC,
        scratch_shapes=[VMEM((LOCAL, ROT, 2 * K), F32), VMEM((LOCAL * QROT * 32, 128), F32)],
        compiler_params=params(16),
        name="pack",
    )(q, references)
    gathered = lax.all_to_all(packed, BLK, 0, 0, tiled=True)
    near = swap(particles, "core")
    near1 = swap(far1, "core")
    far0, near1 = lax.optimization_barrier((far0, near1))
    near0 = swap(far0, "core")
    cand_near = swap(jnp.stack([cand, cand_far]), "core")
    pool, cands = pl.pallas_call(
        pool_kernel,
        out_shape=(
            pltpu.HBM((NPOOL * ROWS, 2 * K), BF16),
            jax.ShapeDtypeStruct((8, NPOOL * ROWS), jnp.int32),
        ),
        in_specs=[SMEM_SPEC] + [ANY_SPEC] * 6 + [VMEM_SPEC] * 3,
        out_specs=(HBM_SPEC, VMEM_SPEC),
        scratch_shapes=[pltpu.SemaphoreType.DMA((6,))],
        compiler_params=params(4),
        name="pool",
    )(
        q, *[in_hbm(x) for x in (particles, near, far0, far1, near0, near1)],
        cand, cand_far, cand_near,
    )

    cosine, sine = phase_tables(offsets)
    wc = (noise_weight * cosine).reshape(NSHIFT * 16, 128)
    ws = (noise_weight * sine).reshape(NSHIFT * 16, 128)
    weight = noise_weight.reshape(16, 128)

    table_rows = NSHIFT * QROT * CLASSES
    terms = pl.pallas_call(
        score_kernel,
        out_shape=[
            jax.ShapeDtypeStruct((56, NPOOL * ROWS), F32 if j == 0 else BF16) for j in range(NPOOL)
        ],
        in_specs=[SMEM_SPEC, VMEM_SPEC, HBM_SPEC] + [VMEM_SPEC] * 4,
        out_specs=[VMEM_SPEC] * NPOOL,
        scratch_shapes=[
            VMEM((NBLK * LOCAL * QROT * 32, 128), F32),
            VMEM((table_rows, 256 * STEP_TILES), BF16),
            VMEM((table_rows, 256 * STEP_TILES), BF16),
            VMEM((table_rows, NPOOL * ROWS), F32),
            VMEM((NPOOL, 56, NPOOL * ROWS), F32),
            VMEM((NPOOL * ROWS, 2 * K), BF16),
            pltpu.SemaphoreType.DMA((16 // STEP_TILES, 2)),
        ],
        compiler_params=params(20),
        name="score",
    )(q, gathered.reshape(NBLK * LOCAL * QROT * 32, 128), in_hbm(pool), wc, ws, weight, cands)
    terms = trade(terms, POOL)

    sums, log_evidence = pl.pallas_call(
        class_kernel,
        out_shape=(
            jax.ShapeDtypeStruct((NBLK, 16, COLS), BF16),
            jax.ShapeDtypeStruct((1, ROWS), F32),
        ),
        in_specs=[SMEM_SPEC] + [VMEM_SPEC] * 7,
        out_specs=(VMEM_SPEC, VMEM_SPEC),
        scratch_shapes=[
            VMEM((NSHIFT * 16, NPOOL * ROWS), F32),
            VMEM((1, NPOOL * ROWS), F32),
        ],
        compiler_params=params(16),
        name="classes",
    )(q, *terms, pool, cosine, sine)
    sums = lax.all_to_all(sums, BLK, 0, 0, tiled=True)

    class_ids = jnp.arange(CLASSES, dtype=jnp.int32)
    shared_owner = class_owner[:, None] == class_owner[None, :]
    earlier = class_ids[:, None] < class_ids[None, :]
    position = jnp.sum((shared_owner & earlier).astype(jnp.int32), axis=0)
    target = class_owner * SLOTS + position
    mine = lax.dynamic_slice(target, (pool_index * QCLS,), (QCLS,))
    mine = jnp.pad(mine, (0, 128 - QCLS), constant_values=-1).reshape(1, 128)
    placed = pl.pallas_call(
        place_kernel,
        out_shape=pltpu.HBM((NDOM, SLOTS, COLS + 128), BF16),
        in_specs=[VMEM_SPEC, VMEM_SPEC],
        out_specs=pl.BlockSpec(memory_space=pltpu.HBM),
        scratch_shapes=[VMEM((NDOM, SLOTS, COLS + 128), BF16), pltpu.SemaphoreType.DMA],
        compiler_params=params(4),
        name="place",
    )(mine, sums)
    placed = lax.all_to_all(placed, DOM, 0, 0, tiled=True)
    means, mass = pl.pallas_call(
        mean_kernel,
        out_shape=(
            jax.ShapeDtypeStruct((SLOTS, COLS), F32),
            jax.ShapeDtypeStruct((SLOTS,), F32),
        ),
        in_specs=[VMEM_SPEC],
        out_specs=(VMEM_SPEC, VMEM_SPEC),
        compiler_params=params(4),
        name="means",
    )(placed)
    return (means, mass, log_evidence.reshape(ROWS))


def solution(mesh):
    fine = Mesh(
        np.asarray(mesh.devices).reshape([size for _, size in FINE]), [name for name, _ in FINE]
    )
    every = DOM + BLK
    return jax.shard_map(
        on_device,
        mesh=fine,
        in_specs=(P(every, None), P(BLK, None, None), P(), P(), P(every, None), P()),
        out_specs=(P(DOM, BLK), P(DOM), P(every)),
        check_vma=False,
    )
```

```python
import math

import jax
import jax.numpy as jnp
import numpy as np
from jax import lax
from jax.experimental import pallas as pl
from jax.experimental.pallas import tpu as pltpu
from jax.sharding import Mesh, PartitionSpec as P

KROW = 64
KCOL = 32
BOX = 256
SLOTS = 8
INV_TEMP = 4.0
FLOOR = -1e30

FINE = (("xh", 2), ("yh", 2), ("yl", 2), ("core", 2), ("z", 8), ("xl", 2))
DOM = ("xh", "yh", "yl", "core")
BLK = ("z", "xl")
POOL = ("yl", "core")

K = 2048
CLASSES = 48
ROT = 12
NSHIFT = 4
ROWS = 128
FIRST = 48
NPOOL = 4
QROT = ROT // NPOOL
QCLS = CLASSES // NPOOL
NBLK = 16
NDOM = 16
LOCAL = 3
COLS = 256
STEP_TILES = 4
F32 = jnp.float32
BF16 = jnp.bfloat16
VMEM = pltpu.VMEM
SMEM_SPEC = pl.BlockSpec(memory_space=pltpu.SMEM)
VMEM_SPEC = pl.BlockSpec(memory_space=pltpu.VMEM)
ANY_SPEC = pl.BlockSpec(memory_space=pl.ANY)
HBM_SPEC = pl.BlockSpec(memory_space=pltpu.HBM)


def params(mib):
    return pltpu.CompilerParams(vmem_limit_bytes=mib << 20)


def pack_kernel(q_ref, refs_ref, out_ref, wide, rows):
    q = q_ref[0]
    wide[...] = refs_ref[...].astype(F32)
    for c in range(LOCAL):
        for r in range(QROT):
            row = wide[c, pl.ds(QROT * q + r, 1), :]
            for a in range(32):
                at = (c * QROT + r) * 32 + a
                rows[at : at + 1, :] = row[:, a * 128 : (a + 1) * 128]
    packed = rows[...].astype(BF16)
    for d in range(NBLK):
        out_ref[d] = packed


def pool_copies(q, parts, pool, sem):
    copies = []
    places = ((0, 0), (1, 0), (2, 0), (2, FIRST), (3, 0), (3, FIRST))
    for i, (part, (j, offset)) in enumerate(zip(parts, places)):
        rows = pl.ds(pl.multiple_of((q ^ j) * ROWS + offset, 16), part.shape[0])
        copies.append(pltpu.make_async_copy(part, pool.at[rows, :], sem.at[i]))
    return copies


def split(x):
    high = x.astype(BF16).astype(F32)
    middle = (x - high).astype(BF16).astype(F32)
    return (high, middle, x - high - middle)


def score_kernel(
    q_ref, refs_ref, p0, p1, p2, p3, p4, p5, wc_ref, ws_ref, w_ref, c0_ref, c1_ref, c23_ref,
    own_ref, near_ref, far_ref, cross_ref, pool,
    wide, table0, table1, scores, groups, cands, sem
):
    q = q_ref[0]
    steps = 16 // STEP_TILES
    wide_cols = 128 * STEP_TILES
    copies = pool_copies(q, (p0, p1, p2, p3, p4, p5), pool, sem)
    for copy in copies:
        copy.start()
    for j, cand in enumerate((c0_ref[...], c23_ref[0], c1_ref[...], c23_ref[1])):
        cands[:, pl.ds(pl.multiple_of((q ^ j) * ROWS, ROWS), ROWS)] = cand
    wide[...] = refs_ref[...].astype(F32)
    energy = [jnp.zeros((CLASSES, 128), F32) for _ in range(QROT)]
    stride = QROT * 32
    tables = (table0, table1)

    def build(step):
        table = tables[step % 2]
        for t in range(STEP_TILES):
            a = step * STEP_TILES + t
            weight = w_ref[a : a + 1, :]
            for r in range(QROT):
                real = wide[pl.ds(r * 32 + a, CLASSES, stride=stride), :]
                imag = wide[pl.ds(r * 32 + 16 + a, CLASSES, stride=stride), :]
                energy[r] = energy[r] + weight * (real * real + imag * imag)
                for s in range(NSHIFT):
                    wc = wc_ref[s * 16 + a : s * 16 + a + 1, :]
                    ws = ws_ref[s * 16 + a : s * 16 + a + 1, :]
                    row = (s * QROT + r) * CLASSES
                    at = slice(t * 128, (t + 1) * 128)
                    at_im = slice(wide_cols + t * 128, wide_cols + (t + 1) * 128)
                    table[row : row + CLASSES, at] = (wc * real - ws * imag).astype(BF16)
                    table[row : row + CLASSES, at_im] = (ws * real + wc * imag).astype(BF16)

    build(0)
    for copy in copies:
        copy.wait()
    for step in range(steps):
        if step + 1 < steps:
            build(step + 1)
        table = tables[step % 2]
        cols = slice(step * wide_cols, (step + 1) * wide_cols)
        cols_im = slice(K + step * wide_cols, K + (step + 1) * wide_cols)
        for n in range(2):
            lanes = slice(n * 256, (n + 1) * 256)
            part = lax.dot_general(
                table[:, 0:wide_cols], pool[lanes, cols], (((1,), (1,)), ((), ())),
                preferred_element_type=F32,
            ) + lax.dot_general(
                table[:, wide_cols:], pool[lanes, cols_im], (((1,), (1,)), ((), ())),
                preferred_element_type=F32,
            )
            if step == 0:
                scores[:, lanes] = part
            else:
                scores[:, lanes] += part

    half_energy = [0.5 * jnp.sum(e, axis=1, keepdims=True) for e in energy]
    class_id = lax.broadcasted_iota(jnp.int32, (CLASSES, 256), 0)
    for n in range(2):
        lanes = slice(n * 256, (n + 1) * 256)
        cand = cands[:, lanes]
        allowed = class_id == cand[0:1, :]
        for k in range(1, 8):
            allowed = allowed | (class_id == cand[k : k + 1, :])
        loglik = []
        for s in range(NSHIFT):
            for r in range(QROT):
                row = (s * QROT + r) * CLASSES
                value = INV_TEMP * (scores[row : row + CLASSES, lanes] - half_energy[r])
                loglik.append(jnp.where(allowed, value, FLOOR))
        top = loglik[0]
        for value in loglik[1:]:
            top = jnp.maximum(top, value)
        peak = jnp.max(top, axis=0, keepdims=True)
        evidence = jnp.zeros((1, 256), F32)
        for s in range(NSHIFT):
            terms = jnp.zeros((CLASSES, 256), F32)
            for r in range(QROT):
                value = loglik[s * QROT + r]
                terms = terms + jnp.where(allowed, jnp.exp(value - peak), 0.0)
            evidence = evidence + jnp.sum(terms, axis=0, keepdims=True)
            for d in range(NPOOL):
                groups[d, s * QCLS : (s + 1) * QCLS, lanes] = terms[d * QCLS : (d + 1) * QCLS]
        pieces = split(peak) + split(evidence)
        for d in range(NPOOL):
            for i, piece in enumerate(pieces):
                groups[d, 48 + i : 49 + i, lanes] = piece
            groups[d, 54:56, lanes] = jnp.zeros((2, 256), F32)
    own_ref[...] = groups[q]
    for j, ref in enumerate((near_ref, far_ref, cross_ref)):
        ref[...] = groups[q ^ (j + 1)].astype(BF16)


def class_kernel(
    q_ref, x0, x1, x2, x3, pool, cos_ref, sin_ref, out_ref, log_ref, slots, line
):
    q = q_ref[0]
    parts = [x[...].astype(F32) for x in (x0, x1, x2, x3)]
    peaks = [x[48:49] + x[49:50] + x[50:51] for x in parts]
    peak = peaks[0]
    for value in peaks[1:]:
        peak = jnp.maximum(peak, value)
    evidence = jnp.zeros_like(peak)
    terms = jnp.zeros((NSHIFT * QCLS, NPOOL * ROWS), F32)
    for x, value in zip(parts, peaks):
        scale = jnp.exp(value - peak)
        evidence = evidence + scale * (x[51:52] + x[52:53] + x[53:54])
        terms = terms + scale * x[0:48]
    line[...] = peak + jnp.log(evidence)
    log_ref[...] = line[:, pl.ds(pl.multiple_of(q * ROWS, ROWS), ROWS)]
    probs = terms / evidence
    for s in range(NSHIFT):
        slots[s * 16 : s * 16 + QCLS, :] = probs[s * QCLS : (s + 1) * QCLS]
        slots[s * 16 + QCLS : (s + 1) * 16, :] = jnp.zeros((4, NPOOL * ROWS), F32)
    padded = slots[...]
    mass = jnp.sum(padded, axis=1, keepdims=True)
    mass = mass[0:16] + mass[16:32] + mass[32:48] + mass[48:64]
    low = padded.astype(BF16)
    row_id = lax.broadcasted_iota(jnp.int32, (16, COLS), 0)
    lane_id = lax.broadcasted_iota(jnp.int32, (16, COLS), 1)
    mass_row = jnp.sum(jnp.where(row_id == lane_id, mass, 0.0), axis=0, keepdims=True)
    mass_high = mass_row.astype(BF16).astype(F32)
    mass_low = mass_row - mass_high
    for b in range(NBLK // 2):
        cols = slice(b * COLS, (b + 1) * COLS)
        cols_im = slice(K + b * COLS, K + (b + 1) * COLS)
        g_re = jnp.dot(low, pool[:, cols], preferred_element_type=F32)
        g_im = jnp.dot(low, pool[:, cols_im], preferred_element_type=F32)
        sum_re = jnp.zeros((16, COLS), F32)
        sum_im = jnp.zeros((16, COLS), F32)
        for s in range(NSHIFT):
            c = cos_ref[s : s + 1, cols]
            z = sin_ref[s : s + 1, cols]
            re = g_re[s * 16 : (s + 1) * 16]
            im = g_im[s * 16 : (s + 1) * 16]
            sum_re = sum_re + (c * re + z * im)
            sum_im = sum_im + (c * im - z * re)
        for dest, value in ((b, sum_re), (NBLK // 2 + b, sum_im)):
            value = jnp.where(row_id == QCLS, mass_high, value)
            value = jnp.where(row_id == QCLS + 1, mass_low, value)
            out_ref[dest] = value.astype(BF16)


def place_kernel(target_ref, y_ref, out_hbm, out_ref, sem):
    total = y_ref[0].astype(F32)
    for b in range(1, NBLK):
        total = total + y_ref[b].astype(F32)
    mass = total[QCLS : QCLS + 1, 0:128] + total[QCLS + 1 : QCLS + 2, 0:128]
    row = lax.broadcasted_iota(jnp.int32, (NDOM * SLOTS, 128), 0)
    hit = target_ref[...] == row
    pick = jnp.where(hit, 1.0, 0.0).astype(BF16)
    placed = jnp.dot(pick[:, 0:16], total.astype(BF16), preferred_element_type=F32)
    placed_mass = jnp.sum(jnp.where(hit, mass, 0.0), axis=1, keepdims=True)
    high = placed_mass.astype(BF16).astype(F32)
    lane = lax.broadcasted_iota(jnp.int32, (NDOM * SLOTS, 128), 1)
    extra = jnp.where(lane == 0, high, jnp.where(lane == 1, placed_mass - high, 0.0))
    out_ref[:, :, 0:COLS] = placed.reshape(NDOM, SLOTS, COLS).astype(BF16)
    out_ref[:, :, COLS:] = extra.reshape(NDOM, SLOTS, 128).astype(BF16)
    send = pltpu.make_async_copy(out_ref, out_hbm, sem)
    send.start()
    send.wait()


def mean_kernel(z_ref, mean_ref, mass_ref):
    total = z_ref[0].astype(F32)
    for d in range(1, NDOM):
        total = total + z_ref[d].astype(F32)
    mass = total[:, COLS : COLS + 1] + total[:, COLS + 1 : COLS + 2]
    mean_ref[...] = total[:, 0:COLS] / (mass + 1.0)
    row = lax.broadcasted_iota(jnp.int32, (SLOTS, 128), 0)
    lane = lax.broadcasted_iota(jnp.int32, (SLOTS, 128), 1)
    mass_ref[...] = jnp.sum(jnp.where(row == lane, mass, 0.0), axis=0)[0:SLOTS]


def phase_tables(offsets):
    index = jnp.arange(KROW * KCOL, dtype=jnp.int32)
    column = index % KCOL
    rowpos = index // KCOL - KROW // 2
    turns = (offsets[:, 0:1] * column[None, :] + offsets[:, 1:2] * rowpos[None, :]).astype(F32)
    angle = turns * (2.0 * math.pi / BOX)
    return (jnp.cos(angle), jnp.sin(angle))


def in_hbm(x):
    return pltpu.with_memory_space_constraint(x, pltpu.HBM)


def swap(x, axis):
    return lax.ppermute(x, axis, [(0, 1), (1, 0)])


def trade(parts, axes):
    own, near, far, cross = parts
    return (
        own,
        swap(near, axes[1]),
        swap(far, axes[0]),
        lax.ppermute(cross, axes, [(i, 3 - i) for i in range(4)]),
    )


def on_device(particles, references, noise_weight, offsets, candidates, class_owner):
    pool_index = (lax.axis_index("yl") * 2 + lax.axis_index("core")).astype(jnp.int32)
    q = pool_index.reshape(1)

    cand = candidates.T
    far0 = swap(particles[:FIRST], "yl")
    cand_far = swap(cand, "yl")
    packed = pl.pallas_call(
        pack_kernel,
        out_shape=jax.ShapeDtypeStruct((NBLK, LOCAL * QROT * 32, 128), BF16),
        in_specs=[SMEM_SPEC, VMEM_SPEC],
        out_specs=VMEM_SPEC,
        scratch_shapes=[VMEM((LOCAL, ROT, 2 * K), F32), VMEM((LOCAL * QROT * 32, 128), F32)],
        compiler_params=params(16),
        name="pack",
    )(q, references)
    packed, whole = lax.optimization_barrier((packed, particles))
    gathered = lax.all_to_all(packed, BLK, 0, 0, tiled=True)
    rest, far0, cand_far = lax.optimization_barrier((whole[FIRST:], far0, cand_far))
    far1 = swap(rest, "yl")
    near = swap(particles, "core")
    near1 = swap(far1, "core")
    far0, near1 = lax.optimization_barrier((far0, near1))
    near0 = swap(far0, "core")
    cand_near = swap(jnp.stack([cand, cand_far]), "core")
    parts = (in_hbm(particles), near, far0, far1, near0, near1)

    cosine, sine = phase_tables(offsets)
    wc = (noise_weight * cosine).reshape(NSHIFT * 16, 128)
    ws = (noise_weight * sine).reshape(NSHIFT * 16, 128)
    weight = noise_weight.reshape(16, 128)

    table_rows = NSHIFT * QROT * CLASSES
    *terms, pool = pl.pallas_call(
        score_kernel,
        out_shape=[
            jax.ShapeDtypeStruct((56, NPOOL * ROWS), F32 if j == 0 else BF16) for j in range(NPOOL)
        ]
        + [jax.ShapeDtypeStruct((NPOOL * ROWS, 2 * K), BF16)],
        in_specs=[SMEM_SPEC, VMEM_SPEC] + [HBM_SPEC] + [ANY_SPEC] * 5 + [VMEM_SPEC] * 6,
        out_specs=[VMEM_SPEC] * (NPOOL + 1),
        scratch_shapes=[
            VMEM((NBLK * LOCAL * QROT * 32, 128), F32),
            VMEM((table_rows, 256 * STEP_TILES), BF16),
            VMEM((table_rows, 256 * STEP_TILES), BF16),
            VMEM((table_rows, NPOOL * ROWS), F32),
            VMEM((NPOOL, 56, NPOOL * ROWS), F32),
            VMEM((8, NPOOL * ROWS), jnp.int32),
            pltpu.SemaphoreType.DMA((6,)),
        ],
        compiler_params=params(20),
        name="score",
    )(
        q, gathered.reshape(NBLK * LOCAL * QROT * 32, 128), *parts,
        wc, ws, weight, cand, cand_far, cand_near,
    )
    terms = trade(terms, POOL)

    sums, log_evidence = pl.pallas_call(
        class_kernel,
        out_shape=(
            jax.ShapeDtypeStruct((NBLK, 16, COLS), BF16),
            jax.ShapeDtypeStruct((1, ROWS), F32),
        ),
        in_specs=[SMEM_SPEC] + [VMEM_SPEC] * 7,
        out_specs=(VMEM_SPEC, VMEM_SPEC),
        scratch_shapes=[
            VMEM((NSHIFT * 16, NPOOL * ROWS), F32),
            VMEM((1, NPOOL * ROWS), F32),
        ],
        compiler_params=params(16),
        name="classes",
    )(q, *terms, pool, cosine, sine)
    sums = lax.all_to_all(sums, BLK, 0, 0, tiled=True)

    class_ids = jnp.arange(CLASSES, dtype=jnp.int32)
    shared_owner = class_owner[:, None] == class_owner[None, :]
    earlier = class_ids[:, None] < class_ids[None, :]
    position = jnp.sum((shared_owner & earlier).astype(jnp.int32), axis=0)
    target = class_owner * SLOTS + position
    mine = lax.dynamic_slice(target, (pool_index * QCLS,), (QCLS,))
    mine = jnp.pad(mine, (0, 128 - QCLS), constant_values=-1).reshape(1, 128)
    placed = pl.pallas_call(
        place_kernel,
        out_shape=pltpu.HBM((NDOM, SLOTS, COLS + 128), BF16),
        in_specs=[VMEM_SPEC, VMEM_SPEC],
        out_specs=pl.BlockSpec(memory_space=pltpu.HBM),
        scratch_shapes=[VMEM((NDOM, SLOTS, COLS + 128), BF16), pltpu.SemaphoreType.DMA],
        compiler_params=params(4),
        name="place",
    )(mine, sums)
    placed = lax.all_to_all(placed, DOM, 0, 0, tiled=True)
    means, mass = pl.pallas_call(
        mean_kernel,
        out_shape=(
            jax.ShapeDtypeStruct((SLOTS, COLS), F32),
            jax.ShapeDtypeStruct((SLOTS,), F32),
        ),
        in_specs=[VMEM_SPEC],
        out_specs=(VMEM_SPEC, VMEM_SPEC),
        compiler_params=params(4),
        name="means",
    )(placed)
    return (means, mass, log_evidence.reshape(ROWS))


def solution(mesh):
    fine = Mesh(
        np.asarray(mesh.devices).reshape([size for _, size in FINE]), [name for name, _ in FINE]
    )
    every = DOM + BLK
    return jax.shard_map(
        on_device,
        mesh=fine,
        in_specs=(P(every, None), P(BLK, None, None), P(), P(), P(every, None), P()),
        out_specs=(P(DOM, BLK), P(DOM), P(every)),
        check_vma=False,
    )
```

```python
import math

import jax
import jax.numpy as jnp
import numpy as np
from jax import lax
from jax.experimental import pallas as pl
from jax.experimental.pallas import tpu as pltpu
from jax.sharding import Mesh, PartitionSpec as P

KROW = 64
KCOL = 32
BOX = 256
SLOTS = 8
INV_TEMP = 4.0
FLOOR = -1e30

FINE = (("xh", 2), ("yh", 2), ("yl", 2), ("core", 2), ("z", 8), ("xl", 2))
DOM = ("xh", "yh", "yl", "core")
BLK = ("z", "xl")
POOL = ("yl", "core")

K = 2048
CLASSES = 48
ROT = 12
NSHIFT = 4
ROWS = 128
FIRST = 64
NPOOL = 4
QROT = ROT // NPOOL
QCLS = CLASSES // NPOOL
NBLK = 16
NDOM = 16
LOCAL = 3
COLS = 256
STEP_TILES = 4
F32 = jnp.float32
BF16 = jnp.bfloat16
VMEM = pltpu.VMEM
SMEM_SPEC = pl.BlockSpec(memory_space=pltpu.SMEM)
VMEM_SPEC = pl.BlockSpec(memory_space=pltpu.VMEM)
ANY_SPEC = pl.BlockSpec(memory_space=pl.ANY)
HBM_SPEC = pl.BlockSpec(memory_space=pltpu.HBM)


def params(mib):
    return pltpu.CompilerParams(vmem_limit_bytes=mib << 20)


def pack_kernel(q_ref, refs_ref, out_ref, wide, rows):
    q = q_ref[0]
    wide[...] = refs_ref[...].astype(F32)
    for c in range(LOCAL):
        for r in range(QROT):
            row = wide[c, pl.ds(QROT * q + r, 1), :]
            for a in range(32):
                at = (c * QROT + r) * 32 + a
                rows[at : at + 1, :] = row[:, a * 128 : (a + 1) * 128]
    packed = rows[...].astype(BF16)
    for d in range(NBLK):
        out_ref[d] = packed


def tables_kernel(off_ref, w_ref, c0_ref, c1_ref, cos_ref, sin_ref, wc_ref, ws_ref, both_ref):
    row = lax.broadcasted_iota(jnp.int32, (16, 128), 0)
    lane = lax.broadcasted_iota(jnp.int32, (16, 128), 1)
    column = lane % KCOL
    rowpos = row * (128 // KCOL) + lane // KCOL - KROW // 2
    weight = w_ref[...]
    for s in range(NSHIFT):
        turns = (off_ref[s, 0] * column + off_ref[s, 1] * rowpos).astype(F32)
        angle = turns * (2.0 * math.pi / BOX)
        cosine, sine = jnp.cos(angle), jnp.sin(angle)
        at = slice(s * 16, (s + 1) * 16)
        cos_ref[at, :] = cosine
        sin_ref[at, :] = sine
        wc_ref[at, :] = weight * cosine
        ws_ref[at, :] = weight * sine
    both_ref[0] = c0_ref[...]
    both_ref[1] = c1_ref[...]


def pool_copies(q, parts, pool, sem):
    copies = []
    places = ((0, 0), (1, 0), (2, 0), (2, FIRST), (3, 0), (3, FIRST))
    for i, (part, (j, offset)) in enumerate(zip(parts, places)):
        rows = pl.ds(pl.multiple_of((q ^ j) * ROWS + offset, 16), part.shape[0])
        copies.append(pltpu.make_async_copy(part, pool.at[rows, :], sem.at[i]))
    return copies


def split(x):
    high = x.astype(BF16).astype(F32)
    middle = (x - high).astype(BF16).astype(F32)
    return (high, middle, x - high - middle)


def score_kernel(
    q_ref, refs_ref, p0, p1, p2, p3, p4, p5, wc_ref, ws_ref, w_ref, c0_ref, c1_ref, c23_ref,
    own_ref, near_ref, far_ref, cross_ref, pool,
    wide, table0, table1, scores, groups, cands, sem
):
    q = q_ref[0]
    steps = 16 // STEP_TILES
    wide_cols = 128 * STEP_TILES
    copies = pool_copies(q, (p0, p1, p2, p3, p4, p5), pool, sem)
    for copy in copies:
        copy.start()
    for j, cand in enumerate((c0_ref[...], c23_ref[0], c1_ref[...], c23_ref[1])):
        cands[:, pl.ds(pl.multiple_of((q ^ j) * ROWS, ROWS), ROWS)] = cand
    wide[...] = refs_ref[...].astype(F32)
    energy = [jnp.zeros((CLASSES, 128), F32) for _ in range(QROT)]
    stride = QROT * 32
    tables = (table0, table1)

    def build(step):
        table = tables[step % 2]
        for t in range(STEP_TILES):
            a = step * STEP_TILES + t
            weight = w_ref[a : a + 1, :]
            for r in range(QROT):
                real = wide[pl.ds(r * 32 + a, CLASSES, stride=stride), :]
                imag = wide[pl.ds(r * 32 + 16 + a, CLASSES, stride=stride), :]
                energy[r] = energy[r] + weight * (real * real + imag * imag)
                for s in range(NSHIFT):
                    wc = wc_ref[s * 16 + a : s * 16 + a + 1, :]
                    ws = ws_ref[s * 16 + a : s * 16 + a + 1, :]
                    row = (s * QROT + r) * CLASSES
                    at = slice(t * 128, (t + 1) * 128)
                    at_im = slice(wide_cols + t * 128, wide_cols + (t + 1) * 128)
                    table[row : row + CLASSES, at] = (wc * real - ws * imag).astype(BF16)
                    table[row : row + CLASSES, at_im] = (ws * real + wc * imag).astype(BF16)

    build(0)
    for copy in copies:
        copy.wait()
    for step in range(steps):
        if step + 1 < steps:
            build(step + 1)
        table = tables[step % 2]
        cols = slice(step * wide_cols, (step + 1) * wide_cols)
        cols_im = slice(K + step * wide_cols, K + (step + 1) * wide_cols)
        for n in range(2):
            lanes = slice(n * 256, (n + 1) * 256)
            part = lax.dot_general(
                table[:, 0:wide_cols], pool[lanes, cols], (((1,), (1,)), ((), ())),
                preferred_element_type=F32,
            ) + lax.dot_general(
                table[:, wide_cols:], pool[lanes, cols_im], (((1,), (1,)), ((), ())),
                preferred_element_type=F32,
            )
            if step == 0:
                scores[:, lanes] = part
            else:
                scores[:, lanes] += part

    half_energy = [0.5 * jnp.sum(e, axis=1, keepdims=True) for e in energy]
    class_id = lax.broadcasted_iota(jnp.int32, (CLASSES, 256), 0)
    for n in range(2):
        lanes = slice(n * 256, (n + 1) * 256)
        cand = cands[:, lanes]
        allowed = class_id == cand[0:1, :]
        for k in range(1, 8):
            allowed = allowed | (class_id == cand[k : k + 1, :])
        loglik = []
        for s in range(NSHIFT):
            for r in range(QROT):
                row = (s * QROT + r) * CLASSES
                value = INV_TEMP * (scores[row : row + CLASSES, lanes] - half_energy[r])
                loglik.append(jnp.where(allowed, value, FLOOR))
        top = loglik[0]
        for value in loglik[1:]:
            top = jnp.maximum(top, value)
        peak = jnp.max(top, axis=0, keepdims=True)
        evidence = jnp.zeros((1, 256), F32)
        for s in range(NSHIFT):
            terms = jnp.zeros((CLASSES, 256), F32)
            for r in range(QROT):
                value = loglik[s * QROT + r]
                terms = terms + jnp.where(allowed, jnp.exp(value - peak), 0.0)
            evidence = evidence + jnp.sum(terms, axis=0, keepdims=True)
            for d in range(NPOOL):
                groups[d, s * QCLS : (s + 1) * QCLS, lanes] = terms[d * QCLS : (d + 1) * QCLS]
        pieces = split(peak) + split(evidence)
        for d in range(NPOOL):
            for i, piece in enumerate(pieces):
                groups[d, 48 + i : 49 + i, lanes] = piece
            groups[d, 54:56, lanes] = jnp.zeros((2, 256), F32)
    own_ref[...] = groups[q]
    for j, ref in enumerate((near_ref, far_ref, cross_ref)):
        ref[...] = groups[q ^ (j + 1)].astype(BF16)


def class_kernel(
    q_ref, x0, x1, x2, x3, pool, cos_ref, sin_ref, out_ref, log_ref, slots, line
):
    q = q_ref[0]
    parts = [x[...].astype(F32) for x in (x0, x1, x2, x3)]
    peaks = [x[48:49] + x[49:50] + x[50:51] for x in parts]
    peak = peaks[0]
    for value in peaks[1:]:
        peak = jnp.maximum(peak, value)
    evidence = jnp.zeros_like(peak)
    terms = jnp.zeros((NSHIFT * QCLS, NPOOL * ROWS), F32)
    for x, value in zip(parts, peaks):
        scale = jnp.exp(value - peak)
        evidence = evidence + scale * (x[51:52] + x[52:53] + x[53:54])
        terms = terms + scale * x[0:48]
    line[...] = peak + jnp.log(evidence)
    log_ref[...] = line[:, pl.ds(pl.multiple_of(q * ROWS, ROWS), ROWS)]
    probs = terms / evidence
    for s in range(NSHIFT):
        slots[s * 16 : s * 16 + QCLS, :] = probs[s * QCLS : (s + 1) * QCLS]
        slots[s * 16 + QCLS : (s + 1) * 16, :] = jnp.zeros((4, NPOOL * ROWS), F32)
    padded = slots[...]
    mass = jnp.sum(padded, axis=1, keepdims=True)
    mass = mass[0:16] + mass[16:32] + mass[32:48] + mass[48:64]
    low = padded.astype(BF16)
    row_id = lax.broadcasted_iota(jnp.int32, (16, COLS), 0)
    lane_id = lax.broadcasted_iota(jnp.int32, (16, COLS), 1)
    mass_row = jnp.sum(jnp.where(row_id == lane_id, mass, 0.0), axis=0, keepdims=True)
    mass_high = mass_row.astype(BF16).astype(F32)
    mass_low = mass_row - mass_high
    for b in range(NBLK // 2):
        cols = slice(b * COLS, (b + 1) * COLS)
        cols_im = slice(K + b * COLS, K + (b + 1) * COLS)
        g_re = jnp.dot(low, pool[:, cols], preferred_element_type=F32)
        g_im = jnp.dot(low, pool[:, cols_im], preferred_element_type=F32)
        sum_re = jnp.zeros((16, COLS), F32)
        sum_im = jnp.zeros((16, COLS), F32)
        for s in range(NSHIFT):
            at = s * 16 + 2 * b
            c = jnp.concatenate([cos_ref[at : at + 1, :], cos_ref[at + 1 : at + 2, :]], axis=1)
            z = jnp.concatenate([sin_ref[at : at + 1, :], sin_ref[at + 1 : at + 2, :]], axis=1)
            re = g_re[s * 16 : (s + 1) * 16]
            im = g_im[s * 16 : (s + 1) * 16]
            sum_re = sum_re + (c * re + z * im)
            sum_im = sum_im + (c * im - z * re)
        for dest, value in ((b, sum_re), (NBLK // 2 + b, sum_im)):
            value = jnp.where(row_id == QCLS, mass_high, value)
            value = jnp.where(row_id == QCLS + 1, mass_low, value)
            out_ref[dest] = value.astype(BF16)


def place_kernel(target_ref, y_ref, out_hbm, out_ref, sem):
    total = y_ref[0].astype(F32)
    for b in range(1, NBLK):
        total = total + y_ref[b].astype(F32)
    mass = total[QCLS : QCLS + 1, 0:128] + total[QCLS + 1 : QCLS + 2, 0:128]
    row = lax.broadcasted_iota(jnp.int32, (NDOM * SLOTS, 128), 0)
    hit = target_ref[...] == row
    pick = jnp.where(hit, 1.0, 0.0).astype(BF16)
    placed = jnp.dot(pick[:, 0:16], total.astype(BF16), preferred_element_type=F32)
    placed_mass = jnp.sum(jnp.where(hit, mass, 0.0), axis=1, keepdims=True)
    high = placed_mass.astype(BF16).astype(F32)
    lane = lax.broadcasted_iota(jnp.int32, (NDOM * SLOTS, 128), 1)
    extra = jnp.where(lane == 0, high, jnp.where(lane == 1, placed_mass - high, 0.0))
    out_ref[:, :, 0:COLS] = placed.reshape(NDOM, SLOTS, COLS).astype(BF16)
    out_ref[:, :, COLS:] = extra.reshape(NDOM, SLOTS, 128).astype(BF16)
    send = pltpu.make_async_copy(out_ref, out_hbm, sem)
    send.start()
    send.wait()


def mean_kernel(z_ref, mean_ref, mass_ref):
    total = z_ref[0].astype(F32)
    for d in range(1, NDOM):
        total = total + z_ref[d].astype(F32)
    mass = total[:, COLS : COLS + 1] + total[:, COLS + 1 : COLS + 2]
    mean_ref[...] = total[:, 0:COLS] / (mass + 1.0)
    row = lax.broadcasted_iota(jnp.int32, (SLOTS, 128), 0)
    lane = lax.broadcasted_iota(jnp.int32, (SLOTS, 128), 1)
    mass_ref[...] = jnp.sum(jnp.where(row == lane, mass, 0.0), axis=0)[0:SLOTS]


def in_hbm(x):
    return pltpu.with_memory_space_constraint(x, pltpu.HBM)


def swap(x, axis):
    return lax.ppermute(x, axis, [(0, 1), (1, 0)])


def trade(parts, axes):
    own, near, far, cross = parts
    return (
        own,
        swap(near, axes[1]),
        swap(far, axes[0]),
        lax.ppermute(cross, axes, [(i, 3 - i) for i in range(4)]),
    )


def on_device(particles, references, noise_weight, offsets, candidates, class_owner):
    pool_index = (lax.axis_index("yl") * 2 + lax.axis_index("core")).astype(jnp.int32)
    q = pool_index.reshape(1)

    cand = candidates.T
    weight = noise_weight.reshape(16, 128)
    far0 = swap(particles[:FIRST], "yl")
    packed = pl.pallas_call(
        pack_kernel,
        out_shape=jax.ShapeDtypeStruct((NBLK, LOCAL * QROT * 32, 128), BF16),
        in_specs=[SMEM_SPEC, VMEM_SPEC],
        out_specs=VMEM_SPEC,
        scratch_shapes=[VMEM((LOCAL, ROT, 2 * K), F32), VMEM((LOCAL * QROT * 32, 128), F32)],
        compiler_params=params(16),
        name="pack",
    )(q, references)
    packed, whole = lax.optimization_barrier((packed, particles))
    rest = whole[FIRST:]
    gathered = lax.all_to_all(packed, BLK, 0, 0, tiled=True)
    rest, far0 = lax.optimization_barrier((rest, far0))
    far1 = swap(rest, "yl")
    near = swap(particles, "core")
    cand, far0 = lax.optimization_barrier((cand, far0))
    cand_far = swap(cand, "yl")
    flat = jax.ShapeDtypeStruct((NSHIFT * 16, 128), F32)
    cosine, sine, wc, ws, both = pl.pallas_call(
        tables_kernel,
        out_shape=(flat, flat, flat, flat, jax.ShapeDtypeStruct((2, 8, ROWS), jnp.int32)),
        in_specs=[SMEM_SPEC] + [VMEM_SPEC] * 3,
        out_specs=(VMEM_SPEC,) * 5,
        compiler_params=params(4),
        cost_estimate=pl.CostEstimate(flops=10 * 10**9, bytes_accessed=30 * 10**6, transcendentals=0),
        name="tables",
    )(offsets, weight, cand, cand_far)
    far1, wc, both = lax.optimization_barrier((far1, wc, both))
    near1 = swap(far1, "core")
    cand_near = swap(both, "core")
    far0, near1 = lax.optimization_barrier((far0, near1))
    near0 = swap(far0, "core")
    parts = (in_hbm(particles), near, far0, far1, near0, in_hbm(near1))

    table_rows = NSHIFT * QROT * CLASSES
    *terms, pool = pl.pallas_call(
        score_kernel,
        out_shape=[
            jax.ShapeDtypeStruct((56, NPOOL * ROWS), F32 if j == 0 else BF16) for j in range(NPOOL)
        ]
        + [jax.ShapeDtypeStruct((NPOOL * ROWS, 2 * K), BF16)],
        in_specs=[SMEM_SPEC, VMEM_SPEC] + [HBM_SPEC] + [ANY_SPEC] * 5 + [VMEM_SPEC] * 6,
        out_specs=[VMEM_SPEC] * (NPOOL + 1),
        scratch_shapes=[
            VMEM((NBLK * LOCAL * QROT * 32, 128), F32),
            VMEM((table_rows, 256 * STEP_TILES), BF16),
            VMEM((table_rows, 256 * STEP_TILES), BF16),
            VMEM((table_rows, NPOOL * ROWS), F32),
            VMEM((NPOOL, 56, NPOOL * ROWS), F32),
            VMEM((8, NPOOL * ROWS), jnp.int32),
            pltpu.SemaphoreType.DMA((6,)),
        ],
        compiler_params=params(20),
        name="score",
    )(
        q, gathered.reshape(NBLK * LOCAL * QROT * 32, 128), *parts,
        wc, ws, weight, cand, cand_far, cand_near,
    )
    terms = trade(terms, POOL)

    sums, log_evidence = pl.pallas_call(
        class_kernel,
        out_shape=(
            jax.ShapeDtypeStruct((NBLK, 16, COLS), BF16),
            jax.ShapeDtypeStruct((1, ROWS), F32),
        ),
        in_specs=[SMEM_SPEC] + [VMEM_SPEC] * 7,
        out_specs=(VMEM_SPEC, VMEM_SPEC),
        scratch_shapes=[
            VMEM((NSHIFT * 16, NPOOL * ROWS), F32),
            VMEM((1, NPOOL * ROWS), F32),
        ],
        compiler_params=params(16),
        name="classes",
    )(q, *terms, pool, cosine, sine)
    sums = lax.all_to_all(sums, BLK, 0, 0, tiled=True)

    class_ids = jnp.arange(CLASSES, dtype=jnp.int32)
    shared_owner = class_owner[:, None] == class_owner[None, :]
    earlier = class_ids[:, None] < class_ids[None, :]
    position = jnp.sum((shared_owner & earlier).astype(jnp.int32), axis=0)
    target = class_owner * SLOTS + position
    mine = lax.dynamic_slice(target, (pool_index * QCLS,), (QCLS,))
    mine = jnp.pad(mine, (0, 128 - QCLS), constant_values=-1).reshape(1, 128)
    placed = pl.pallas_call(
        place_kernel,
        out_shape=pltpu.HBM((NDOM, SLOTS, COLS + 128), BF16),
        in_specs=[VMEM_SPEC, VMEM_SPEC],
        out_specs=pl.BlockSpec(memory_space=pltpu.HBM),
        scratch_shapes=[VMEM((NDOM, SLOTS, COLS + 128), BF16), pltpu.SemaphoreType.DMA],
        compiler_params=params(4),
        name="place",
    )(mine, sums)
    placed = lax.all_to_all(placed, DOM, 0, 0, tiled=True)
    means, mass = pl.pallas_call(
        mean_kernel,
        out_shape=(
            jax.ShapeDtypeStruct((SLOTS, COLS), F32),
            jax.ShapeDtypeStruct((SLOTS,), F32),
        ),
        in_specs=[VMEM_SPEC],
        out_specs=(VMEM_SPEC, VMEM_SPEC),
        compiler_params=params(4),
        name="means",
    )(placed)
    return (means, mass, log_evidence.reshape(ROWS))


def solution(mesh):
    fine = Mesh(
        np.asarray(mesh.devices).reshape([size for _, size in FINE]), [name for name, _ in FINE]
    )
    every = DOM + BLK
    return jax.shard_map(
        on_device,
        mesh=fine,
        in_specs=(P(every, None), P(BLK, None, None), P(), P(), P(every, None), P()),
        out_specs=(P(DOM, BLK), P(DOM), P(every)),
        check_vma=False,
    )
```

```python
import math

import jax
import jax.numpy as jnp
import numpy as np
from jax import lax
from jax.experimental import pallas as pl
from jax.experimental.pallas import tpu as pltpu
from jax.sharding import Mesh, PartitionSpec as P

KROW = 64
KCOL = 32
BOX = 256
SLOTS = 8
INV_TEMP = 4.0
FLOOR = -1e30

FINE = (("xh", 2), ("yh", 2), ("yl", 2), ("core", 2), ("z", 8), ("xl", 2))
DOM = ("xh", "yh", "yl", "core")
BLK = ("z", "xl")
POOL = ("yl", "core")

K = 2048
CLASSES = 48
ROT = 12
NSHIFT = 4
ROWS = 128
EXTENDED = ROWS + 8
NPOOL = 4
QROT = ROT // NPOOL
QCLS = CLASSES // NPOOL
NBLK = 16
NDOM = 16
LOCAL = 3
BLOCK = LOCAL * QROT * 32
COLS = 256
STEP_TILES = 4
F32 = jnp.float32
BF16 = jnp.bfloat16
VMEM = pltpu.VMEM
SMEM_SPEC = pl.BlockSpec(memory_space=pltpu.SMEM)
VMEM_SPEC = pl.BlockSpec(memory_space=pltpu.VMEM)
ANY_SPEC = pl.BlockSpec(memory_space=pl.ANY)
HBM_SPEC = pl.BlockSpec(memory_space=pltpu.HBM)


def params(mib):
    return pltpu.CompilerParams(vmem_limit_bytes=mib << 20)


def pack_kernel(q_ref, refs_ref, out_ref, wide, rows):
    q = q_ref[0]
    wide[...] = refs_ref[...].astype(F32)
    for c in range(LOCAL):
        for r in range(QROT):
            row = wide[c, pl.ds(QROT * q + r, 1), :]
            for a in range(32):
                at = (c * QROT + r) * 32 + a
                rows[at : at + 1, :] = row[:, a * 128 : (a + 1) * 128]
    out_ref[...] = rows[...].astype(BF16)


def extend_kernel(cand_ref, particles_hbm, out_ref, sem):
    copy = pltpu.make_async_copy(particles_hbm, out_ref.at[pl.ds(0, ROWS), :], sem)
    copy.start()
    out_ref[ROWS:EXTENDED, 0:128] = cand_ref[...].astype(F32).astype(BF16)
    out_ref[ROWS:EXTENDED, 128:] = jnp.zeros((8, 2 * K - 128), BF16)
    copy.wait()


def tables_kernel(off_ref, w_ref, cos_ref, sin_ref, wc_ref, ws_ref):
    row = lax.broadcasted_iota(jnp.int32, (16, 128), 0)
    lane = lax.broadcasted_iota(jnp.int32, (16, 128), 1)
    column = lane % KCOL
    rowpos = row * (128 // KCOL) + lane // KCOL - KROW // 2
    weight = w_ref[...]
    for s in range(NSHIFT):
        turns = (off_ref[s, 0] * column + off_ref[s, 1] * rowpos).astype(F32)
        angle = turns * (2.0 * math.pi / BOX)
        cosine, sine = jnp.cos(angle), jnp.sin(angle)
        at = slice(s * 16, (s + 1) * 16)
        cos_ref[at, :] = cosine
        sin_ref[at, :] = sine
        wc_ref[at, :] = weight * cosine
        ws_ref[at, :] = weight * sine


def pool_copies(q, parts, pool, listed, sem):
    copies = []
    for j, part in enumerate(parts):
        rows = pl.ds(pl.multiple_of((q ^ j) * ROWS, ROWS), ROWS)
        copies.append(pltpu.make_async_copy(part.at[pl.ds(0, ROWS), :], pool.at[rows, :], sem.at[0, j]))
        few = part.at[pl.ds(ROWS, 8), pl.ds(0, ROWS)]
        copies.append(pltpu.make_async_copy(few, listed.at[j], sem.at[1, j]))
    return copies


def split(x):
    high = x.astype(BF16).astype(F32)
    middle = (x - high).astype(BF16).astype(F32)
    return (high, middle, x - high - middle)


def score_kernel(
    index_ref, *refs
):
    blocks = refs[:NBLK]
    p0, p1, p2, p3, wc_ref, ws_ref, w_ref = refs[NBLK : NBLK + 7]
    own_ref, near_ref, far_ref, cross_ref, pool = refs[NBLK + 7 : NBLK + 12]
    wide, table0, table1, scores, groups, cands, listed, sem = refs[NBLK + 12 :]
    q, z, xl = index_ref[0], index_ref[1], index_ref[2]
    steps = 16 // STEP_TILES
    wide_cols = 128 * STEP_TILES
    copies = pool_copies(q, (p0, p1, p2, p3), pool, listed, sem)
    for copy in copies:
        copy.start()
    for i, block in enumerate(blocks):
        source = ((z + NBLK // 2 - i // 2) % (NBLK // 2)) * 2 + (xl ^ (i % 2))
        wide[pl.ds(pl.multiple_of(source * BLOCK, BLOCK), BLOCK), :] = block[...].astype(F32)
    energy = [jnp.zeros((CLASSES, 128), F32) for _ in range(QROT)]
    stride = QROT * 32
    tables = (table0, table1)

    def build(step):
        table = tables[step % 2]
        for t in range(STEP_TILES):
            a = step * STEP_TILES + t
            weight = w_ref[a : a + 1, :]
            for r in range(QROT):
                real = wide[pl.ds(r * 32 + a, CLASSES, stride=stride), :]
                imag = wide[pl.ds(r * 32 + 16 + a, CLASSES, stride=stride), :]
                energy[r] = energy[r] + weight * (real * real + imag * imag)
                for s in range(NSHIFT):
                    wc = wc_ref[s * 16 + a : s * 16 + a + 1, :]
                    ws = ws_ref[s * 16 + a : s * 16 + a + 1, :]
                    row = (s * QROT + r) * CLASSES
                    at = slice(t * 128, (t + 1) * 128)
                    at_im = slice(wide_cols + t * 128, wide_cols + (t + 1) * 128)
                    table[row : row + CLASSES, at] = (wc * real - ws * imag).astype(BF16)
                    table[row : row + CLASSES, at_im] = (ws * real + wc * imag).astype(BF16)

    build(0)
    for copy in copies:
        copy.wait()
    for j in range(NPOOL):
        cand = listed[j].astype(F32).astype(jnp.int32)
        cands[:, pl.ds(pl.multiple_of((q ^ j) * ROWS, ROWS), ROWS)] = cand
    for step in range(steps):
        if step + 1 < steps:
            build(step + 1)
        table = tables[step % 2]
        cols = slice(step * wide_cols, (step + 1) * wide_cols)
        cols_im = slice(K + step * wide_cols, K + (step + 1) * wide_cols)
        for n in range(2):
            lanes = slice(n * 256, (n + 1) * 256)
            part = lax.dot_general(
                table[:, 0:wide_cols], pool[lanes, cols], (((1,), (1,)), ((), ())),
                preferred_element_type=F32,
            ) + lax.dot_general(
                table[:, wide_cols:], pool[lanes, cols_im], (((1,), (1,)), ((), ())),
                preferred_element_type=F32,
            )
            if step == 0:
                scores[:, lanes] = part
            else:
                scores[:, lanes] += part

    half_energy = [0.5 * jnp.sum(e, axis=1, keepdims=True) for e in energy]
    class_id = lax.broadcasted_iota(jnp.int32, (CLASSES, 256), 0)
    for n in range(2):
        lanes = slice(n * 256, (n + 1) * 256)
        cand = cands[:, lanes]
        allowed = class_id == cand[0:1, :]
        for k in range(1, 8):
            allowed = allowed | (class_id == cand[k : k + 1, :])
        loglik = []
        for s in range(NSHIFT):
            for r in range(QROT):
                row = (s * QROT + r) * CLASSES
                value = INV_TEMP * (scores[row : row + CLASSES, lanes] - half_energy[r])
                loglik.append(jnp.where(allowed, value, FLOOR))
        top = loglik[0]
        for value in loglik[1:]:
            top = jnp.maximum(top, value)
        peak = jnp.max(top, axis=0, keepdims=True)
        evidence = jnp.zeros((1, 256), F32)
        for s in range(NSHIFT):
            terms = jnp.zeros((CLASSES, 256), F32)
            for r in range(QROT):
                value = loglik[s * QROT + r]
                terms = terms + jnp.where(allowed, jnp.exp(value - peak), 0.0)
            evidence = evidence + jnp.sum(terms, axis=0, keepdims=True)
            for d in range(NPOOL):
                groups[d, s * QCLS : (s + 1) * QCLS, lanes] = terms[d * QCLS : (d + 1) * QCLS]
        pieces = split(peak) + split(evidence)
        for d in range(NPOOL):
            for i, piece in enumerate(pieces):
                groups[d, 48 + i : 49 + i, lanes] = piece
            groups[d, 54:56, lanes] = jnp.zeros((2, 256), F32)
    own_ref[...] = groups[q]
    for j, ref in enumerate((near_ref, far_ref, cross_ref)):
        ref[...] = groups[q ^ (j + 1)].astype(BF16)


def class_kernel(
    q_ref, x0, x1, x2, x3, pool, cos_ref, sin_ref, out_ref, log_ref, slots, line
):
    q = q_ref[0]
    parts = [x[...].astype(F32) for x in (x0, x1, x2, x3)]
    peaks = [x[48:49] + x[49:50] + x[50:51] for x in parts]
    peak = peaks[0]
    for value in peaks[1:]:
        peak = jnp.maximum(peak, value)
    evidence = jnp.zeros_like(peak)
    terms = jnp.zeros((NSHIFT * QCLS, NPOOL * ROWS), F32)
    for x, value in zip(parts, peaks):
        scale = jnp.exp(value - peak)
        evidence = evidence + scale * (x[51:52] + x[52:53] + x[53:54])
        terms = terms + scale * x[0:48]
    line[...] = peak + jnp.log(evidence)
    log_ref[...] = line[:, pl.ds(pl.multiple_of(q * ROWS, ROWS), ROWS)]
    probs = terms / evidence
    for s in range(NSHIFT):
        slots[s * 16 : s * 16 + QCLS, :] = probs[s * QCLS : (s + 1) * QCLS]
        slots[s * 16 + QCLS : (s + 1) * 16, :] = jnp.zeros((4, NPOOL * ROWS), F32)
    padded = slots[...]
    mass = jnp.sum(padded, axis=1, keepdims=True)
    mass = mass[0:16] + mass[16:32] + mass[32:48] + mass[48:64]
    low = padded.astype(BF16)
    row_id = lax.broadcasted_iota(jnp.int32, (16, COLS), 0)
    lane_id = lax.broadcasted_iota(jnp.int32, (16, COLS), 1)
    mass_row = jnp.sum(jnp.where(row_id == lane_id, mass, 0.0), axis=0, keepdims=True)
    mass_high = mass_row.astype(BF16).astype(F32)
    mass_low = mass_row - mass_high
    for b in range(NBLK // 2):
        cols = slice(b * COLS, (b + 1) * COLS)
        cols_im = slice(K + b * COLS, K + (b + 1) * COLS)
        g_re = jnp.dot(low, pool[:, cols], preferred_element_type=F32)
        g_im = jnp.dot(low, pool[:, cols_im], preferred_element_type=F32)
        sum_re = jnp.zeros((16, COLS), F32)
        sum_im = jnp.zeros((16, COLS), F32)
        for s in range(NSHIFT):
            at = s * 16 + 2 * b
            c = jnp.concatenate([cos_ref[at : at + 1, :], cos_ref[at + 1 : at + 2, :]], axis=1)
            z = jnp.concatenate([sin_ref[at : at + 1, :], sin_ref[at + 1 : at + 2, :]], axis=1)
            re = g_re[s * 16 : (s + 1) * 16]
            im = g_im[s * 16 : (s + 1) * 16]
            sum_re = sum_re + (c * re + z * im)
            sum_im = sum_im + (c * im - z * re)
        for dest, value in ((b, sum_re), (NBLK // 2 + b, sum_im)):
            value = jnp.where(row_id == QCLS, mass_high, value)
            value = jnp.where(row_id == QCLS + 1, mass_low, value)
            out_ref[dest] = value.astype(BF16)


def place_kernel(target_ref, y_ref, out_hbm, out_ref, sem):
    total = y_ref[0].astype(F32)
    for b in range(1, NBLK):
        total = total + y_ref[b].astype(F32)
    mass = total[QCLS : QCLS + 1, 0:128] + total[QCLS + 1 : QCLS + 2, 0:128]
    row = lax.broadcasted_iota(jnp.int32, (NDOM * SLOTS, 128), 0)
    hit = target_ref[...] == row
    pick = jnp.where(hit, 1.0, 0.0).astype(BF16)
    placed = jnp.dot(pick[:, 0:16], total.astype(BF16), preferred_element_type=F32)
    placed_mass = jnp.sum(jnp.where(hit, mass, 0.0), axis=1, keepdims=True)
    high = placed_mass.astype(BF16).astype(F32)
    lane = lax.broadcasted_iota(jnp.int32, (NDOM * SLOTS, 128), 1)
    extra = jnp.where(lane == 0, high, jnp.where(lane == 1, placed_mass - high, 0.0))
    out_ref[:, :, 0:COLS] = placed.reshape(NDOM, SLOTS, COLS).astype(BF16)
    out_ref[:, :, COLS:] = extra.reshape(NDOM, SLOTS, 128).astype(BF16)
    send = pltpu.make_async_copy(out_ref, out_hbm, sem)
    send.start()
    send.wait()


def mean_kernel(z_ref, mean_ref, mass_ref):
    total = z_ref[0].astype(F32)
    for d in range(1, NDOM):
        total = total + z_ref[d].astype(F32)
    mass = total[:, COLS : COLS + 1] + total[:, COLS + 1 : COLS + 2]
    mean_ref[...] = total[:, 0:COLS] / (mass + 1.0)
    row = lax.broadcasted_iota(jnp.int32, (SLOTS, 128), 0)
    lane = lax.broadcasted_iota(jnp.int32, (SLOTS, 128), 1)
    mass_ref[...] = jnp.sum(jnp.where(row == lane, mass, 0.0), axis=0)[0:SLOTS]


def in_hbm(x):
    return pltpu.with_memory_space_constraint(x, pltpu.HBM)


def swap(x, axis):
    return lax.ppermute(x, axis, [(0, 1), (1, 0)])


def trade(parts, axes):
    own, near, far, cross = parts
    return (
        own,
        swap(near, axes[1]),
        swap(far, axes[0]),
        lax.ppermute(cross, axes, [(i, 3 - i) for i in range(4)]),
    )


def on_device(particles, references, noise_weight, offsets, candidates, class_owner):
    pool_index = (lax.axis_index("yl") * 2 + lax.axis_index("core")).astype(jnp.int32)
    q = pool_index.reshape(1)

    zi, xi = lax.axis_index("z").astype(jnp.int32), lax.axis_index("xl").astype(jnp.int32)
    place = jnp.stack([pool_index, zi, xi])
    weight = noise_weight.reshape(16, 128)
    particles = pl.pallas_call(
        extend_kernel,
        out_shape=jax.ShapeDtypeStruct((EXTENDED, 2 * K), BF16),
        in_specs=[VMEM_SPEC, HBM_SPEC],
        out_specs=VMEM_SPEC,
        scratch_shapes=[pltpu.SemaphoreType.DMA],
        compiler_params=params(4),
        name="extend",
    )(candidates.T, in_hbm(particles))
    far = swap(particles, "yl")
    packed = pl.pallas_call(
        pack_kernel,
        out_shape=jax.ShapeDtypeStruct((BLOCK, 128), BF16),
        in_specs=[SMEM_SPEC, VMEM_SPEC],
        out_specs=VMEM_SPEC,
        scratch_shapes=[VMEM((LOCAL, ROT, 2 * K), F32), VMEM((BLOCK, 128), F32)],
        compiler_params=params(16),
        name="pack",
    )(q, references)
    depth = NBLK // 2
    along = [packed] + [
        lax.ppermute(packed, "z", [(i, (i + k) % depth) for i in range(depth)])
        for k in range(1, depth)
    ]
    across = [swap(block, "xl") for block in along]
    near = swap(particles, "core")
    flat = jax.ShapeDtypeStruct((NSHIFT * 16, 128), F32)
    cosine, sine, wc, ws = pl.pallas_call(
        tables_kernel,
        out_shape=(flat, flat, flat, flat),
        in_specs=[SMEM_SPEC, VMEM_SPEC],
        out_specs=(VMEM_SPEC,) * 4,
        compiler_params=params(4),
        cost_estimate=pl.CostEstimate(flops=4 * 10**9, bytes_accessed=12 * 10**6, transcendentals=0),
        name="tables",
    )(offsets, weight)
    far, wc, along[1:], across = lax.optimization_barrier((far, wc, along[1:], across))
    parts = (particles, near, far, swap(far, "core"))
    blocks = [block for pair in zip(along, across) for block in pair]

    table_rows = NSHIFT * QROT * CLASSES
    *terms, pool = pl.pallas_call(
        score_kernel,
        out_shape=[
            jax.ShapeDtypeStruct((56, NPOOL * ROWS), F32 if j == 0 else BF16) for j in range(NPOOL)
        ]
        + [jax.ShapeDtypeStruct((NPOOL * ROWS, 2 * K), BF16)],
        in_specs=[SMEM_SPEC] + [VMEM_SPEC] * NBLK + [ANY_SPEC] * 4 + [VMEM_SPEC] * 3,
        out_specs=[VMEM_SPEC] * (NPOOL + 1),
        scratch_shapes=[
            VMEM((NBLK * LOCAL * QROT * 32, 128), F32),
            VMEM((table_rows, 256 * STEP_TILES), BF16),
            VMEM((table_rows, 256 * STEP_TILES), BF16),
            VMEM((table_rows, NPOOL * ROWS), F32),
            VMEM((NPOOL, 56, NPOOL * ROWS), F32),
            VMEM((8, NPOOL * ROWS), jnp.int32),
            VMEM((NPOOL, 8, ROWS), BF16),
            pltpu.SemaphoreType.DMA((2, NPOOL)),
        ],
        compiler_params=params(20),
        name="score",
    )(
        place, *blocks, *parts,
        wc, ws, weight,
    )
    terms = trade(terms, POOL)

    sums, log_evidence = pl.pallas_call(
        class_kernel,
        out_shape=(
            jax.ShapeDtypeStruct((NBLK, 16, COLS), BF16),
            jax.ShapeDtypeStruct((1, ROWS), F32),
        ),
        in_specs=[SMEM_SPEC] + [VMEM_SPEC] * 7,
        out_specs=(VMEM_SPEC, VMEM_SPEC),
        scratch_shapes=[
            VMEM((NSHIFT * 16, NPOOL * ROWS), F32),
            VMEM((1, NPOOL * ROWS), F32),
        ],
        compiler_params=params(16),
        name="classes",
    )(q, *terms, pool, cosine, sine)
    sums = lax.all_to_all(sums, BLK, 0, 0, tiled=True)

    class_ids = jnp.arange(CLASSES, dtype=jnp.int32)
    shared_owner = class_owner[:, None] == class_owner[None, :]
    earlier = class_ids[:, None] < class_ids[None, :]
    position = jnp.sum((shared_owner & earlier).astype(jnp.int32), axis=0)
    target = class_owner * SLOTS + position
    mine = lax.dynamic_slice(target, (pool_index * QCLS,), (QCLS,))
    mine = jnp.pad(mine, (0, 128 - QCLS), constant_values=-1).reshape(1, 128)
    placed = pl.pallas_call(
        place_kernel,
        out_shape=pltpu.HBM((NDOM, SLOTS, COLS + 128), BF16),
        in_specs=[VMEM_SPEC, VMEM_SPEC],
        out_specs=pl.BlockSpec(memory_space=pltpu.HBM),
        scratch_shapes=[VMEM((NDOM, SLOTS, COLS + 128), BF16), pltpu.SemaphoreType.DMA],
        compiler_params=params(4),
        name="place",
    )(mine, sums)
    placed = lax.all_to_all(placed, DOM, 0, 0, tiled=True)
    means, mass = pl.pallas_call(
        mean_kernel,
        out_shape=(
            jax.ShapeDtypeStruct((SLOTS, COLS), F32),
            jax.ShapeDtypeStruct((SLOTS,), F32),
        ),
        in_specs=[VMEM_SPEC],
        out_specs=(VMEM_SPEC, VMEM_SPEC),
        compiler_params=params(4),
        name="means",
    )(placed)
    return (means, mass, log_evidence.reshape(ROWS))


def solution(mesh):
    fine = Mesh(
        np.asarray(mesh.devices).reshape([size for _, size in FINE]), [name for name, _ in FINE]
    )
    every = DOM + BLK
    return jax.shard_map(
        on_device,
        mesh=fine,
        in_specs=(P(every, None), P(BLK, None, None), P(), P(), P(every, None), P()),
        out_specs=(P(DOM, BLK), P(DOM), P(every)),
        check_vma=False,
    )
```

```python
import math

import jax
import jax.numpy as jnp
import numpy as np
from jax import lax
from jax.experimental import pallas as pl
from jax.experimental.pallas import tpu as pltpu
from jax.sharding import Mesh, PartitionSpec as P

KROW = 64
KCOL = 32
BOX = 256
SLOTS = 8
INV_TEMP = 4.0
FLOOR = -1e30

FINE = (("xh", 2), ("yh", 2), ("yl", 2), ("core", 2), ("z", 8), ("xl", 2))
DOM = ("xh", "yh", "yl", "core")
BLK = ("z", "xl")
POOL = ("yl", "core")

K = 2048
CLASSES = 48
ROT = 12
NSHIFT = 4
ROWS = 128
EXTENDED = ROWS + 8
NPOOL = 4
QROT = ROT // NPOOL
QCLS = CLASSES // NPOOL
NBLK = 16
NDOM = 16
LOCAL = 3
DEPTH = 8
BLOCK = LOCAL * QROT * 32
COLS = 256
STEP_TILES = 2
F32 = jnp.float32
BF16 = jnp.bfloat16
VMEM = pltpu.VMEM
SMEM_SPEC = pl.BlockSpec(memory_space=pltpu.SMEM)
VMEM_SPEC = pl.BlockSpec(memory_space=pltpu.VMEM)
ANY_SPEC = pl.BlockSpec(memory_space=pl.ANY)
HBM_SPEC = pl.BlockSpec(memory_space=pltpu.HBM)


def params(mib):
    return pltpu.CompilerParams(vmem_limit_bytes=mib << 20)


def pack_kernel(q_ref, cand_ref, refs_ref, particles_hbm, out_ref, extended_ref, wide, rows, sem):
    copy = pltpu.make_async_copy(particles_hbm, extended_ref.at[pl.ds(0, ROWS), :], sem)
    copy.start()
    extended_ref[ROWS:EXTENDED, 0:128] = cand_ref[...].astype(F32).astype(BF16)
    extended_ref[ROWS:EXTENDED, 128:] = jnp.zeros((8, 2 * K - 128), BF16)
    q = q_ref[0]
    wide[...] = refs_ref[...].astype(F32)
    for c in range(LOCAL):
        for r in range(QROT):
            row = wide[c, pl.ds(QROT * q + r, 1), :]
            for a in range(32):
                at = (c * QROT + r) * 32 + a
                rows[at : at + 1, :] = row[:, a * 128 : (a + 1) * 128]
    out_ref[...] = rows[...].astype(BF16)
    copy.wait()


def tables_kernel(off_ref, w_ref, cos_ref, sin_ref, wc_ref, ws_ref):
    row = lax.broadcasted_iota(jnp.int32, (16, 128), 0)
    lane = lax.broadcasted_iota(jnp.int32, (16, 128), 1)
    column = lane % KCOL
    rowpos = row * (128 // KCOL) + lane // KCOL - KROW // 2
    weight = w_ref[...]
    for s in range(NSHIFT):
        turns = (off_ref[s, 0] * column + off_ref[s, 1] * rowpos).astype(F32)
        angle = turns * (2.0 * math.pi / BOX)
        cosine, sine = jnp.cos(angle), jnp.sin(angle)
        at = slice(s * 16, (s + 1) * 16)
        cos_ref[at, :] = cosine
        sin_ref[at, :] = sine
        wc_ref[at, :] = weight * cosine
        ws_ref[at, :] = weight * sine


def pool_copies(q, parts, pool, listed, sem):
    copies = []
    for j, part in enumerate(parts):
        rows = pl.ds(pl.multiple_of((q ^ j) * ROWS, ROWS), ROWS)
        copies.append(pltpu.make_async_copy(part.at[pl.ds(0, ROWS), :], pool.at[rows, :], sem.at[0, j]))
        few = part.at[pl.ds(ROWS, 8), pl.ds(0, ROWS)]
        copies.append(pltpu.make_async_copy(few, listed.at[j], sem.at[1, j]))
    return copies


def split(x):
    high = x.astype(BF16).astype(F32)
    middle = (x - high).astype(BF16).astype(F32)
    return (high, middle, x - high - middle)


def score_kernel(
    index_ref, *refs
):
    blocks = refs[:DEPTH]
    p0, p1, p2, p3, wc_ref, ws_ref, w_ref = refs[DEPTH : DEPTH + 7]
    own_ref, near_ref, far_ref, cross_ref, pool = refs[DEPTH + 7 : DEPTH + 12]
    stage, wide, table0, table1, scores, groups, cands, listed, sem, block_sem = refs[DEPTH + 12 :]
    q, z, xl = index_ref[0], index_ref[1], index_ref[2]
    block_copies = []
    for k, block in enumerate(blocks):
        for side in range(2):
            source = ((z + DEPTH - k) % DEPTH) * 2 + (xl ^ side)
            rows = pl.ds(pl.multiple_of(source * BLOCK, BLOCK), BLOCK)
            block_copies.append(
                pltpu.make_async_copy(block.at[side], stage.at[rows, :], block_sem.at[k, side])
            )
    for copy in block_copies:
        copy.start()
    steps = 16 // STEP_TILES
    wide_cols = 128 * STEP_TILES
    copies = pool_copies(q, (p0, p1, p2, p3), pool, listed, sem)
    for copy in copies:
        copy.start()
    for copy in block_copies:
        copy.wait()
    wide[...] = stage[...].astype(F32)
    energy = [jnp.zeros((CLASSES, 128), F32) for _ in range(QROT)]
    stride = QROT * 32
    tables = (table0, table1)

    def build(step):
        table = tables[step % 2]
        for t in range(STEP_TILES):
            a = step * STEP_TILES + t
            weight = w_ref[a : a + 1, :]
            for r in range(QROT):
                real = wide[pl.ds(r * 32 + a, CLASSES, stride=stride), :]
                imag = wide[pl.ds(r * 32 + 16 + a, CLASSES, stride=stride), :]
                energy[r] = energy[r] + weight * (real * real + imag * imag)
                for s in range(NSHIFT):
                    wc = wc_ref[s * 16 + a : s * 16 + a + 1, :]
                    ws = ws_ref[s * 16 + a : s * 16 + a + 1, :]
                    row = (s * QROT + r) * CLASSES
                    at = slice(t * 128, (t + 1) * 128)
                    at_im = slice(wide_cols + t * 128, wide_cols + (t + 1) * 128)
                    table[row : row + CLASSES, at] = (wc * real - ws * imag).astype(BF16)
                    table[row : row + CLASSES, at_im] = (ws * real + wc * imag).astype(BF16)

    build(0)
    for copy in copies:
        copy.wait()
    for j in range(NPOOL):
        cand = listed[j].astype(F32).astype(jnp.int32)
        cands[:, pl.ds(pl.multiple_of((q ^ j) * ROWS, ROWS), ROWS)] = cand
    for step in range(steps):
        if step + 1 < steps:
            build(step + 1)
        table = tables[step % 2]
        cols = slice(step * wide_cols, (step + 1) * wide_cols)
        cols_im = slice(K + step * wide_cols, K + (step + 1) * wide_cols)
        for n in range(2):
            lanes = slice(n * 256, (n + 1) * 256)
            part = lax.dot_general(
                table[:, 0:wide_cols], pool[lanes, cols], (((1,), (1,)), ((), ())),
                preferred_element_type=F32,
            ) + lax.dot_general(
                table[:, wide_cols:], pool[lanes, cols_im], (((1,), (1,)), ((), ())),
                preferred_element_type=F32,
            )
            if step == 0:
                scores[:, lanes] = part
            else:
                scores[:, lanes] += part

    half_energy = [0.5 * jnp.sum(e, axis=1, keepdims=True) for e in energy]
    class_id = lax.broadcasted_iota(jnp.int32, (CLASSES, 256), 0)
    for n in range(2):
        lanes = slice(n * 256, (n + 1) * 256)
        cand = cands[:, lanes]
        allowed = class_id == cand[0:1, :]
        for k in range(1, 8):
            allowed = allowed | (class_id == cand[k : k + 1, :])
        loglik = []
        for s in range(NSHIFT):
            for r in range(QROT):
                row = (s * QROT + r) * CLASSES
                value = INV_TEMP * (scores[row : row + CLASSES, lanes] - half_energy[r])
                loglik.append(jnp.where(allowed, value, FLOOR))
        top = loglik[0]
        for value in loglik[1:]:
            top = jnp.maximum(top, value)
        peak = jnp.max(top, axis=0, keepdims=True)
        evidence = jnp.zeros((1, 256), F32)
        for s in range(NSHIFT):
            terms = jnp.zeros((CLASSES, 256), F32)
            for r in range(QROT):
                value = loglik[s * QROT + r]
                terms = terms + jnp.where(allowed, jnp.exp(value - peak), 0.0)
            evidence = evidence + jnp.sum(terms, axis=0, keepdims=True)
            for d in range(NPOOL):
                groups[d, s * QCLS : (s + 1) * QCLS, lanes] = terms[d * QCLS : (d + 1) * QCLS]
        pieces = split(peak) + split(evidence)
        for d in range(NPOOL):
            for i, piece in enumerate(pieces):
                groups[d, 48 + i : 49 + i, lanes] = piece
            groups[d, 54:56, lanes] = jnp.zeros((2, 256), F32)
    own_ref[...] = groups[q]
    for j, ref in enumerate((near_ref, far_ref, cross_ref)):
        ref[...] = groups[q ^ (j + 1)].astype(BF16)


def class_kernel(
    q_ref, x0, x1, x2, x3, pool, cos_ref, sin_ref, out_ref, log_ref, slots, line
):
    q = q_ref[0]
    parts = [x[...].astype(F32) for x in (x0, x1, x2, x3)]
    peaks = [x[48:49] + x[49:50] + x[50:51] for x in parts]
    peak = peaks[0]
    for value in peaks[1:]:
        peak = jnp.maximum(peak, value)
    evidence = jnp.zeros_like(peak)
    terms = jnp.zeros((NSHIFT * QCLS, NPOOL * ROWS), F32)
    for x, value in zip(parts, peaks):
        scale = jnp.exp(value - peak)
        evidence = evidence + scale * (x[51:52] + x[52:53] + x[53:54])
        terms = terms + scale * x[0:48]
    line[...] = peak + jnp.log(evidence)
    log_ref[...] = line[:, pl.ds(pl.multiple_of(q * ROWS, ROWS), ROWS)]
    probs = terms / evidence
    for s in range(NSHIFT):
        slots[s * 16 : s * 16 + QCLS, :] = probs[s * QCLS : (s + 1) * QCLS]
        slots[s * 16 + QCLS : (s + 1) * 16, :] = jnp.zeros((4, NPOOL * ROWS), F32)
    padded = slots[...]
    mass = jnp.sum(padded, axis=1, keepdims=True)
    mass = mass[0:16] + mass[16:32] + mass[32:48] + mass[48:64]
    low = padded.astype(BF16)
    row_id = lax.broadcasted_iota(jnp.int32, (16, COLS), 0)
    lane_id = lax.broadcasted_iota(jnp.int32, (16, COLS), 1)
    mass_row = jnp.sum(jnp.where(row_id == lane_id, mass, 0.0), axis=0, keepdims=True)
    mass_high = mass_row.astype(BF16).astype(F32)
    mass_low = mass_row - mass_high
    for b in range(NBLK // 2):
        cols = slice(b * COLS, (b + 1) * COLS)
        cols_im = slice(K + b * COLS, K + (b + 1) * COLS)
        g_re = jnp.dot(low, pool[:, cols], preferred_element_type=F32)
        g_im = jnp.dot(low, pool[:, cols_im], preferred_element_type=F32)
        sum_re = jnp.zeros((16, COLS), F32)
        sum_im = jnp.zeros((16, COLS), F32)
        for s in range(NSHIFT):
            at = s * 16 + 2 * b
            c = jnp.concatenate([cos_ref[at : at + 1, :], cos_ref[at + 1 : at + 2, :]], axis=1)
            z = jnp.concatenate([sin_ref[at : at + 1, :], sin_ref[at + 1 : at + 2, :]], axis=1)
            re = g_re[s * 16 : (s + 1) * 16]
            im = g_im[s * 16 : (s + 1) * 16]
            sum_re = sum_re + (c * re + z * im)
            sum_im = sum_im + (c * im - z * re)
        for dest, value in ((b, sum_re), (NBLK // 2 + b, sum_im)):
            value = jnp.where(row_id == QCLS, mass_high, value)
            value = jnp.where(row_id == QCLS + 1, mass_low, value)
            out_ref[dest] = value.astype(BF16)


def place_kernel(target_ref, y_ref, out_hbm, out_ref, sem):
    total = y_ref[0].astype(F32)
    for b in range(1, NBLK):
        total = total + y_ref[b].astype(F32)
    mass = total[QCLS : QCLS + 1, 0:128] + total[QCLS + 1 : QCLS + 2, 0:128]
    row = lax.broadcasted_iota(jnp.int32, (NDOM * SLOTS, 128), 0)
    hit = target_ref[...] == row
    pick = jnp.where(hit, 1.0, 0.0).astype(BF16)
    placed = jnp.dot(pick[:, 0:16], total.astype(BF16), preferred_element_type=F32)
    placed_mass = jnp.sum(jnp.where(hit, mass, 0.0), axis=1, keepdims=True)
    high = placed_mass.astype(BF16).astype(F32)
    lane = lax.broadcasted_iota(jnp.int32, (NDOM * SLOTS, 128), 1)
    extra = jnp.where(lane == 0, high, jnp.where(lane == 1, placed_mass - high, 0.0))
    out_ref[:, :, 0:COLS] = placed.reshape(NDOM, SLOTS, COLS).astype(BF16)
    out_ref[:, :, COLS:] = extra.reshape(NDOM, SLOTS, 128).astype(BF16)
    send = pltpu.make_async_copy(out_ref, out_hbm, sem)
    send.start()
    send.wait()


def mean_kernel(z_ref, mean_ref, mass_ref):
    total = z_ref[0].astype(F32)
    for d in range(1, NDOM):
        total = total + z_ref[d].astype(F32)
    mass = total[:, COLS : COLS + 1] + total[:, COLS + 1 : COLS + 2]
    mean_ref[...] = total[:, 0:COLS] / (mass + 1.0)
    row = lax.broadcasted_iota(jnp.int32, (SLOTS, 128), 0)
    lane = lax.broadcasted_iota(jnp.int32, (SLOTS, 128), 1)
    mass_ref[...] = jnp.sum(jnp.where(row == lane, mass, 0.0), axis=0)[0:SLOTS]


def in_hbm(x):
    return pltpu.with_memory_space_constraint(x, pltpu.HBM)


def swap(x, axis):
    return lax.ppermute(x, axis, [(0, 1), (1, 0)])


def turn(x, step):
    return lax.ppermute(x, "z", [(i, (i + step) % DEPTH) for i in range(DEPTH)])


def trade(parts, axes):
    own, near, far, cross = parts
    return (
        own,
        swap(near, axes[1]),
        swap(far, axes[0]),
        lax.ppermute(cross, axes, [(i, 3 - i) for i in range(4)]),
    )


def on_device(particles, references, noise_weight, offsets, candidates, class_owner):
    pool_index = (lax.axis_index("yl") * 2 + lax.axis_index("core")).astype(jnp.int32)
    q = pool_index.reshape(1)

    zi, xi = lax.axis_index("z").astype(jnp.int32), lax.axis_index("xl").astype(jnp.int32)
    place = jnp.stack([pool_index, zi, xi])
    weight = noise_weight.reshape(16, 128)
    packed, particles = pl.pallas_call(
        pack_kernel,
        out_shape=(
            jax.ShapeDtypeStruct((BLOCK, 128), BF16),
            jax.ShapeDtypeStruct((EXTENDED, 2 * K), BF16),
        ),
        in_specs=[SMEM_SPEC, VMEM_SPEC, VMEM_SPEC, HBM_SPEC],
        out_specs=(VMEM_SPEC, VMEM_SPEC),
        scratch_shapes=[
            VMEM((LOCAL, ROT, 2 * K), F32),
            VMEM((BLOCK, 128), F32),
            pltpu.SemaphoreType.DMA,
        ],
        compiler_params=params(8),
        name="pack",
    )(q, candidates.T, references, in_hbm(particles))
    far = swap(particles, "yl")
    ring = [None] * DEPTH
    ring[0] = up = down = jnp.stack([packed, swap(packed, "xl")])
    for k in range(1, DEPTH // 2):
        ring[k] = up = turn(up, 1)
        ring[DEPTH - k] = down = turn(down, -1)
    ring[DEPTH // 2] = turn(up, 1)
    near = swap(particles, "core")
    flat = jax.ShapeDtypeStruct((NSHIFT * 16, 128), F32)
    cosine, sine, wc, ws = pl.pallas_call(
        tables_kernel,
        out_shape=(flat, flat, flat, flat),
        in_specs=[SMEM_SPEC, VMEM_SPEC],
        out_specs=(VMEM_SPEC,) * 4,
        compiler_params=params(4),
        cost_estimate=pl.CostEstimate(flops=1 * 10**9, bytes_accessed=3 * 10**6, transcendentals=0),
        name="tables",
    )(offsets, weight)
    far, wc, ring = lax.optimization_barrier((far, wc, ring))
    parts = (particles, near, far, swap(far, "core"))
    table_rows = NSHIFT * QROT * CLASSES
    *terms, pool = pl.pallas_call(
        score_kernel,
        out_shape=[
            jax.ShapeDtypeStruct((56, NPOOL * ROWS), F32 if j == 0 else BF16) for j in range(NPOOL)
        ]
        + [jax.ShapeDtypeStruct((NPOOL * ROWS, 2 * K), BF16)],
        in_specs=[SMEM_SPEC] + [HBM_SPEC] * DEPTH + [ANY_SPEC] * 4 + [VMEM_SPEC] * 3,
        out_specs=[VMEM_SPEC] * (NPOOL + 1),
        scratch_shapes=[
            VMEM((NBLK * BLOCK, 128), BF16),
            VMEM((NBLK * BLOCK, 128), F32),
            VMEM((table_rows, 256 * STEP_TILES), BF16),
            VMEM((table_rows, 256 * STEP_TILES), BF16),
            VMEM((table_rows, NPOOL * ROWS), F32),
            VMEM((NPOOL, 56, NPOOL * ROWS), F32),
            VMEM((8, NPOOL * ROWS), jnp.int32),
            VMEM((NPOOL, 8, ROWS), BF16),
            pltpu.SemaphoreType.DMA((2, NPOOL)),
            pltpu.SemaphoreType.DMA((DEPTH, 2)),
        ],
        compiler_params=params(20),
        name="score",
    )(
        place, *[in_hbm(x) for x in ring], *parts,
        wc, ws, weight,
    )
    terms = trade(terms, POOL)

    sums, log_evidence = pl.pallas_call(
        class_kernel,
        out_shape=(
            jax.ShapeDtypeStruct((NBLK, 16, COLS), BF16),
            jax.ShapeDtypeStruct((1, ROWS), F32),
        ),
        in_specs=[SMEM_SPEC] + [VMEM_SPEC] * 7,
        out_specs=(VMEM_SPEC, VMEM_SPEC),
        scratch_shapes=[
            VMEM((NSHIFT * 16, NPOOL * ROWS), F32),
            VMEM((1, NPOOL * ROWS), F32),
        ],
        compiler_params=params(16),
        name="classes",
    )(q, *terms, pool, cosine, sine)
    sums = lax.all_to_all(sums, BLK, 0, 0, tiled=True)

    class_ids = jnp.arange(CLASSES, dtype=jnp.int32)
    shared_owner = class_owner[:, None] == class_owner[None, :]
    earlier = class_ids[:, None] < class_ids[None, :]
    position = jnp.sum((shared_owner & earlier).astype(jnp.int32), axis=0)
    target = class_owner * SLOTS + position
    mine = lax.dynamic_slice(target, (pool_index * QCLS,), (QCLS,))
    mine = jnp.pad(mine, (0, 128 - QCLS), constant_values=-1).reshape(1, 128)
    placed = pl.pallas_call(
        place_kernel,
        out_shape=pltpu.HBM((NDOM, SLOTS, COLS + 128), BF16),
        in_specs=[VMEM_SPEC, VMEM_SPEC],
        out_specs=pl.BlockSpec(memory_space=pltpu.HBM),
        scratch_shapes=[VMEM((NDOM, SLOTS, COLS + 128), BF16), pltpu.SemaphoreType.DMA],
        compiler_params=params(4),
        name="place",
    )(mine, sums)
    placed = lax.all_to_all(placed, DOM, 0, 0, tiled=True)
    means, mass = pl.pallas_call(
        mean_kernel,
        out_shape=(
            jax.ShapeDtypeStruct((SLOTS, COLS), F32),
            jax.ShapeDtypeStruct((SLOTS,), F32),
        ),
        in_specs=[VMEM_SPEC],
        out_specs=(VMEM_SPEC, VMEM_SPEC),
        compiler_params=params(4),
        name="means",
    )(placed)
    return (means, mass, log_evidence.reshape(ROWS))


def solution(mesh):
    fine = Mesh(
        np.asarray(mesh.devices).reshape([size for _, size in FINE]), [name for name, _ in FINE]
    )
    every = DOM + BLK
    return jax.shard_map(
        on_device,
        mesh=fine,
        in_specs=(P(every, None), P(BLK, None, None), P(), P(), P(every, None), P()),
        out_specs=(P(DOM, BLK), P(DOM), P(every)),
        check_vma=False,
    )
```

```python
import math

import jax
import jax.numpy as jnp
import numpy as np
from jax import lax
from jax.experimental import pallas as pl
from jax.experimental.pallas import tpu as pltpu
from jax.sharding import Mesh, PartitionSpec as P

KROW = 64
KCOL = 32
BOX = 256
SLOTS = 8
INV_TEMP = 4.0
FLOOR = -1e30

FINE = (("xh", 2), ("yh", 2), ("yl", 2), ("core", 2), ("z", 8), ("xl", 2))
DOM = ("xh", "yh", "yl", "core")
BLK = ("z", "xl")
POOL = ("yl", "core")

K = 2048
CLASSES = 48
ROT = 12
NSHIFT = 4
ROWS = 128
EXTENDED = ROWS + 8
NPOOL = 4
QROT = ROT // NPOOL
QCLS = CLASSES // NPOOL
NBLK = 16
NDOM = 16
LOCAL = 3
DEPTH = 8
BLOCK = LOCAL * QROT * 32
COLS = 256
STEP_TILES = 2
F32 = jnp.float32
BF16 = jnp.bfloat16
VMEM = pltpu.VMEM
SMEM_SPEC = pl.BlockSpec(memory_space=pltpu.SMEM)
VMEM_SPEC = pl.BlockSpec(memory_space=pltpu.VMEM)
ANY_SPEC = pl.BlockSpec(memory_space=pl.ANY)
HBM_SPEC = pl.BlockSpec(memory_space=pltpu.HBM)


def params(mib):
    return pltpu.CompilerParams(vmem_limit_bytes=mib << 20)


def pack_kernel(q_ref, cand_ref, refs_ref, particles_hbm, out_ref, extended_ref, wide, rows, sem):
    copy = pltpu.make_async_copy(particles_hbm, extended_ref.at[pl.ds(0, ROWS), :], sem)
    copy.start()
    extended_ref[ROWS:EXTENDED, 0:128] = cand_ref[...].astype(F32).astype(BF16)
    extended_ref[ROWS:EXTENDED, 128:] = jnp.zeros((8, 2 * K - 128), BF16)
    q = q_ref[0]
    wide[...] = refs_ref[...].astype(F32)
    for c in range(LOCAL):
        for r in range(QROT):
            row = wide[c, pl.ds(QROT * q + r, 1), :]
            for a in range(32):
                at = (c * QROT + r) * 32 + a
                rows[at : at + 1, :] = row[:, a * 128 : (a + 1) * 128]
    out_ref[...] = rows[...].astype(BF16)
    copy.wait()


def tables_kernel(off_ref, w_ref, cos_ref, sin_ref, wc_ref, ws_ref):
    row = lax.broadcasted_iota(jnp.int32, (16, 128), 0)
    lane = lax.broadcasted_iota(jnp.int32, (16, 128), 1)
    column = lane % KCOL
    rowpos = row * (128 // KCOL) + lane // KCOL - KROW // 2
    weight = w_ref[...]
    for s in range(NSHIFT):
        turns = (off_ref[s, 0] * column + off_ref[s, 1] * rowpos).astype(F32)
        angle = turns * (2.0 * math.pi / BOX)
        cosine, sine = jnp.cos(angle), jnp.sin(angle)
        at = slice(s * 16, (s + 1) * 16)
        cos_ref[at, :] = cosine
        sin_ref[at, :] = sine
        wc_ref[at, :] = weight * cosine
        ws_ref[at, :] = weight * sine


def pool_copies(q, parts, pool, listed, sem):
    copies = []
    for j, part in enumerate(parts):
        rows = pl.ds(pl.multiple_of((q ^ j) * ROWS, ROWS), ROWS)
        copies.append(pltpu.make_async_copy(part.at[pl.ds(0, ROWS), :], pool.at[rows, :], sem.at[0, j]))
        few = part.at[pl.ds(ROWS, 8), pl.ds(0, ROWS)]
        copies.append(pltpu.make_async_copy(few, listed.at[j], sem.at[1, j]))
    return copies


def split(x):
    high = x.astype(BF16).astype(F32)
    middle = (x - high).astype(BF16).astype(F32)
    return (high, middle, x - high - middle)


def score_kernel(
    index_ref, *refs
):
    blocks = refs[:DEPTH]
    p0, p1, p2, p3, wc_ref, ws_ref, w_ref = refs[DEPTH : DEPTH + 7]
    own_ref, near_ref, far_ref, cross_ref, pool = refs[DEPTH + 7 : DEPTH + 12]
    stage, wide, table0, table1, scores, groups, cands, listed, sem, block_sem = refs[DEPTH + 12 :]
    q, z, xl = index_ref[0], index_ref[1], index_ref[2]
    block_copies = []
    for k, block in enumerate(blocks):
        for side in range(2):
            source = ((z + DEPTH - k) % DEPTH) * 2 + (xl ^ side)
            rows = pl.ds(pl.multiple_of(source * BLOCK, BLOCK), BLOCK)
            block_copies.append(
                pltpu.make_async_copy(block.at[side], stage.at[rows, :], block_sem.at[k, side])
            )
    for copy in block_copies:
        copy.start()
    steps = 16 // STEP_TILES
    wide_cols = 128 * STEP_TILES
    copies = pool_copies(q, (p0, p1, p2, p3), pool, listed, sem)
    for copy in copies:
        copy.start()
    for copy in block_copies:
        copy.wait()
    wide[...] = stage[...].astype(F32)
    energy = [jnp.zeros((CLASSES, 128), F32) for _ in range(QROT)]
    stride = QROT * 32
    tables = (table0, table1)

    def build(step):
        table = tables[step % 2]
        for t in range(STEP_TILES):
            a = step * STEP_TILES + t
            weight = w_ref[a : a + 1, :]
            for r in range(QROT):
                real = wide[pl.ds(r * 32 + a, CLASSES, stride=stride), :]
                imag = wide[pl.ds(r * 32 + 16 + a, CLASSES, stride=stride), :]
                energy[r] = energy[r] + weight * (real * real + imag * imag)
                for s in range(NSHIFT):
                    wc = wc_ref[s * 16 + a : s * 16 + a + 1, :]
                    ws = ws_ref[s * 16 + a : s * 16 + a + 1, :]
                    row = (s * QROT + r) * CLASSES
                    at = slice(t * 128, (t + 1) * 128)
                    at_im = slice(wide_cols + t * 128, wide_cols + (t + 1) * 128)
                    table[row : row + CLASSES, at] = (wc * real - ws * imag).astype(BF16)
                    table[row : row + CLASSES, at_im] = (ws * real + wc * imag).astype(BF16)

    build(0)
    for copy in copies:
        copy.wait()
    for j in range(NPOOL):
        cand = listed[j].astype(F32).astype(jnp.int32)
        cands[:, pl.ds(pl.multiple_of((q ^ j) * ROWS, ROWS), ROWS)] = cand
    for step in range(steps):
        if step + 1 < steps:
            build(step + 1)
        table = tables[step % 2]
        cols = slice(step * wide_cols, (step + 1) * wide_cols)
        cols_im = slice(K + step * wide_cols, K + (step + 1) * wide_cols)
        for n in range(2):
            lanes = slice(n * 256, (n + 1) * 256)
            part = lax.dot_general(
                table[:, 0:wide_cols], pool[lanes, cols], (((1,), (1,)), ((), ())),
                preferred_element_type=F32,
            ) + lax.dot_general(
                table[:, wide_cols:], pool[lanes, cols_im], (((1,), (1,)), ((), ())),
                preferred_element_type=F32,
            )
            if step == 0:
                scores[:, lanes] = part
            else:
                scores[:, lanes] += part

    half_energy = [0.5 * jnp.sum(e, axis=1, keepdims=True) for e in energy]
    class_id = lax.broadcasted_iota(jnp.int32, (CLASSES, 256), 0)
    for n in range(2):
        lanes = slice(n * 256, (n + 1) * 256)
        cand = cands[:, lanes]
        allowed = class_id == cand[0:1, :]
        for k in range(1, 8):
            allowed = allowed | (class_id == cand[k : k + 1, :])
        loglik = []
        for s in range(NSHIFT):
            for r in range(QROT):
                row = (s * QROT + r) * CLASSES
                value = INV_TEMP * (scores[row : row + CLASSES, lanes] - half_energy[r])
                loglik.append(jnp.where(allowed, value, FLOOR))
        top = loglik[0]
        for value in loglik[1:]:
            top = jnp.maximum(top, value)
        peak = jnp.max(top, axis=0, keepdims=True)
        evidence = jnp.zeros((1, 256), F32)
        for s in range(NSHIFT):
            terms = jnp.zeros((CLASSES, 256), F32)
            for r in range(QROT):
                value = loglik[s * QROT + r]
                terms = terms + jnp.where(allowed, jnp.exp(value - peak), 0.0)
            evidence = evidence + jnp.sum(terms, axis=0, keepdims=True)
            for d in range(NPOOL):
                groups[d, s * QCLS : (s + 1) * QCLS, lanes] = terms[d * QCLS : (d + 1) * QCLS]
        pieces = split(peak) + split(evidence)
        for d in range(NPOOL):
            for i, piece in enumerate(pieces):
                groups[d, 48 + i : 49 + i, lanes] = piece
            groups[d, 54:56, lanes] = jnp.zeros((2, 256), F32)
    own_ref[...] = groups[q]
    for j, ref in enumerate((near_ref, far_ref, cross_ref)):
        ref[...] = groups[q ^ (j + 1)].astype(BF16)


def class_kernel(
    q_ref, x0, x1, x2, x3, pool, cos_ref, sin_ref, out_ref, log_ref, slots, line
):
    q = q_ref[0]
    parts = [x[...].astype(F32) for x in (x0, x1, x2, x3)]
    peaks = [x[48:49] + x[49:50] + x[50:51] for x in parts]
    peak = peaks[0]
    for value in peaks[1:]:
        peak = jnp.maximum(peak, value)
    evidence = jnp.zeros_like(peak)
    terms = jnp.zeros((NSHIFT * QCLS, NPOOL * ROWS), F32)
    for x, value in zip(parts, peaks):
        scale = jnp.exp(value - peak)
        evidence = evidence + scale * (x[51:52] + x[52:53] + x[53:54])
        terms = terms + scale * x[0:48]
    line[...] = peak + jnp.log(evidence)
    log_ref[...] = line[:, pl.ds(pl.multiple_of(q * ROWS, ROWS), ROWS)]
    probs = terms / evidence
    for s in range(NSHIFT):
        slots[s * 16 : s * 16 + QCLS, :] = probs[s * QCLS : (s + 1) * QCLS]
        slots[s * 16 + QCLS : (s + 1) * 16, :] = jnp.zeros((4, NPOOL * ROWS), F32)
    padded = slots[...]
    mass = jnp.sum(padded, axis=1, keepdims=True)
    mass = mass[0:16] + mass[16:32] + mass[32:48] + mass[48:64]
    low = padded.astype(BF16)
    row_id = lax.broadcasted_iota(jnp.int32, (16, COLS), 0)
    lane_id = lax.broadcasted_iota(jnp.int32, (16, COLS), 1)
    mass_row = jnp.sum(jnp.where(row_id == lane_id, mass, 0.0), axis=0, keepdims=True)
    mass_high = mass_row.astype(BF16).astype(F32)
    mass_low = mass_row - mass_high
    for b in range(NBLK // 2):
        cols = slice(b * COLS, (b + 1) * COLS)
        cols_im = slice(K + b * COLS, K + (b + 1) * COLS)
        g_re = jnp.dot(low, pool[:, cols], preferred_element_type=F32)
        g_im = jnp.dot(low, pool[:, cols_im], preferred_element_type=F32)
        sum_re = jnp.zeros((16, COLS), F32)
        sum_im = jnp.zeros((16, COLS), F32)
        for s in range(NSHIFT):
            at = s * 16 + 2 * b
            c = jnp.concatenate([cos_ref[at : at + 1, :], cos_ref[at + 1 : at + 2, :]], axis=1)
            z = jnp.concatenate([sin_ref[at : at + 1, :], sin_ref[at + 1 : at + 2, :]], axis=1)
            re = g_re[s * 16 : (s + 1) * 16]
            im = g_im[s * 16 : (s + 1) * 16]
            sum_re = sum_re + (c * re + z * im)
            sum_im = sum_im + (c * im - z * re)
        for dest, value in ((b, sum_re), (NBLK // 2 + b, sum_im)):
            value = jnp.where(row_id == QCLS, mass_high, value)
            value = jnp.where(row_id == QCLS + 1, mass_low, value)
            out_ref[dest] = value.astype(BF16)


def place_kernel(target_ref, y_ref, out_hbm, out_ref, sem):
    total = y_ref[0].astype(F32)
    for b in range(1, NBLK):
        total = total + y_ref[b].astype(F32)
    mass = total[QCLS : QCLS + 1, 0:128] + total[QCLS + 1 : QCLS + 2, 0:128]
    row = lax.broadcasted_iota(jnp.int32, (NDOM * SLOTS, 128), 0)
    hit = target_ref[...] == row
    pick = jnp.where(hit, 1.0, 0.0).astype(BF16)
    placed = jnp.dot(pick[:, 0:16], total.astype(BF16), preferred_element_type=F32)
    placed_mass = jnp.sum(jnp.where(hit, mass, 0.0), axis=1, keepdims=True)
    high = placed_mass.astype(BF16).astype(F32)
    lane = lax.broadcasted_iota(jnp.int32, (NDOM * SLOTS, 128), 1)
    extra = jnp.where(lane == 0, high, jnp.where(lane == 1, placed_mass - high, 0.0))
    out_ref[:, :, 0:COLS] = placed.reshape(NDOM, SLOTS, COLS).astype(BF16)
    out_ref[:, :, COLS:] = extra.reshape(NDOM, SLOTS, 128).astype(BF16)
    send = pltpu.make_async_copy(out_ref, out_hbm, sem)
    send.start()
    send.wait()


def mean_kernel(z_ref, mean_ref, mass_ref):
    total = z_ref[0].astype(F32)
    for d in range(1, NDOM):
        total = total + z_ref[d].astype(F32)
    mass = total[:, COLS : COLS + 1] + total[:, COLS + 1 : COLS + 2]
    mean_ref[...] = total[:, 0:COLS] / (mass + 1.0)
    row = lax.broadcasted_iota(jnp.int32, (SLOTS, 128), 0)
    lane = lax.broadcasted_iota(jnp.int32, (SLOTS, 128), 1)
    mass_ref[...] = jnp.sum(jnp.where(row == lane, mass, 0.0), axis=0)[0:SLOTS]


def in_hbm(x):
    return pltpu.with_memory_space_constraint(x, pltpu.HBM)


def swap(x, axis):
    return lax.ppermute(x, axis, [(0, 1), (1, 0)])


def turn(x, step):
    return lax.ppermute(x, "z", [(i, (i + step) % DEPTH) for i in range(DEPTH)])


def trade(parts, axes):
    own, near, far, cross = parts
    return (
        own,
        swap(near, axes[1]),
        swap(far, axes[0]),
        lax.ppermute(cross, axes, [(i, 3 - i) for i in range(4)]),
    )


def on_device(particles, references, noise_weight, offsets, candidates, class_owner):
    pool_index = (lax.axis_index("yl") * 2 + lax.axis_index("core")).astype(jnp.int32)
    q = pool_index.reshape(1)

    zi, xi = lax.axis_index("z").astype(jnp.int32), lax.axis_index("xl").astype(jnp.int32)
    place = jnp.stack([pool_index, zi, xi])
    weight = noise_weight.reshape(16, 128)
    packed, particles = pl.pallas_call(
        pack_kernel,
        out_shape=(
            jax.ShapeDtypeStruct((BLOCK, 128), BF16),
            jax.ShapeDtypeStruct((EXTENDED, 2 * K), BF16),
        ),
        in_specs=[SMEM_SPEC, VMEM_SPEC, VMEM_SPEC, HBM_SPEC],
        out_specs=(VMEM_SPEC, VMEM_SPEC),
        scratch_shapes=[
            VMEM((LOCAL, ROT, 2 * K), F32),
            VMEM((BLOCK, 128), F32),
            pltpu.SemaphoreType.DMA,
        ],
        compiler_params=params(8),
        name="pack",
    )(q, in_hbm(candidates.T), in_hbm(references), in_hbm(particles))
    far = swap(particles, "yl")
    ring = [None] * DEPTH
    near, beside = lax.optimization_barrier((swap(particles, "core"), swap(packed, "xl")))
    ring[0] = up = down = jnp.stack([packed, beside])
    for k in range(1, DEPTH // 2):
        ring[k] = up = turn(up, 1)
        ring[DEPTH - k] = down = turn(down, -1)
    ring[DEPTH // 2] = turn(up, 1)
    flat = jax.ShapeDtypeStruct((NSHIFT * 16, 128), F32)
    cosine, sine, wc, ws = pl.pallas_call(
        tables_kernel,
        out_shape=(flat, flat, flat, flat),
        in_specs=[SMEM_SPEC, VMEM_SPEC],
        out_specs=(VMEM_SPEC,) * 4,
        compiler_params=params(4),
        cost_estimate=pl.CostEstimate(flops=1 * 10**9, bytes_accessed=3 * 10**6, transcendentals=0),
        name="tables",
    )(offsets, weight)
    last = DEPTH // 2
    far, wc, ring[last - 1], ring[last + 1] = lax.optimization_barrier(
        (far, wc, ring[last - 1], ring[last + 1])
    )
    parts = (particles, near, far, swap(far, "core"))
    table_rows = NSHIFT * QROT * CLASSES
    *terms, pool = pl.pallas_call(
        score_kernel,
        out_shape=[
            jax.ShapeDtypeStruct((56, NPOOL * ROWS), F32 if j == 0 else BF16) for j in range(NPOOL)
        ]
        + [jax.ShapeDtypeStruct((NPOOL * ROWS, 2 * K), BF16)],
        in_specs=[SMEM_SPEC] + [HBM_SPEC] * DEPTH + [ANY_SPEC] * 4 + [VMEM_SPEC] * 3,
        out_specs=[VMEM_SPEC] * (NPOOL + 1),
        scratch_shapes=[
            VMEM((NBLK * BLOCK, 128), BF16),
            VMEM((NBLK * BLOCK, 128), F32),
            VMEM((table_rows, 256 * STEP_TILES), BF16),
            VMEM((table_rows, 256 * STEP_TILES), BF16),
            VMEM((table_rows, NPOOL * ROWS), F32),
            VMEM((NPOOL, 56, NPOOL * ROWS), F32),
            VMEM((8, NPOOL * ROWS), jnp.int32),
            VMEM((NPOOL, 8, ROWS), BF16),
            pltpu.SemaphoreType.DMA((2, NPOOL)),
            pltpu.SemaphoreType.DMA((DEPTH, 2)),
        ],
        compiler_params=params(20),
        name="score",
    )(
        place, *[in_hbm(x) for x in ring], *parts,
        wc, ws, weight,
    )
    terms = trade(terms, POOL)

    sums, log_evidence = pl.pallas_call(
        class_kernel,
        out_shape=(
            jax.ShapeDtypeStruct((NBLK, 16, COLS), BF16),
            jax.ShapeDtypeStruct((1, ROWS), F32),
        ),
        in_specs=[SMEM_SPEC] + [VMEM_SPEC] * 7,
        out_specs=(VMEM_SPEC, VMEM_SPEC),
        scratch_shapes=[
            VMEM((NSHIFT * 16, NPOOL * ROWS), F32),
            VMEM((1, NPOOL * ROWS), F32),
        ],
        compiler_params=params(16),
        name="classes",
    )(q, *terms, pool, cosine, sine)
    sums = lax.all_to_all(sums, BLK, 0, 0, tiled=True)

    class_ids = jnp.arange(CLASSES, dtype=jnp.int32)
    shared_owner = class_owner[:, None] == class_owner[None, :]
    earlier = class_ids[:, None] < class_ids[None, :]
    position = jnp.sum((shared_owner & earlier).astype(jnp.int32), axis=0)
    target = class_owner * SLOTS + position
    mine = lax.dynamic_slice(target, (pool_index * QCLS,), (QCLS,))
    mine = jnp.pad(mine, (0, 128 - QCLS), constant_values=-1).reshape(1, 128)
    placed = pl.pallas_call(
        place_kernel,
        out_shape=pltpu.HBM((NDOM, SLOTS, COLS + 128), BF16),
        in_specs=[VMEM_SPEC, VMEM_SPEC],
        out_specs=pl.BlockSpec(memory_space=pltpu.HBM),
        scratch_shapes=[VMEM((NDOM, SLOTS, COLS + 128), BF16), pltpu.SemaphoreType.DMA],
        compiler_params=params(4),
        name="place",
    )(mine, sums)
    placed = lax.all_to_all(placed, DOM, 0, 0, tiled=True)
    means, mass = pl.pallas_call(
        mean_kernel,
        out_shape=(
            jax.ShapeDtypeStruct((SLOTS, COLS), F32),
            jax.ShapeDtypeStruct((SLOTS,), F32),
        ),
        in_specs=[VMEM_SPEC],
        out_specs=(VMEM_SPEC, VMEM_SPEC),
        compiler_params=params(4),
        name="means",
    )(placed)
    return (means, mass, log_evidence.reshape(ROWS))


def solution(mesh):
    fine = Mesh(
        np.asarray(mesh.devices).reshape([size for _, size in FINE]), [name for name, _ in FINE]
    )
    every = DOM + BLK
    return jax.shard_map(
        on_device,
        mesh=fine,
        in_specs=(P(every, None), P(BLK, None, None), P(), P(), P(every, None), P()),
        out_specs=(P(DOM, BLK), P(DOM), P(every)),
        check_vma=False,
    )
```

```python
import math

import jax
import jax.numpy as jnp
import numpy as np
from jax import lax
from jax.experimental import pallas as pl
from jax.experimental.pallas import tpu as pltpu
from jax.sharding import Mesh, PartitionSpec as P

KROW = 64
KCOL = 32
BOX = 256
SLOTS = 8
INV_TEMP = 4.0
FLOOR = -1e30

FINE = (("xh", 2), ("yh", 2), ("yl", 2), ("core", 2), ("z", 8), ("xl", 2))
DOM = ("xh", "yh", "yl", "core")
BLK = ("z", "xl")
POOL = ("yl", "core")

K = 2048
CLASSES = 48
ROT = 12
NSHIFT = 4
ROWS = 128
EXTENDED = ROWS + 8
NPOOL = 4
QROT = ROT // NPOOL
QCLS = CLASSES // NPOOL
NBLK = 16
NDOM = 16
LOCAL = 3
DEPTH = 8
BLOCK = LOCAL * QROT * 32
COLS = 256
STEP_TILES = 2
F32 = jnp.float32
BF16 = jnp.bfloat16
VMEM = pltpu.VMEM
SMEM_SPEC = pl.BlockSpec(memory_space=pltpu.SMEM)
VMEM_SPEC = pl.BlockSpec(memory_space=pltpu.VMEM)
ANY_SPEC = pl.BlockSpec(memory_space=pl.ANY)
HBM_SPEC = pl.BlockSpec(memory_space=pltpu.HBM)


def params(mib):
    return pltpu.CompilerParams(vmem_limit_bytes=mib << 20)


def pack_kernel(q_ref, cand_ref, refs_ref, particles_hbm, out_ref, extended_ref, wide, rows, sem):
    copy = pltpu.make_async_copy(particles_hbm, extended_ref.at[pl.ds(0, ROWS), :], sem)
    copy.start()
    extended_ref[ROWS:EXTENDED, 0:128] = cand_ref[...].astype(F32).astype(BF16)
    extended_ref[ROWS:EXTENDED, 128:] = jnp.zeros((8, 2 * K - 128), BF16)
    q = q_ref[0]
    wide[...] = refs_ref[...].astype(F32)
    for c in range(LOCAL):
        for r in range(QROT):
            row = wide[c, pl.ds(QROT * q + r, 1), :]
            for a in range(32):
                at = (c * QROT + r) * 32 + a
                rows[at : at + 1, :] = row[:, a * 128 : (a + 1) * 128]
    out_ref[...] = rows[...].astype(BF16)
    copy.wait()


def tables_kernel(off_ref, w_ref, cos_ref, sin_ref, wc_ref, ws_ref):
    row = lax.broadcasted_iota(jnp.int32, (16, 128), 0)
    lane = lax.broadcasted_iota(jnp.int32, (16, 128), 1)
    column = lane % KCOL
    rowpos = row * (128 // KCOL) + lane // KCOL - KROW // 2
    weight = w_ref[...]
    for s in range(NSHIFT):
        turns = (off_ref[s, 0] * column + off_ref[s, 1] * rowpos).astype(F32)
        angle = turns * (2.0 * math.pi / BOX)
        cosine, sine = jnp.cos(angle), jnp.sin(angle)
        at = slice(s * 16, (s + 1) * 16)
        cos_ref[at, :] = cosine
        sin_ref[at, :] = sine
        wc_ref[at, :] = weight * cosine
        ws_ref[at, :] = weight * sine


def pool_copies(q, parts, pool, listed, sem):
    copies = []
    for j, part in enumerate(parts):
        rows = pl.ds(pl.multiple_of((q ^ j) * ROWS, ROWS), ROWS)
        copies.append(pltpu.make_async_copy(part.at[pl.ds(0, ROWS), :], pool.at[rows, :], sem.at[0, j]))
        few = part.at[pl.ds(ROWS, 8), pl.ds(0, ROWS)]
        copies.append(pltpu.make_async_copy(few, listed.at[j], sem.at[1, j]))
    return copies


def split(x):
    high = x.astype(BF16).astype(F32)
    middle = (x - high).astype(BF16).astype(F32)
    return (high, middle, x - high - middle)


def score_kernel(
    index_ref, *refs
):
    blocks = refs[:DEPTH]
    p0, p1, p2, p3, wc_ref, ws_ref, w_ref = refs[DEPTH : DEPTH + 7]
    own_ref, near_ref, far_ref, cross_ref, pool = refs[DEPTH + 7 : DEPTH + 12]
    stage, wide, table0, table1, scores, groups, cands, listed, sem, block_sem = refs[DEPTH + 12 :]
    q, z, xl = index_ref[0], index_ref[1], index_ref[2]
    block_copies = []
    for k, block in enumerate(blocks):
        block_copies.append(pltpu.make_async_copy(block, stage.at[k], block_sem.at[k]))
    for copy in block_copies:
        copy.start()
    steps = 16 // STEP_TILES
    wide_cols = 128 * STEP_TILES
    copies = pool_copies(q, (p0, p1, p2, p3), pool, listed, sem)
    for copy in copies:
        copy.start()
    for k, copy in enumerate(block_copies):
        copy.wait()
        for side in range(2):
            source = ((z + DEPTH - k) % DEPTH) * 2 + (xl ^ side)
            rows = pl.ds(pl.multiple_of(source * BLOCK, BLOCK), BLOCK)
            wide[rows, :] = stage[k, side].astype(F32)
    energy = [jnp.zeros((CLASSES, 128), F32) for _ in range(QROT)]
    stride = QROT * 32
    tables = (table0, table1)

    def build(step):
        table = tables[step % 2]
        for t in range(STEP_TILES):
            a = step * STEP_TILES + t
            weight = w_ref[a : a + 1, :]
            for r in range(QROT):
                real = wide[pl.ds(r * 32 + a, CLASSES, stride=stride), :]
                imag = wide[pl.ds(r * 32 + 16 + a, CLASSES, stride=stride), :]
                energy[r] = energy[r] + weight * (real * real + imag * imag)
                for s in range(NSHIFT):
                    wc = wc_ref[s * 16 + a : s * 16 + a + 1, :]
                    ws = ws_ref[s * 16 + a : s * 16 + a + 1, :]
                    row = (s * QROT + r) * CLASSES
                    at = slice(t * 128, (t + 1) * 128)
                    at_im = slice(wide_cols + t * 128, wide_cols + (t + 1) * 128)
                    table[row : row + CLASSES, at] = (wc * real - ws * imag).astype(BF16)
                    table[row : row + CLASSES, at_im] = (ws * real + wc * imag).astype(BF16)

    build(0)
    for copy in copies:
        copy.wait()
    for j in range(NPOOL):
        cand = listed[j].astype(F32).astype(jnp.int32)
        cands[:, pl.ds(pl.multiple_of((q ^ j) * ROWS, ROWS), ROWS)] = cand
    for step in range(steps):
        if step + 1 < steps:
            build(step + 1)
        table = tables[step % 2]
        cols = slice(step * wide_cols, (step + 1) * wide_cols)
        cols_im = slice(K + step * wide_cols, K + (step + 1) * wide_cols)
        for n in range(2):
            lanes = slice(n * 256, (n + 1) * 256)
            part = lax.dot_general(
                table[:, 0:wide_cols], pool[lanes, cols], (((1,), (1,)), ((), ())),
                preferred_element_type=F32,
            ) + lax.dot_general(
                table[:, wide_cols:], pool[lanes, cols_im], (((1,), (1,)), ((), ())),
                preferred_element_type=F32,
            )
            if step == 0:
                scores[:, lanes] = part
            else:
                scores[:, lanes] += part

    half_energy = [0.5 * jnp.sum(e, axis=1, keepdims=True) for e in energy]
    class_id = lax.broadcasted_iota(jnp.int32, (CLASSES, 256), 0)
    for n in range(2):
        lanes = slice(n * 256, (n + 1) * 256)
        cand = cands[:, lanes]
        allowed = class_id == cand[0:1, :]
        for k in range(1, 8):
            allowed = allowed | (class_id == cand[k : k + 1, :])
        loglik = []
        for s in range(NSHIFT):
            for r in range(QROT):
                row = (s * QROT + r) * CLASSES
                value = INV_TEMP * (scores[row : row + CLASSES, lanes] - half_energy[r])
                loglik.append(jnp.where(allowed, value, FLOOR))
        top = loglik[0]
        for value in loglik[1:]:
            top = jnp.maximum(top, value)
        peak = jnp.max(top, axis=0, keepdims=True)
        evidence = jnp.zeros((1, 256), F32)
        for s in range(NSHIFT):
            terms = jnp.zeros((CLASSES, 256), F32)
            for r in range(QROT):
                value = loglik[s * QROT + r]
                terms = terms + jnp.where(allowed, jnp.exp(value - peak), 0.0)
            evidence = evidence + jnp.sum(terms, axis=0, keepdims=True)
            for d in range(NPOOL):
                groups[d, s * QCLS : (s + 1) * QCLS, lanes] = terms[d * QCLS : (d + 1) * QCLS]
        pieces = split(peak) + split(evidence)
        for d in range(NPOOL):
            for i, piece in enumerate(pieces):
                groups[d, 48 + i : 49 + i, lanes] = piece
            groups[d, 54:56, lanes] = jnp.zeros((2, 256), F32)
    own_ref[...] = groups[q]
    for j, ref in enumerate((near_ref, far_ref, cross_ref)):
        ref[...] = groups[q ^ (j + 1)].astype(BF16)


def class_kernel(
    q_ref, x0, x1, x2, x3, pool, cos_ref, sin_ref, out_ref, log_ref, slots, line
):
    q = q_ref[0]
    parts = [x[...].astype(F32) for x in (x0, x1, x2, x3)]
    peaks = [x[48:49] + x[49:50] + x[50:51] for x in parts]
    peak = peaks[0]
    for value in peaks[1:]:
        peak = jnp.maximum(peak, value)
    evidence = jnp.zeros_like(peak)
    terms = jnp.zeros((NSHIFT * QCLS, NPOOL * ROWS), F32)
    for x, value in zip(parts, peaks):
        scale = jnp.exp(value - peak)
        evidence = evidence + scale * (x[51:52] + x[52:53] + x[53:54])
        terms = terms + scale * x[0:48]
    line[...] = peak + jnp.log(evidence)
    log_ref[...] = line[:, pl.ds(pl.multiple_of(q * ROWS, ROWS), ROWS)]
    probs = terms / evidence
    for s in range(NSHIFT):
        slots[s * 16 : s * 16 + QCLS, :] = probs[s * QCLS : (s + 1) * QCLS]
        slots[s * 16 + QCLS : (s + 1) * 16, :] = jnp.zeros((4, NPOOL * ROWS), F32)
    padded = slots[...]
    mass = jnp.sum(padded, axis=1, keepdims=True)
    mass = mass[0:16] + mass[16:32] + mass[32:48] + mass[48:64]
    low = padded.astype(BF16)
    row_id = lax.broadcasted_iota(jnp.int32, (16, COLS), 0)
    lane_id = lax.broadcasted_iota(jnp.int32, (16, COLS), 1)
    mass_row = jnp.sum(jnp.where(row_id == lane_id, mass, 0.0), axis=0, keepdims=True)
    mass_high = mass_row.astype(BF16).astype(F32)
    mass_low = mass_row - mass_high
    for b in range(NBLK // 2):
        cols = slice(b * COLS, (b + 1) * COLS)
        cols_im = slice(K + b * COLS, K + (b + 1) * COLS)
        g_re = jnp.dot(low, pool[:, cols], preferred_element_type=F32)
        g_im = jnp.dot(low, pool[:, cols_im], preferred_element_type=F32)
        sum_re = jnp.zeros((16, COLS), F32)
        sum_im = jnp.zeros((16, COLS), F32)
        for s in range(NSHIFT):
            at = s * 16 + 2 * b
            c = jnp.concatenate([cos_ref[at : at + 1, :], cos_ref[at + 1 : at + 2, :]], axis=1)
            z = jnp.concatenate([sin_ref[at : at + 1, :], sin_ref[at + 1 : at + 2, :]], axis=1)
            re = g_re[s * 16 : (s + 1) * 16]
            im = g_im[s * 16 : (s + 1) * 16]
            sum_re = sum_re + (c * re + z * im)
            sum_im = sum_im + (c * im - z * re)
        for dest, value in ((b, sum_re), (NBLK // 2 + b, sum_im)):
            value = jnp.where(row_id == QCLS, mass_high, value)
            value = jnp.where(row_id == QCLS + 1, mass_low, value)
            out_ref[dest] = value.astype(BF16)


def place_kernel(target_ref, y_ref, out_hbm, out_ref, sem):
    total = y_ref[0].astype(F32)
    for b in range(1, NBLK):
        total = total + y_ref[b].astype(F32)
    mass = total[QCLS : QCLS + 1, 0:128] + total[QCLS + 1 : QCLS + 2, 0:128]
    row = lax.broadcasted_iota(jnp.int32, (NDOM * SLOTS, 128), 0)
    hit = target_ref[...] == row
    pick = jnp.where(hit, 1.0, 0.0).astype(BF16)
    placed = jnp.dot(pick[:, 0:16], total.astype(BF16), preferred_element_type=F32)
    placed_mass = jnp.sum(jnp.where(hit, mass, 0.0), axis=1, keepdims=True)
    high = placed_mass.astype(BF16).astype(F32)
    lane = lax.broadcasted_iota(jnp.int32, (NDOM * SLOTS, 128), 1)
    extra = jnp.where(lane == 0, high, jnp.where(lane == 1, placed_mass - high, 0.0))
    out_ref[:, :, 0:COLS] = placed.reshape(NDOM, SLOTS, COLS).astype(BF16)
    out_ref[:, :, COLS:] = extra.reshape(NDOM, SLOTS, 128).astype(BF16)
    send = pltpu.make_async_copy(out_ref, out_hbm, sem)
    send.start()
    send.wait()


def mean_kernel(z_ref, mean_ref, mass_ref):
    total = z_ref[0].astype(F32)
    for d in range(1, NDOM):
        total = total + z_ref[d].astype(F32)
    mass = total[:, COLS : COLS + 1] + total[:, COLS + 1 : COLS + 2]
    mean_ref[...] = total[:, 0:COLS] / (mass + 1.0)
    row = lax.broadcasted_iota(jnp.int32, (SLOTS, 128), 0)
    lane = lax.broadcasted_iota(jnp.int32, (SLOTS, 128), 1)
    mass_ref[...] = jnp.sum(jnp.where(row == lane, mass, 0.0), axis=0)[0:SLOTS]


def in_hbm(x):
    return pltpu.with_memory_space_constraint(x, pltpu.HBM)


def swap(x, axis):
    return lax.ppermute(x, axis, [(0, 1), (1, 0)])


def turn(x, step):
    return lax.ppermute(x, "z", [(i, (i + step) % DEPTH) for i in range(DEPTH)])


def trade(parts, axes):
    own, near, far, cross = parts
    return (
        own,
        swap(near, axes[1]),
        swap(far, axes[0]),
        lax.ppermute(cross, axes, [(i, 3 - i) for i in range(4)]),
    )


def on_device(particles, references, noise_weight, offsets, candidates, class_owner):
    pool_index = (lax.axis_index("yl") * 2 + lax.axis_index("core")).astype(jnp.int32)
    q = pool_index.reshape(1)

    zi, xi = lax.axis_index("z").astype(jnp.int32), lax.axis_index("xl").astype(jnp.int32)
    place = jnp.stack([pool_index, zi, xi])
    weight = noise_weight.reshape(16, 128)
    packed, particles = pl.pallas_call(
        pack_kernel,
        out_shape=(
            jax.ShapeDtypeStruct((BLOCK, 128), BF16),
            jax.ShapeDtypeStruct((EXTENDED, 2 * K), BF16),
        ),
        in_specs=[SMEM_SPEC, VMEM_SPEC, VMEM_SPEC, HBM_SPEC],
        out_specs=(VMEM_SPEC, VMEM_SPEC),
        scratch_shapes=[
            VMEM((LOCAL, ROT, 2 * K), F32),
            VMEM((BLOCK, 128), F32),
            pltpu.SemaphoreType.DMA,
        ],
        compiler_params=params(8),
        name="pack",
    )(q, in_hbm(candidates.T), in_hbm(references), in_hbm(particles))
    far = swap(particles, "yl")
    ring = [None] * DEPTH
    near, beside = lax.optimization_barrier((swap(particles, "core"), swap(packed, "xl")))
    ring[0] = up = down = jnp.stack([packed, beside])
    for k in range(1, DEPTH // 2):
        ring[k] = up = turn(up, 1)
        ring[DEPTH - k] = down = turn(down, -1)
    ring[DEPTH // 2] = turn(up, 1)
    flat = jax.ShapeDtypeStruct((NSHIFT * 16, 128), F32)
    cosine, sine, wc, ws = pl.pallas_call(
        tables_kernel,
        out_shape=(flat, flat, flat, flat),
        in_specs=[SMEM_SPEC, VMEM_SPEC],
        out_specs=(VMEM_SPEC,) * 4,
        compiler_params=params(4),
        cost_estimate=pl.CostEstimate(flops=1 * 10**9, bytes_accessed=3 * 10**6, transcendentals=0),
        name="tables",
    )(offsets, weight)
    far, wc, ring = lax.optimization_barrier((far, wc, ring))
    parts = (particles, near, far, swap(far, "core"))
    table_rows = NSHIFT * QROT * CLASSES
    *terms, pool = pl.pallas_call(
        score_kernel,
        out_shape=[
            jax.ShapeDtypeStruct((56, NPOOL * ROWS), F32 if j == 0 else BF16) for j in range(NPOOL)
        ]
        + [jax.ShapeDtypeStruct((NPOOL * ROWS, 2 * K), BF16)],
        in_specs=[SMEM_SPEC] + [HBM_SPEC] * DEPTH + [ANY_SPEC] * 4 + [VMEM_SPEC] * 3,
        out_specs=[VMEM_SPEC] * (NPOOL + 1),
        scratch_shapes=[
            VMEM((DEPTH, 2, BLOCK, 128), BF16),
            VMEM((NBLK * BLOCK, 128), F32),
            VMEM((table_rows, 256 * STEP_TILES), BF16),
            VMEM((table_rows, 256 * STEP_TILES), BF16),
            VMEM((table_rows, NPOOL * ROWS), F32),
            VMEM((NPOOL, 56, NPOOL * ROWS), F32),
            VMEM((8, NPOOL * ROWS), jnp.int32),
            VMEM((NPOOL, 8, ROWS), BF16),
            pltpu.SemaphoreType.DMA((2, NPOOL)),
            pltpu.SemaphoreType.DMA((DEPTH,)),
        ],
        compiler_params=params(20),
        name="score",
    )(
        place, *[in_hbm(x) for x in ring], *parts,
        wc, ws, weight,
    )
    terms = trade(terms, POOL)

    sums, log_evidence = pl.pallas_call(
        class_kernel,
        out_shape=(
            jax.ShapeDtypeStruct((NBLK, 16, COLS), BF16),
            jax.ShapeDtypeStruct((1, ROWS), F32),
        ),
        in_specs=[SMEM_SPEC] + [VMEM_SPEC] * 7,
        out_specs=(VMEM_SPEC, VMEM_SPEC),
        scratch_shapes=[
            VMEM((NSHIFT * 16, NPOOL * ROWS), F32),
            VMEM((1, NPOOL * ROWS), F32),
        ],
        compiler_params=params(16),
        name="classes",
    )(q, *terms, pool, cosine, sine)
    sums = lax.all_to_all(sums, BLK, 0, 0, tiled=True)

    class_ids = jnp.arange(CLASSES, dtype=jnp.int32)
    shared_owner = class_owner[:, None] == class_owner[None, :]
    earlier = class_ids[:, None] < class_ids[None, :]
    position = jnp.sum((shared_owner & earlier).astype(jnp.int32), axis=0)
    target = class_owner * SLOTS + position
    mine = lax.dynamic_slice(target, (pool_index * QCLS,), (QCLS,))
    mine = jnp.pad(mine, (0, 128 - QCLS), constant_values=-1).reshape(1, 128)
    placed = pl.pallas_call(
        place_kernel,
        out_shape=pltpu.HBM((NDOM, SLOTS, COLS + 128), BF16),
        in_specs=[VMEM_SPEC, VMEM_SPEC],
        out_specs=pl.BlockSpec(memory_space=pltpu.HBM),
        scratch_shapes=[VMEM((NDOM, SLOTS, COLS + 128), BF16), pltpu.SemaphoreType.DMA],
        compiler_params=params(4),
        name="place",
    )(mine, sums)
    placed = lax.all_to_all(placed, DOM, 0, 0, tiled=True)
    means, mass = pl.pallas_call(
        mean_kernel,
        out_shape=(
            jax.ShapeDtypeStruct((SLOTS, COLS), F32),
            jax.ShapeDtypeStruct((SLOTS,), F32),
        ),
        in_specs=[VMEM_SPEC],
        out_specs=(VMEM_SPEC, VMEM_SPEC),
        compiler_params=params(4),
        name="means",
    )(placed)
    return (means, mass, log_evidence.reshape(ROWS))


def solution(mesh):
    fine = Mesh(
        np.asarray(mesh.devices).reshape([size for _, size in FINE]), [name for name, _ in FINE]
    )
    every = DOM + BLK
    return jax.shard_map(
        on_device,
        mesh=fine,
        in_specs=(P(every, None), P(BLK, None, None), P(), P(), P(every, None), P()),
        out_specs=(P(DOM, BLK), P(DOM), P(every)),
        check_vma=False,
    )
```

```python
import math

import jax
import jax.numpy as jnp
import numpy as np
from jax import lax
from jax.experimental import pallas as pl
from jax.experimental.pallas import tpu as pltpu
from jax.sharding import Mesh, PartitionSpec as P

KROW = 64
KCOL = 32
BOX = 256
SLOTS = 8
INV_TEMP = 4.0
FLOOR = -1e30

FINE = (("xh", 2), ("yh", 2), ("yl", 2), ("core", 2), ("z", 8), ("xl", 2))
DOM = ("xh", "yh", "yl", "core")
BLK = ("z", "xl")
POOL = ("yl", "core")

K = 2048
CLASSES = 48
ROT = 12
NSHIFT = 4
ROWS = 128
EXTENDED = 2 * K + 128
NPOOL = 4
QROT = ROT // NPOOL
QCLS = CLASSES // NPOOL
NBLK = 16
NDOM = 16
LOCAL = 3
DEPTH = 8
BLOCK = LOCAL * QROT * 32
COLS = 256
STEP_TILES = 2
F32 = jnp.float32
BF16 = jnp.bfloat16
VMEM = pltpu.VMEM
SMEM_SPEC = pl.BlockSpec(memory_space=pltpu.SMEM)
VMEM_SPEC = pl.BlockSpec(memory_space=pltpu.VMEM)
ANY_SPEC = pl.BlockSpec(memory_space=pl.ANY)
HBM_SPEC = pl.BlockSpec(memory_space=pltpu.HBM)


def params(mib):
    return pltpu.CompilerParams(vmem_limit_bytes=mib << 20)


def pack_kernel(q_ref, cand_ref, refs_ref, particles_hbm, out_ref, extended_ref, wide, rows, sem):
    copy = pltpu.make_async_copy(particles_hbm, extended_ref.at[:, pl.ds(0, 2 * K)], sem)
    copy.start()
    cand = jnp.concatenate([cand_ref[...].astype(F32), jnp.zeros((ROWS - 8, 128), F32)], axis=0)
    extended_ref[:, 2 * K :] = cand.astype(BF16)
    q = q_ref[0]
    wide[...] = refs_ref[...].astype(F32)
    for c in range(LOCAL):
        for r in range(QROT):
            row = wide[c, pl.ds(QROT * q + r, 1), :]
            for a in range(32):
                at = (c * QROT + r) * 32 + a
                rows[at : at + 1, :] = row[:, a * 128 : (a + 1) * 128]
    out_ref[...] = rows[...].astype(BF16)
    copy.wait()


def tables_kernel(off_ref, w_ref, cos_ref, sin_ref, wc_ref, ws_ref):
    row = lax.broadcasted_iota(jnp.int32, (16, 128), 0)
    lane = lax.broadcasted_iota(jnp.int32, (16, 128), 1)
    column = lane % KCOL
    rowpos = row * (128 // KCOL) + lane // KCOL - KROW // 2
    weight = w_ref[...]
    for s in range(NSHIFT):
        turns = (off_ref[s, 0] * column + off_ref[s, 1] * rowpos).astype(F32)
        angle = turns * (2.0 * math.pi / BOX)
        cosine, sine = jnp.cos(angle), jnp.sin(angle)
        at = slice(s * 16, (s + 1) * 16)
        cos_ref[at, :] = cosine
        sin_ref[at, :] = sine
        wc_ref[at, :] = weight * cosine
        ws_ref[at, :] = weight * sine


def pool_copies(q, parts, pool, listed, sem):
    copies = []
    for j, part in enumerate(parts):
        rows = pl.ds(pl.multiple_of((q ^ j) * ROWS, ROWS), ROWS)
        whole = part.at[:, pl.ds(0, 2 * K)]
        copies.append(pltpu.make_async_copy(whole, pool.at[rows, :], sem.at[0, j]))
        few = part.at[pl.ds(0, 8), pl.ds(2 * K, ROWS)]
        copies.append(pltpu.make_async_copy(few, listed.at[j], sem.at[1, j]))
    return copies


def split(x):
    high = x.astype(BF16).astype(F32)
    middle = (x - high).astype(BF16).astype(F32)
    return (high, middle, x - high - middle)


def score_kernel(
    index_ref, *refs
):
    blocks = refs[:DEPTH]
    p0, p1, p2, p3, wc_ref, ws_ref, w_ref = refs[DEPTH : DEPTH + 7]
    own_ref, near_ref, far_ref, cross_ref, pool = refs[DEPTH + 7 : DEPTH + 12]
    stage, wide, table0, table1, scores, groups, cands, listed, sem, block_sem = refs[DEPTH + 12 :]
    q, z, xl = index_ref[0], index_ref[1], index_ref[2]
    block_copies = []
    for k, block in enumerate(blocks):
        block_copies.append(pltpu.make_async_copy(block, stage.at[k], block_sem.at[k]))
    for copy in block_copies:
        copy.start()
    steps = 16 // STEP_TILES
    wide_cols = 128 * STEP_TILES
    copies = pool_copies(q, (p0, p1, p2, p3), pool, listed, sem)
    for copy in copies:
        copy.start()
    for k, copy in enumerate(block_copies):
        copy.wait()
        for side in range(2):
            source = ((z + DEPTH - k) % DEPTH) * 2 + (xl ^ side)
            rows = pl.ds(pl.multiple_of(source * BLOCK, BLOCK), BLOCK)
            wide[rows, :] = stage[k, side].astype(F32)
    energy = [jnp.zeros((CLASSES, 128), F32) for _ in range(QROT)]
    stride = QROT * 32
    tables = (table0, table1)

    def build(step):
        table = tables[step % 2]
        for t in range(STEP_TILES):
            a = step * STEP_TILES + t
            weight = w_ref[a : a + 1, :]
            for r in range(QROT):
                real = wide[pl.ds(r * 32 + a, CLASSES, stride=stride), :]
                imag = wide[pl.ds(r * 32 + 16 + a, CLASSES, stride=stride), :]
                energy[r] = energy[r] + weight * (real * real + imag * imag)
                for s in range(NSHIFT):
                    wc = wc_ref[s * 16 + a : s * 16 + a + 1, :]
                    ws = ws_ref[s * 16 + a : s * 16 + a + 1, :]
                    row = (s * QROT + r) * CLASSES
                    at = slice(t * 128, (t + 1) * 128)
                    at_im = slice(wide_cols + t * 128, wide_cols + (t + 1) * 128)
                    table[row : row + CLASSES, at] = (wc * real - ws * imag).astype(BF16)
                    table[row : row + CLASSES, at_im] = (ws * real + wc * imag).astype(BF16)

    build(0)
    for copy in copies:
        copy.wait()
    for j in range(NPOOL):
        cand = listed[j].astype(F32).astype(jnp.int32)
        cands[:, pl.ds(pl.multiple_of((q ^ j) * ROWS, ROWS), ROWS)] = cand
    for step in range(steps):
        if step + 1 < steps:
            build(step + 1)
        table = tables[step % 2]
        cols = slice(step * wide_cols, (step + 1) * wide_cols)
        cols_im = slice(K + step * wide_cols, K + (step + 1) * wide_cols)
        for n in range(2):
            lanes = slice(n * 256, (n + 1) * 256)
            part = lax.dot_general(
                table[:, 0:wide_cols], pool[lanes, cols], (((1,), (1,)), ((), ())),
                preferred_element_type=F32,
            ) + lax.dot_general(
                table[:, wide_cols:], pool[lanes, cols_im], (((1,), (1,)), ((), ())),
                preferred_element_type=F32,
            )
            if step == 0:
                scores[:, lanes] = part
            else:
                scores[:, lanes] += part

    half_energy = [0.5 * jnp.sum(e, axis=1, keepdims=True) for e in energy]
    class_id = lax.broadcasted_iota(jnp.int32, (CLASSES, 256), 0)
    for n in range(2):
        lanes = slice(n * 256, (n + 1) * 256)
        cand = cands[:, lanes]
        allowed = class_id == cand[0:1, :]
        for k in range(1, 8):
            allowed = allowed | (class_id == cand[k : k + 1, :])
        loglik = []
        for s in range(NSHIFT):
            for r in range(QROT):
                row = (s * QROT + r) * CLASSES
                value = INV_TEMP * (scores[row : row + CLASSES, lanes] - half_energy[r])
                loglik.append(jnp.where(allowed, value, FLOOR))
        top = loglik[0]
        for value in loglik[1:]:
            top = jnp.maximum(top, value)
        peak = jnp.max(top, axis=0, keepdims=True)
        evidence = jnp.zeros((1, 256), F32)
        for s in range(NSHIFT):
            terms = jnp.zeros((CLASSES, 256), F32)
            for r in range(QROT):
                value = loglik[s * QROT + r]
                terms = terms + jnp.where(allowed, jnp.exp(value - peak), 0.0)
            evidence = evidence + jnp.sum(terms, axis=0, keepdims=True)
            for d in range(NPOOL):
                groups[d, s * QCLS : (s + 1) * QCLS, lanes] = terms[d * QCLS : (d + 1) * QCLS]
        pieces = split(peak) + split(evidence)
        for d in range(NPOOL):
            for i, piece in enumerate(pieces):
                groups[d, 48 + i : 49 + i, lanes] = piece
            groups[d, 54:56, lanes] = jnp.zeros((2, 256), F32)
    own_ref[...] = groups[q]
    for j, ref in enumerate((near_ref, far_ref, cross_ref)):
        ref[...] = groups[q ^ (j + 1)].astype(BF16)


def class_kernel(
    q_ref, x0, x1, x2, x3, pool, cos_ref, sin_ref, out_ref, log_ref, slots, line
):
    q = q_ref[0]
    parts = [x[...].astype(F32) for x in (x0, x1, x2, x3)]
    peaks = [x[48:49] + x[49:50] + x[50:51] for x in parts]
    peak = peaks[0]
    for value in peaks[1:]:
        peak = jnp.maximum(peak, value)
    evidence = jnp.zeros_like(peak)
    terms = jnp.zeros((NSHIFT * QCLS, NPOOL * ROWS), F32)
    for x, value in zip(parts, peaks):
        scale = jnp.exp(value - peak)
        evidence = evidence + scale * (x[51:52] + x[52:53] + x[53:54])
        terms = terms + scale * x[0:48]
    line[...] = peak + jnp.log(evidence)
    log_ref[...] = line[:, pl.ds(pl.multiple_of(q * ROWS, ROWS), ROWS)]
    probs = terms / evidence
    for s in range(NSHIFT):
        slots[s * 16 : s * 16 + QCLS, :] = probs[s * QCLS : (s + 1) * QCLS]
        slots[s * 16 + QCLS : (s + 1) * 16, :] = jnp.zeros((4, NPOOL * ROWS), F32)
    padded = slots[...]
    mass = jnp.sum(padded, axis=1, keepdims=True)
    mass = mass[0:16] + mass[16:32] + mass[32:48] + mass[48:64]
    low = padded.astype(BF16)
    row_id = lax.broadcasted_iota(jnp.int32, (16, COLS), 0)
    lane_id = lax.broadcasted_iota(jnp.int32, (16, COLS), 1)
    mass_row = jnp.sum(jnp.where(row_id == lane_id, mass, 0.0), axis=0, keepdims=True)
    mass_high = mass_row.astype(BF16).astype(F32)
    mass_low = mass_row - mass_high
    for b in range(NBLK // 2):
        cols = slice(b * COLS, (b + 1) * COLS)
        cols_im = slice(K + b * COLS, K + (b + 1) * COLS)
        g_re = jnp.dot(low, pool[:, cols], preferred_element_type=F32)
        g_im = jnp.dot(low, pool[:, cols_im], preferred_element_type=F32)
        sum_re = jnp.zeros((16, COLS), F32)
        sum_im = jnp.zeros((16, COLS), F32)
        for s in range(NSHIFT):
            at = s * 16 + 2 * b
            c = jnp.concatenate([cos_ref[at : at + 1, :], cos_ref[at + 1 : at + 2, :]], axis=1)
            z = jnp.concatenate([sin_ref[at : at + 1, :], sin_ref[at + 1 : at + 2, :]], axis=1)
            re = g_re[s * 16 : (s + 1) * 16]
            im = g_im[s * 16 : (s + 1) * 16]
            sum_re = sum_re + (c * re + z * im)
            sum_im = sum_im + (c * im - z * re)
        for dest, value in ((b, sum_re), (NBLK // 2 + b, sum_im)):
            value = jnp.where(row_id == QCLS, mass_high, value)
            value = jnp.where(row_id == QCLS + 1, mass_low, value)
            out_ref[dest] = value.astype(BF16)


def place_kernel(target_ref, y_ref, out_hbm, out_ref, sem):
    total = y_ref[0].astype(F32)
    for b in range(1, NBLK):
        total = total + y_ref[b].astype(F32)
    mass = total[QCLS : QCLS + 1, 0:128] + total[QCLS + 1 : QCLS + 2, 0:128]
    row = lax.broadcasted_iota(jnp.int32, (NDOM * SLOTS, 128), 0)
    hit = target_ref[...] == row
    pick = jnp.where(hit, 1.0, 0.0).astype(BF16)
    placed = jnp.dot(pick[:, 0:16], total.astype(BF16), preferred_element_type=F32)
    placed_mass = jnp.sum(jnp.where(hit, mass, 0.0), axis=1, keepdims=True)
    high = placed_mass.astype(BF16).astype(F32)
    lane = lax.broadcasted_iota(jnp.int32, (NDOM * SLOTS, 128), 1)
    extra = jnp.where(lane == 0, high, jnp.where(lane == 1, placed_mass - high, 0.0))
    out_ref[:, :, 0:COLS] = placed.reshape(NDOM, SLOTS, COLS).astype(BF16)
    out_ref[:, :, COLS:] = extra.reshape(NDOM, SLOTS, 128).astype(BF16)
    send = pltpu.make_async_copy(out_ref, out_hbm, sem)
    send.start()
    send.wait()


def mean_kernel(z_ref, mean_ref, mass_ref):
    total = z_ref[0].astype(F32)
    for d in range(1, NDOM):
        total = total + z_ref[d].astype(F32)
    mass = total[:, COLS : COLS + 1] + total[:, COLS + 1 : COLS + 2]
    mean_ref[...] = total[:, 0:COLS] / (mass + 1.0)
    row = lax.broadcasted_iota(jnp.int32, (SLOTS, 128), 0)
    lane = lax.broadcasted_iota(jnp.int32, (SLOTS, 128), 1)
    mass_ref[...] = jnp.sum(jnp.where(row == lane, mass, 0.0), axis=0)[0:SLOTS]


def in_hbm(x):
    return pltpu.with_memory_space_constraint(x, pltpu.HBM)


def swap(x, axis):
    return lax.ppermute(x, axis, [(0, 1), (1, 0)])


def turn(x, step):
    return lax.ppermute(x, "z", [(i, (i + step) % DEPTH) for i in range(DEPTH)])


def trade(parts, axes):
    own, near, far, cross = parts
    return (
        own,
        swap(near, axes[1]),
        swap(far, axes[0]),
        lax.ppermute(cross, axes, [(i, 3 - i) for i in range(4)]),
    )


def on_device(particles, references, noise_weight, offsets, candidates, class_owner):
    pool_index = (lax.axis_index("yl") * 2 + lax.axis_index("core")).astype(jnp.int32)
    q = pool_index.reshape(1)

    zi, xi = lax.axis_index("z").astype(jnp.int32), lax.axis_index("xl").astype(jnp.int32)
    place = jnp.stack([pool_index, zi, xi])
    weight = noise_weight.reshape(16, 128)
    packed, particles = pl.pallas_call(
        pack_kernel,
        out_shape=(
            jax.ShapeDtypeStruct((BLOCK, 128), BF16),
            jax.ShapeDtypeStruct((ROWS, EXTENDED), BF16),
        ),
        in_specs=[SMEM_SPEC, VMEM_SPEC, VMEM_SPEC, HBM_SPEC],
        out_specs=(VMEM_SPEC, VMEM_SPEC),
        scratch_shapes=[
            VMEM((LOCAL, ROT, 2 * K), F32),
            VMEM((BLOCK, 128), F32),
            pltpu.SemaphoreType.DMA,
        ],
        compiler_params=params(8),
        name="pack",
    )(q, in_hbm(candidates.T), in_hbm(references), in_hbm(particles))
    far = swap(particles, "yl")
    ring = [None] * DEPTH
    near, beside = lax.optimization_barrier((swap(particles, "core"), swap(packed, "xl")))
    ring[0] = up = down = jnp.stack([packed, beside])
    for k in range(1, DEPTH // 2):
        ring[k] = up = turn(up, 1)
        ring[DEPTH - k] = down = turn(down, -1)
    ring[DEPTH // 2] = turn(up, 1)
    flat = jax.ShapeDtypeStruct((NSHIFT * 16, 128), F32)
    cosine, sine, wc, ws = pl.pallas_call(
        tables_kernel,
        out_shape=(flat, flat, flat, flat),
        in_specs=[SMEM_SPEC, VMEM_SPEC],
        out_specs=(VMEM_SPEC,) * 4,
        compiler_params=params(4),
        cost_estimate=pl.CostEstimate(flops=1 * 10**9, bytes_accessed=3 * 10**6, transcendentals=0),
        name="tables",
    )(offsets, weight)
    far, wc, ring = lax.optimization_barrier((far, wc, ring))
    parts = (particles, near, far, swap(far, "core"))
    table_rows = NSHIFT * QROT * CLASSES
    *terms, pool = pl.pallas_call(
        score_kernel,
        out_shape=[
            jax.ShapeDtypeStruct((56, NPOOL * ROWS), F32 if j == 0 else BF16) for j in range(NPOOL)
        ]
        + [jax.ShapeDtypeStruct((NPOOL * ROWS, 2 * K), BF16)],
        in_specs=[SMEM_SPEC] + [HBM_SPEC] * DEPTH + [ANY_SPEC] * 4 + [VMEM_SPEC] * 3,
        out_specs=[VMEM_SPEC] * (NPOOL + 1),
        scratch_shapes=[
            VMEM((DEPTH, 2, BLOCK, 128), BF16),
            VMEM((NBLK * BLOCK, 128), F32),
            VMEM((table_rows, 256 * STEP_TILES), BF16),
            VMEM((table_rows, 256 * STEP_TILES), BF16),
            VMEM((table_rows, NPOOL * ROWS), F32),
            VMEM((NPOOL, 56, NPOOL * ROWS), F32),
            VMEM((8, NPOOL * ROWS), jnp.int32),
            VMEM((NPOOL, 8, ROWS), BF16),
            pltpu.SemaphoreType.DMA((2, NPOOL)),
            pltpu.SemaphoreType.DMA((DEPTH,)),
        ],
        compiler_params=params(20),
        name="score",
    )(
        place, *[in_hbm(x) for x in ring], *parts,
        wc, ws, weight,
    )
    terms = trade(terms, POOL)

    sums, log_evidence = pl.pallas_call(
        class_kernel,
        out_shape=(
            jax.ShapeDtypeStruct((NBLK, 16, COLS), BF16),
            jax.ShapeDtypeStruct((1, ROWS), F32),
        ),
        in_specs=[SMEM_SPEC] + [VMEM_SPEC] * 7,
        out_specs=(VMEM_SPEC, VMEM_SPEC),
        scratch_shapes=[
            VMEM((NSHIFT * 16, NPOOL * ROWS), F32),
            VMEM((1, NPOOL * ROWS), F32),
        ],
        compiler_params=params(16),
        name="classes",
    )(q, *terms, pool, cosine, sine)
    sums = lax.all_to_all(sums, BLK, 0, 0, tiled=True)

    class_ids = jnp.arange(CLASSES, dtype=jnp.int32)
    shared_owner = class_owner[:, None] == class_owner[None, :]
    earlier = class_ids[:, None] < class_ids[None, :]
    position = jnp.sum((shared_owner & earlier).astype(jnp.int32), axis=0)
    target = class_owner * SLOTS + position
    mine = lax.dynamic_slice(target, (pool_index * QCLS,), (QCLS,))
    mine = jnp.pad(mine, (0, 128 - QCLS), constant_values=-1).reshape(1, 128)
    placed = pl.pallas_call(
        place_kernel,
        out_shape=pltpu.HBM((NDOM, SLOTS, COLS + 128), BF16),
        in_specs=[VMEM_SPEC, VMEM_SPEC],
        out_specs=pl.BlockSpec(memory_space=pltpu.HBM),
        scratch_shapes=[VMEM((NDOM, SLOTS, COLS + 128), BF16), pltpu.SemaphoreType.DMA],
        compiler_params=params(4),
        name="place",
    )(mine, sums)
    placed = lax.all_to_all(placed, DOM, 0, 0, tiled=True)
    means, mass = pl.pallas_call(
        mean_kernel,
        out_shape=(
            jax.ShapeDtypeStruct((SLOTS, COLS), F32),
            jax.ShapeDtypeStruct((SLOTS,), F32),
        ),
        in_specs=[VMEM_SPEC],
        out_specs=(VMEM_SPEC, VMEM_SPEC),
        compiler_params=params(4),
        name="means",
    )(placed)
    return (means, mass, log_evidence.reshape(ROWS))


def solution(mesh):
    fine = Mesh(
        np.asarray(mesh.devices).reshape([size for _, size in FINE]), [name for name, _ in FINE]
    )
    every = DOM + BLK
    return jax.shard_map(
        on_device,
        mesh=fine,
        in_specs=(P(every, None), P(BLK, None, None), P(), P(), P(every, None), P()),
        out_specs=(P(DOM, BLK), P(DOM), P(every)),
        check_vma=False,
    )
```

```python
import math

import jax
import jax.numpy as jnp
import numpy as np
from jax import lax
from jax.experimental import pallas as pl
from jax.experimental.pallas import tpu as pltpu
from jax.sharding import Mesh, PartitionSpec as P

KROW = 64
KCOL = 32
BOX = 256
SLOTS = 8
INV_TEMP = 4.0
FLOOR = -1e30

FINE = (("xh", 2), ("yh", 2), ("yl", 2), ("core", 2), ("z", 8), ("xl", 2))
DOM = ("xh", "yh", "yl", "core")
BLK = ("z", "xl")
POOL = ("yl", "core")

K = 2048
CLASSES = 48
ROT = 12
NSHIFT = 4
ROWS = 128
EXTENDED = 2 * K + 128
NPOOL = 4
QROT = ROT // NPOOL
QCLS = CLASSES // NPOOL
NBLK = 16
NDOM = 16
LOCAL = 3
DEPTH = 8
BLOCK = LOCAL * QROT * 32
COLS = 256
STEP_TILES = 2
F32 = jnp.float32
BF16 = jnp.bfloat16
VMEM = pltpu.VMEM
SMEM_SPEC = pl.BlockSpec(memory_space=pltpu.SMEM)
VMEM_SPEC = pl.BlockSpec(memory_space=pltpu.VMEM)
ANY_SPEC = pl.BlockSpec(memory_space=pl.ANY)
HBM_SPEC = pl.BlockSpec(memory_space=pltpu.HBM)


def params(mib):
    return pltpu.CompilerParams(vmem_limit_bytes=mib << 20)


def pack_kernel(q_ref, cand_ref, refs_ref, particles_hbm, out_ref, extended_ref, wide, rows, sem):
    copy = pltpu.make_async_copy(particles_hbm, extended_ref.at[:, pl.ds(0, 2 * K)], sem)
    copy.start()
    cand = jnp.concatenate([cand_ref[...].astype(F32), jnp.zeros((ROWS - 8, 128), F32)], axis=0)
    extended_ref[:, 2 * K :] = cand.astype(BF16)
    q = q_ref[0]
    wide[...] = refs_ref[...].astype(F32)
    for c in range(LOCAL):
        for r in range(QROT):
            row = wide[c, pl.ds(QROT * q + r, 1), :]
            for a in range(32):
                at = (c * QROT + r) * 32 + a
                rows[at : at + 1, :] = row[:, a * 128 : (a + 1) * 128]
    out_ref[...] = rows[...].astype(BF16)
    copy.wait()


def tables_kernel(off_ref, w_ref, cos_ref, sin_ref, wc_ref, ws_ref):
    row = lax.broadcasted_iota(jnp.int32, (16, 128), 0)
    lane = lax.broadcasted_iota(jnp.int32, (16, 128), 1)
    column = lane % KCOL
    rowpos = row * (128 // KCOL) + lane // KCOL - KROW // 2
    weight = w_ref[...]
    for s in range(NSHIFT):
        turns = (off_ref[s, 0] * column + off_ref[s, 1] * rowpos).astype(F32)
        angle = turns * (2.0 * math.pi / BOX)
        cosine, sine = jnp.cos(angle), jnp.sin(angle)
        at = slice(s * 16, (s + 1) * 16)
        cos_ref[at, :] = cosine
        sin_ref[at, :] = sine
        wc_ref[at, :] = weight * cosine
        ws_ref[at, :] = weight * sine


def pool_copies(q, parts, pool, listed, sem):
    copies = []
    for j, part in enumerate(parts):
        rows = pl.ds(pl.multiple_of((q ^ j) * ROWS, ROWS), ROWS)
        whole = part.at[:, pl.ds(0, 2 * K)]
        copies.append(pltpu.make_async_copy(whole, pool.at[rows, :], sem.at[0, j]))
        few = part.at[pl.ds(0, 8), pl.ds(2 * K, ROWS)]
        copies.append(pltpu.make_async_copy(few, listed.at[j], sem.at[1, j]))
    return copies


def split(x):
    high = x.astype(BF16).astype(F32)
    middle = (x - high).astype(BF16).astype(F32)
    return (high, middle, x - high - middle)


def score_kernel(
    index_ref, *refs
):
    blocks, refs = refs[: DEPTH + 1], refs[1:]
    p0, p1, p2, p3, wc_ref, ws_ref, w_ref = refs[DEPTH : DEPTH + 7]
    own_ref, near_ref, far_ref, cross_ref, pool = refs[DEPTH + 7 : DEPTH + 12]
    stage, wide, table0, table1, scores, groups, cands, listed, sem, block_sem = refs[DEPTH + 12 :]
    q, z, xl = index_ref[0], index_ref[1], index_ref[2]
    block_copies = []
    for k, block in enumerate(blocks):
        slot = stage.at[k % DEPTH]
        if k in (DEPTH // 2, DEPTH):
            slot = stage.at[DEPTH // 2, k // DEPTH]
        block_copies.append(pltpu.make_async_copy(block, slot, block_sem.at[k]))
    for copy in block_copies:
        copy.start()
    steps = 16 // STEP_TILES
    wide_cols = 128 * STEP_TILES
    copies = pool_copies(q, (p0, p1, p2, p3), pool, listed, sem)
    for copy in copies:
        copy.start()
    for k in range(DEPTH):
        block_copies[k].wait()
        if k == DEPTH // 2:
            block_copies[DEPTH].wait()
        for side in range(2):
            source = ((z + DEPTH - k) % DEPTH) * 2 + (xl ^ side)
            rows = pl.ds(pl.multiple_of(source * BLOCK, BLOCK), BLOCK)
            wide[rows, :] = stage[k, side].astype(F32)
    energy = [jnp.zeros((CLASSES, 128), F32) for _ in range(QROT)]
    stride = QROT * 32
    tables = (table0, table1)

    def build(step):
        table = tables[step % 2]
        for t in range(STEP_TILES):
            a = step * STEP_TILES + t
            weight = w_ref[a : a + 1, :]
            for r in range(QROT):
                real = wide[pl.ds(r * 32 + a, CLASSES, stride=stride), :]
                imag = wide[pl.ds(r * 32 + 16 + a, CLASSES, stride=stride), :]
                energy[r] = energy[r] + weight * (real * real + imag * imag)
                for s in range(NSHIFT):
                    wc = wc_ref[s * 16 + a : s * 16 + a + 1, :]
                    ws = ws_ref[s * 16 + a : s * 16 + a + 1, :]
                    row = (s * QROT + r) * CLASSES
                    at = slice(t * 128, (t + 1) * 128)
                    at_im = slice(wide_cols + t * 128, wide_cols + (t + 1) * 128)
                    table[row : row + CLASSES, at] = (wc * real - ws * imag).astype(BF16)
                    table[row : row + CLASSES, at_im] = (ws * real + wc * imag).astype(BF16)

    build(0)
    for copy in copies:
        copy.wait()
    for j in range(NPOOL):
        cand = listed[j].astype(F32).astype(jnp.int32)
        cands[:, pl.ds(pl.multiple_of((q ^ j) * ROWS, ROWS), ROWS)] = cand
    for step in range(steps):
        if step + 1 < steps:
            build(step + 1)
        table = tables[step % 2]
        cols = slice(step * wide_cols, (step + 1) * wide_cols)
        cols_im = slice(K + step * wide_cols, K + (step + 1) * wide_cols)
        for n in range(2):
            lanes = slice(n * 256, (n + 1) * 256)
            part = lax.dot_general(
                table[:, 0:wide_cols], pool[lanes, cols], (((1,), (1,)), ((), ())),
                preferred_element_type=F32,
            ) + lax.dot_general(
                table[:, wide_cols:], pool[lanes, cols_im], (((1,), (1,)), ((), ())),
                preferred_element_type=F32,
            )
            if step == 0:
                scores[:, lanes] = part
            else:
                scores[:, lanes] += part

    half_energy = [0.5 * jnp.sum(e, axis=1, keepdims=True) for e in energy]
    class_id = lax.broadcasted_iota(jnp.int32, (CLASSES, 256), 0)
    for n in range(2):
        lanes = slice(n * 256, (n + 1) * 256)
        cand = cands[:, lanes]
        allowed = class_id == cand[0:1, :]
        for k in range(1, 8):
            allowed = allowed | (class_id == cand[k : k + 1, :])
        loglik = []
        for s in range(NSHIFT):
            for r in range(QROT):
                row = (s * QROT + r) * CLASSES
                value = INV_TEMP * (scores[row : row + CLASSES, lanes] - half_energy[r])
                loglik.append(jnp.where(allowed, value, FLOOR))
        top = loglik[0]
        for value in loglik[1:]:
            top = jnp.maximum(top, value)
        peak = jnp.max(top, axis=0, keepdims=True)
        evidence = jnp.zeros((1, 256), F32)
        for s in range(NSHIFT):
            terms = jnp.zeros((CLASSES, 256), F32)
            for r in range(QROT):
                value = loglik[s * QROT + r]
                terms = terms + jnp.where(allowed, jnp.exp(value - peak), 0.0)
            evidence = evidence + jnp.sum(terms, axis=0, keepdims=True)
            for d in range(NPOOL):
                groups[d, s * QCLS : (s + 1) * QCLS, lanes] = terms[d * QCLS : (d + 1) * QCLS]
        pieces = split(peak) + split(evidence)
        for d in range(NPOOL):
            for i, piece in enumerate(pieces):
                groups[d, 48 + i : 49 + i, lanes] = piece
            groups[d, 54:56, lanes] = jnp.zeros((2, 256), F32)
    own_ref[...] = groups[q]
    for j, ref in enumerate((near_ref, far_ref, cross_ref)):
        ref[...] = groups[q ^ (j + 1)].astype(BF16)


def class_kernel(
    q_ref, x0, x1, x2, x3, pool, cos_ref, sin_ref, out_ref, log_ref, slots, line
):
    q = q_ref[0]
    parts = [x[...].astype(F32) for x in (x0, x1, x2, x3)]
    peaks = [x[48:49] + x[49:50] + x[50:51] for x in parts]
    peak = peaks[0]
    for value in peaks[1:]:
        peak = jnp.maximum(peak, value)
    evidence = jnp.zeros_like(peak)
    terms = jnp.zeros((NSHIFT * QCLS, NPOOL * ROWS), F32)
    for x, value in zip(parts, peaks):
        scale = jnp.exp(value - peak)
        evidence = evidence + scale * (x[51:52] + x[52:53] + x[53:54])
        terms = terms + scale * x[0:48]
    line[...] = peak + jnp.log(evidence)
    log_ref[...] = line[:, pl.ds(pl.multiple_of(q * ROWS, ROWS), ROWS)]
    probs = terms / evidence
    for s in range(NSHIFT):
        slots[s * 16 : s * 16 + QCLS, :] = probs[s * QCLS : (s + 1) * QCLS]
        slots[s * 16 + QCLS : (s + 1) * 16, :] = jnp.zeros((4, NPOOL * ROWS), F32)
    padded = slots[...]
    mass = jnp.sum(padded, axis=1, keepdims=True)
    mass = mass[0:16] + mass[16:32] + mass[32:48] + mass[48:64]
    low = padded.astype(BF16)
    row_id = lax.broadcasted_iota(jnp.int32, (16, COLS), 0)
    lane_id = lax.broadcasted_iota(jnp.int32, (16, COLS), 1)
    mass_row = jnp.sum(jnp.where(row_id == lane_id, mass, 0.0), axis=0, keepdims=True)
    mass_high = mass_row.astype(BF16).astype(F32)
    mass_low = mass_row - mass_high
    for b in range(NBLK // 2):
        cols = slice(b * COLS, (b + 1) * COLS)
        cols_im = slice(K + b * COLS, K + (b + 1) * COLS)
        g_re = jnp.dot(low, pool[:, cols], preferred_element_type=F32)
        g_im = jnp.dot(low, pool[:, cols_im], preferred_element_type=F32)
        sum_re = jnp.zeros((16, COLS), F32)
        sum_im = jnp.zeros((16, COLS), F32)
        for s in range(NSHIFT):
            at = s * 16 + 2 * b
            c = jnp.concatenate([cos_ref[at : at + 1, :], cos_ref[at + 1 : at + 2, :]], axis=1)
            z = jnp.concatenate([sin_ref[at : at + 1, :], sin_ref[at + 1 : at + 2, :]], axis=1)
            re = g_re[s * 16 : (s + 1) * 16]
            im = g_im[s * 16 : (s + 1) * 16]
            sum_re = sum_re + (c * re + z * im)
            sum_im = sum_im + (c * im - z * re)
        for dest, value in ((b, sum_re), (NBLK // 2 + b, sum_im)):
            value = jnp.where(row_id == QCLS, mass_high, value)
            value = jnp.where(row_id == QCLS + 1, mass_low, value)
            out_ref[dest] = value.astype(BF16)


def place_kernel(target_ref, y_ref, out_hbm, out_ref, sem):
    total = y_ref[0].astype(F32)
    for b in range(1, NBLK):
        total = total + y_ref[b].astype(F32)
    mass = total[QCLS : QCLS + 1, 0:128] + total[QCLS + 1 : QCLS + 2, 0:128]
    row = lax.broadcasted_iota(jnp.int32, (NDOM * SLOTS, 128), 0)
    hit = target_ref[...] == row
    pick = jnp.where(hit, 1.0, 0.0).astype(BF16)
    placed = jnp.dot(pick[:, 0:16], total.astype(BF16), preferred_element_type=F32)
    placed_mass = jnp.sum(jnp.where(hit, mass, 0.0), axis=1, keepdims=True)
    high = placed_mass.astype(BF16).astype(F32)
    lane = lax.broadcasted_iota(jnp.int32, (NDOM * SLOTS, 128), 1)
    extra = jnp.where(lane == 0, high, jnp.where(lane == 1, placed_mass - high, 0.0))
    out_ref[:, :, 0:COLS] = placed.reshape(NDOM, SLOTS, COLS).astype(BF16)
    out_ref[:, :, COLS:] = extra.reshape(NDOM, SLOTS, 128).astype(BF16)
    send = pltpu.make_async_copy(out_ref, out_hbm, sem)
    send.start()
    send.wait()


def mean_kernel(z_ref, mean_ref, mass_ref):
    total = z_ref[0].astype(F32)
    for d in range(1, NDOM):
        total = total + z_ref[d].astype(F32)
    mass = total[:, COLS : COLS + 1] + total[:, COLS + 1 : COLS + 2]
    mean_ref[...] = total[:, 0:COLS] / (mass + 1.0)
    row = lax.broadcasted_iota(jnp.int32, (SLOTS, 128), 0)
    lane = lax.broadcasted_iota(jnp.int32, (SLOTS, 128), 1)
    mass_ref[...] = jnp.sum(jnp.where(row == lane, mass, 0.0), axis=0)[0:SLOTS]


def in_hbm(x):
    return pltpu.with_memory_space_constraint(x, pltpu.HBM)


def swap(x, axis):
    return lax.ppermute(x, axis, [(0, 1), (1, 0)])


def turn(x, step):
    return lax.ppermute(x, "z", [(i, (i + step) % DEPTH) for i in range(DEPTH)])


def trade(parts, axes):
    own, near, far, cross = parts
    return (
        own,
        swap(near, axes[1]),
        swap(far, axes[0]),
        lax.ppermute(cross, axes, [(i, 3 - i) for i in range(4)]),
    )


def on_device(particles, references, noise_weight, offsets, candidates, class_owner):
    pool_index = (lax.axis_index("yl") * 2 + lax.axis_index("core")).astype(jnp.int32)
    q = pool_index.reshape(1)

    zi, xi = lax.axis_index("z").astype(jnp.int32), lax.axis_index("xl").astype(jnp.int32)
    place = jnp.stack([pool_index, zi, xi])
    weight = noise_weight.reshape(16, 128)
    packed, particles = pl.pallas_call(
        pack_kernel,
        out_shape=(
            jax.ShapeDtypeStruct((BLOCK, 128), BF16),
            jax.ShapeDtypeStruct((ROWS, EXTENDED), BF16),
        ),
        in_specs=[SMEM_SPEC, VMEM_SPEC, VMEM_SPEC, HBM_SPEC],
        out_specs=(VMEM_SPEC, VMEM_SPEC),
        scratch_shapes=[
            VMEM((LOCAL, ROT, 2 * K), F32),
            VMEM((BLOCK, 128), F32),
            pltpu.SemaphoreType.DMA,
        ],
        compiler_params=params(8),
        name="pack",
    )(q, in_hbm(candidates.T), in_hbm(references), in_hbm(particles))
    far = swap(particles, "yl")
    ring = [None] * DEPTH
    near, beside = lax.optimization_barrier((swap(particles, "core"), swap(packed, "xl")))
    ring[0] = up = down = jnp.stack([packed, beside])
    for k in range(1, DEPTH // 2):
        ring[k] = up = turn(up, 1)
        ring[DEPTH - k] = down = turn(down, -1)
    ring[DEPTH // 2] = turn(up[0], 1)
    ring.append(turn(down[1], -1))
    flat = jax.ShapeDtypeStruct((NSHIFT * 16, 128), F32)
    cosine, sine, wc, ws = pl.pallas_call(
        tables_kernel,
        out_shape=(flat, flat, flat, flat),
        in_specs=[SMEM_SPEC, VMEM_SPEC],
        out_specs=(VMEM_SPEC,) * 4,
        compiler_params=params(4),
        cost_estimate=pl.CostEstimate(flops=1 * 10**9, bytes_accessed=3 * 10**6, transcendentals=0),
        name="tables",
    )(offsets, weight)
    far, wc, ring = lax.optimization_barrier((far, wc, ring))
    parts = (particles, near, far, swap(far, "core"))
    table_rows = NSHIFT * QROT * CLASSES
    *terms, pool = pl.pallas_call(
        score_kernel,
        out_shape=[
            jax.ShapeDtypeStruct((56, NPOOL * ROWS), F32 if j == 0 else BF16) for j in range(NPOOL)
        ]
        + [jax.ShapeDtypeStruct((NPOOL * ROWS, 2 * K), BF16)],
        in_specs=[SMEM_SPEC] + [HBM_SPEC] * (DEPTH + 1) + [ANY_SPEC] * 4 + [VMEM_SPEC] * 3,
        out_specs=[VMEM_SPEC] * (NPOOL + 1),
        scratch_shapes=[
            VMEM((DEPTH, 2, BLOCK, 128), BF16),
            VMEM((NBLK * BLOCK, 128), F32),
            VMEM((table_rows, 256 * STEP_TILES), BF16),
            VMEM((table_rows, 256 * STEP_TILES), BF16),
            VMEM((table_rows, NPOOL * ROWS), F32),
            VMEM((NPOOL, 56, NPOOL * ROWS), F32),
            VMEM((8, NPOOL * ROWS), jnp.int32),
            VMEM((NPOOL, 8, ROWS), BF16),
            pltpu.SemaphoreType.DMA((2, NPOOL)),
            pltpu.SemaphoreType.DMA((DEPTH + 1,)),
        ],
        compiler_params=params(20),
        name="score",
    )(
        place, *[in_hbm(x) for x in ring], *parts,
        wc, ws, weight,
    )
    terms = trade(terms, POOL)

    sums, log_evidence = pl.pallas_call(
        class_kernel,
        out_shape=(
            jax.ShapeDtypeStruct((NBLK, 16, COLS), BF16),
            jax.ShapeDtypeStruct((1, ROWS), F32),
        ),
        in_specs=[SMEM_SPEC] + [VMEM_SPEC] * 7,
        out_specs=(VMEM_SPEC, VMEM_SPEC),
        scratch_shapes=[
            VMEM((NSHIFT * 16, NPOOL * ROWS), F32),
            VMEM((1, NPOOL * ROWS), F32),
        ],
        compiler_params=params(16),
        name="classes",
    )(q, *terms, pool, cosine, sine)
    sums = lax.all_to_all(sums, BLK, 0, 0, tiled=True)

    class_ids = jnp.arange(CLASSES, dtype=jnp.int32)
    shared_owner = class_owner[:, None] == class_owner[None, :]
    earlier = class_ids[:, None] < class_ids[None, :]
    position = jnp.sum((shared_owner & earlier).astype(jnp.int32), axis=0)
    target = class_owner * SLOTS + position
    mine = lax.dynamic_slice(target, (pool_index * QCLS,), (QCLS,))
    mine = jnp.pad(mine, (0, 128 - QCLS), constant_values=-1).reshape(1, 128)
    placed = pl.pallas_call(
        place_kernel,
        out_shape=pltpu.HBM((NDOM, SLOTS, COLS + 128), BF16),
        in_specs=[VMEM_SPEC, VMEM_SPEC],
        out_specs=pl.BlockSpec(memory_space=pltpu.HBM),
        scratch_shapes=[VMEM((NDOM, SLOTS, COLS + 128), BF16), pltpu.SemaphoreType.DMA],
        compiler_params=params(4),
        name="place",
    )(mine, sums)
    placed = lax.all_to_all(placed, DOM, 0, 0, tiled=True)
    means, mass = pl.pallas_call(
        mean_kernel,
        out_shape=(
            jax.ShapeDtypeStruct((SLOTS, COLS), F32),
            jax.ShapeDtypeStruct((SLOTS,), F32),
        ),
        in_specs=[VMEM_SPEC],
        out_specs=(VMEM_SPEC, VMEM_SPEC),
        compiler_params=params(4),
        name="means",
    )(placed)
    return (means, mass, log_evidence.reshape(ROWS))


def solution(mesh):
    fine = Mesh(
        np.asarray(mesh.devices).reshape([size for _, size in FINE]), [name for name, _ in FINE]
    )
    every = DOM + BLK
    return jax.shard_map(
        on_device,
        mesh=fine,
        in_specs=(P(every, None), P(BLK, None, None), P(), P(), P(every, None), P()),
        out_specs=(P(DOM, BLK), P(DOM), P(every)),
        check_vma=False,
    )
```

```python
import math

import jax
import jax.numpy as jnp
import numpy as np
from jax import lax
from jax.experimental import pallas as pl
from jax.experimental.pallas import tpu as pltpu
from jax.sharding import Mesh, PartitionSpec as P

KROW = 64
KCOL = 32
BOX = 256
SLOTS = 8
INV_TEMP = 4.0
FLOOR = -1e30

FINE = (("xh", 2), ("yh", 2), ("yl", 2), ("core", 2), ("z", 8), ("xl", 2))
DOM = ("xh", "yh", "yl", "core")
BLK = ("z", "xl")
POOL = ("yl", "core")

K = 2048
CLASSES = 48
ROT = 12
NSHIFT = 4
ROWS = 128
EXTENDED = 2 * K + 128
NPOOL = 4
QROT = ROT // NPOOL
QCLS = CLASSES // NPOOL
NBLK = 16
NDOM = 16
LOCAL = 3
DEPTH = 8
BLOCK = LOCAL * QROT * 32
COLS = 256
STEP_TILES = 4
F32 = jnp.float32
BF16 = jnp.bfloat16
VMEM = pltpu.VMEM
SMEM_SPEC = pl.BlockSpec(memory_space=pltpu.SMEM)
VMEM_SPEC = pl.BlockSpec(memory_space=pltpu.VMEM)
ANY_SPEC = pl.BlockSpec(memory_space=pl.ANY)
HBM_SPEC = pl.BlockSpec(memory_space=pltpu.HBM)


def params(mib):
    return pltpu.CompilerParams(vmem_limit_bytes=mib << 20)


def pack_kernel(q_ref, cand_ref, refs_ref, particles_hbm, out_ref, extended_ref, wide, rows, sem):
    copy = pltpu.make_async_copy(particles_hbm, extended_ref.at[:, pl.ds(0, 2 * K)], sem)
    copy.start()
    cand = jnp.concatenate([cand_ref[...].astype(F32), jnp.zeros((ROWS - 8, 128), F32)], axis=0)
    extended_ref[:, 2 * K :] = cand.astype(BF16)
    q = q_ref[0]
    wide[...] = refs_ref[...].astype(F32)
    for c in range(LOCAL):
        for r in range(QROT):
            row = wide[c, pl.ds(QROT * q + r, 1), :]
            for a in range(32):
                at = (c * QROT + r) * 32 + a
                rows[at : at + 1, :] = row[:, a * 128 : (a + 1) * 128]
    out_ref[...] = rows[...].astype(BF16)
    copy.wait()


def tables_kernel(off_ref, w_ref, cos_ref, sin_ref, wc_ref, ws_ref):
    row = lax.broadcasted_iota(jnp.int32, (16, 128), 0)
    lane = lax.broadcasted_iota(jnp.int32, (16, 128), 1)
    column = lane % KCOL
    rowpos = row * (128 // KCOL) + lane // KCOL - KROW // 2
    weight = w_ref[...]
    for s in range(NSHIFT):
        turns = (off_ref[s, 0] * column + off_ref[s, 1] * rowpos).astype(F32)
        angle = turns * (2.0 * math.pi / BOX)
        cosine, sine = jnp.cos(angle), jnp.sin(angle)
        at = slice(s * 16, (s + 1) * 16)
        cos_ref[at, :] = cosine
        sin_ref[at, :] = sine
        wc_ref[at, :] = weight * cosine
        ws_ref[at, :] = weight * sine


def pool_copies(q, parts, pool, listed, sem):
    copies = []
    for j, part in enumerate(parts):
        rows = pl.ds(pl.multiple_of((q ^ j) * ROWS, ROWS), ROWS)
        whole = part.at[:, pl.ds(0, 2 * K)]
        copies.append(pltpu.make_async_copy(whole, pool.at[rows, :], sem.at[0, j]))
        few = part.at[pl.ds(0, 8), pl.ds(2 * K, ROWS)]
        copies.append(pltpu.make_async_copy(few, listed.at[j], sem.at[1, j]))
    return copies


def split(x):
    high = x.astype(BF16).astype(F32)
    middle = (x - high).astype(BF16).astype(F32)
    return (high, middle, x - high - middle)


def score_kernel(
    index_ref, *refs
):
    blocks = refs[:DEPTH]
    p0, p1, p2, p3, wc_ref, ws_ref, w_ref = refs[DEPTH : DEPTH + 7]
    own_ref, near_ref, far_ref, cross_ref, pool = refs[DEPTH + 7 : DEPTH + 12]
    stage, wide, table0, table1, scores, groups, cands, listed, sem, block_sem = refs[DEPTH + 12 :]
    q, z, xl = index_ref[0], index_ref[1], index_ref[2]
    block_copies = []
    for k, block in enumerate(blocks):
        block_copies.append(pltpu.make_async_copy(block, stage.at[k], block_sem.at[k]))
    for copy in block_copies:
        copy.start()
    steps = 16 // STEP_TILES
    wide_cols = 128 * STEP_TILES
    copies = pool_copies(q, (p0, p1, p2, p3), pool, listed, sem)
    for copy in copies:
        copy.start()
    for k, copy in enumerate(block_copies):
        copy.wait()
        for side in range(2):
            source = ((z + DEPTH - k) % DEPTH) * 2 + (xl ^ side)
            rows = pl.ds(pl.multiple_of(source * BLOCK, BLOCK), BLOCK)
            wide[rows, :] = stage[k, side].astype(F32)
    energy = [jnp.zeros((CLASSES, 128), F32) for _ in range(QROT)]
    stride = QROT * 32
    tables = (table0, table1)

    def build(step):
        table = tables[step % 2]
        for t in range(STEP_TILES):
            a = step * STEP_TILES + t
            weight = w_ref[a : a + 1, :]
            for r in range(QROT):
                real = wide[pl.ds(r * 32 + a, CLASSES, stride=stride), :]
                imag = wide[pl.ds(r * 32 + 16 + a, CLASSES, stride=stride), :]
                energy[r] = energy[r] + weight * (real * real + imag * imag)
                for s in range(NSHIFT):
                    wc = wc_ref[s * 16 + a : s * 16 + a + 1, :]
                    ws = ws_ref[s * 16 + a : s * 16 + a + 1, :]
                    row = (s * QROT + r) * CLASSES
                    at = slice(t * 128, (t + 1) * 128)
                    at_im = slice(wide_cols + t * 128, wide_cols + (t + 1) * 128)
                    table[row : row + CLASSES, at] = (wc * real - ws * imag).astype(BF16)
                    table[row : row + CLASSES, at_im] = (ws * real + wc * imag).astype(BF16)

    build(0)
    for copy in copies:
        copy.wait()
    for j in range(NPOOL):
        cand = listed[j].astype(F32).astype(jnp.int32)
        cands[:, pl.ds(pl.multiple_of((q ^ j) * ROWS, ROWS), ROWS)] = cand
    for step in range(steps):
        if step + 1 < steps:
            build(step + 1)
        table = tables[step % 2]
        cols = slice(step * wide_cols, (step + 1) * wide_cols)
        cols_im = slice(K + step * wide_cols, K + (step + 1) * wide_cols)
        for n in range(2):
            lanes = slice(n * 256, (n + 1) * 256)
            part = lax.dot_general(
                table[:, 0:wide_cols], pool[lanes, cols], (((1,), (1,)), ((), ())),
                preferred_element_type=F32,
            ) + lax.dot_general(
                table[:, wide_cols:], pool[lanes, cols_im], (((1,), (1,)), ((), ())),
                preferred_element_type=F32,
            )
            if step == 0:
                scores[:, lanes] = part
            else:
                scores[:, lanes] += part

    half_energy = [0.5 * jnp.sum(e, axis=1, keepdims=True) for e in energy]
    class_id = lax.broadcasted_iota(jnp.int32, (CLASSES, 256), 0)
    for n in range(2):
        lanes = slice(n * 256, (n + 1) * 256)
        cand = cands[:, lanes]
        allowed = class_id == cand[0:1, :]
        for k in range(1, 8):
            allowed = allowed | (class_id == cand[k : k + 1, :])
        loglik = []
        for s in range(NSHIFT):
            for r in range(QROT):
                row = (s * QROT + r) * CLASSES
                value = INV_TEMP * (scores[row : row + CLASSES, lanes] - half_energy[r])
                loglik.append(jnp.where(allowed, value, FLOOR))
        top = loglik[0]
        for value in loglik[1:]:
            top = jnp.maximum(top, value)
        peak = jnp.max(top, axis=0, keepdims=True)
        evidence = jnp.zeros((1, 256), F32)
        for s in range(NSHIFT):
            terms = jnp.zeros((CLASSES, 256), F32)
            for r in range(QROT):
                value = loglik[s * QROT + r]
                terms = terms + jnp.where(allowed, jnp.exp(value - peak), 0.0)
            evidence = evidence + jnp.sum(terms, axis=0, keepdims=True)
            for d in range(NPOOL):
                groups[d, s * QCLS : (s + 1) * QCLS, lanes] = terms[d * QCLS : (d + 1) * QCLS]
        pieces = split(peak) + split(evidence)
        for d in range(NPOOL):
            for i, piece in enumerate(pieces):
                groups[d, 48 + i : 49 + i, lanes] = piece
            groups[d, 54:56, lanes] = jnp.zeros((2, 256), F32)
    own_ref[...] = groups[q]
    for j, ref in enumerate((near_ref, far_ref, cross_ref)):
        ref[...] = groups[q ^ (j + 1)].astype(BF16)


def class_kernel(
    q_ref, x0, x1, x2, x3, pool, cos_ref, sin_ref, out_ref, log_ref, slots, line
):
    q = q_ref[0]
    parts = [x[...].astype(F32) for x in (x0, x1, x2, x3)]
    peaks = [x[48:49] + x[49:50] + x[50:51] for x in parts]
    peak = peaks[0]
    for value in peaks[1:]:
        peak = jnp.maximum(peak, value)
    evidence = jnp.zeros_like(peak)
    terms = jnp.zeros((NSHIFT * QCLS, NPOOL * ROWS), F32)
    for x, value in zip(parts, peaks):
        scale = jnp.exp(value - peak)
        evidence = evidence + scale * (x[51:52] + x[52:53] + x[53:54])
        terms = terms + scale * x[0:48]
    line[...] = peak + jnp.log(evidence)
    log_ref[...] = line[:, pl.ds(pl.multiple_of(q * ROWS, ROWS), ROWS)]
    probs = terms / evidence
    for s in range(NSHIFT):
        slots[s * 16 : s * 16 + QCLS, :] = probs[s * QCLS : (s + 1) * QCLS]
        slots[s * 16 + QCLS : (s + 1) * 16, :] = jnp.zeros((4, NPOOL * ROWS), F32)
    padded = slots[...]
    mass = jnp.sum(padded, axis=1, keepdims=True)
    mass = mass[0:16] + mass[16:32] + mass[32:48] + mass[48:64]
    low = padded.astype(BF16)
    row_id = lax.broadcasted_iota(jnp.int32, (16, COLS), 0)
    lane_id = lax.broadcasted_iota(jnp.int32, (16, COLS), 1)
    mass_row = jnp.sum(jnp.where(row_id == lane_id, mass, 0.0), axis=0, keepdims=True)
    mass_high = mass_row.astype(BF16).astype(F32)
    mass_low = mass_row - mass_high
    for b in range(NBLK // 2):
        cols = slice(b * COLS, (b + 1) * COLS)
        cols_im = slice(K + b * COLS, K + (b + 1) * COLS)
        g_re = jnp.dot(low, pool[:, cols], preferred_element_type=F32)
        g_im = jnp.dot(low, pool[:, cols_im], preferred_element_type=F32)
        sum_re = jnp.zeros((16, COLS), F32)
        sum_im = jnp.zeros((16, COLS), F32)
        for s in range(NSHIFT):
            at = s * 16 + 2 * b
            c = jnp.concatenate([cos_ref[at : at + 1, :], cos_ref[at + 1 : at + 2, :]], axis=1)
            z = jnp.concatenate([sin_ref[at : at + 1, :], sin_ref[at + 1 : at + 2, :]], axis=1)
            re = g_re[s * 16 : (s + 1) * 16]
            im = g_im[s * 16 : (s + 1) * 16]
            sum_re = sum_re + (c * re + z * im)
            sum_im = sum_im + (c * im - z * re)
        for dest, value in ((b, sum_re), (NBLK // 2 + b, sum_im)):
            value = jnp.where(row_id == QCLS, mass_high, value)
            value = jnp.where(row_id == QCLS + 1, mass_low, value)
            out_ref[dest] = value.astype(BF16)


def place_kernel(target_ref, y_ref, out_hbm, out_ref, sem):
    total = y_ref[0].astype(F32)
    for b in range(1, NBLK):
        total = total + y_ref[b].astype(F32)
    mass = total[QCLS : QCLS + 1, 0:128] + total[QCLS + 1 : QCLS + 2, 0:128]
    row = lax.broadcasted_iota(jnp.int32, (NDOM * SLOTS, 128), 0)
    hit = target_ref[...] == row
    pick = jnp.where(hit, 1.0, 0.0).astype(BF16)
    placed = jnp.dot(pick[:, 0:16], total.astype(BF16), preferred_element_type=F32)
    placed_mass = jnp.sum(jnp.where(hit, mass, 0.0), axis=1, keepdims=True)
    high = placed_mass.astype(BF16).astype(F32)
    lane = lax.broadcasted_iota(jnp.int32, (NDOM * SLOTS, 128), 1)
    extra = jnp.where(lane == 0, high, jnp.where(lane == 1, placed_mass - high, 0.0))
    out_ref[:, :, 0:COLS] = placed.reshape(NDOM, SLOTS, COLS).astype(BF16)
    out_ref[:, :, COLS:] = extra.reshape(NDOM, SLOTS, 128).astype(BF16)
    send = pltpu.make_async_copy(out_ref, out_hbm, sem)
    send.start()
    send.wait()


def mean_kernel(z_ref, mean_ref, mass_ref):
    total = z_ref[0].astype(F32)
    for d in range(1, NDOM):
        total = total + z_ref[d].astype(F32)
    mass = total[:, COLS : COLS + 1] + total[:, COLS + 1 : COLS + 2]
    mean_ref[...] = total[:, 0:COLS] / (mass + 1.0)
    row = lax.broadcasted_iota(jnp.int32, (SLOTS, 128), 0)
    lane = lax.broadcasted_iota(jnp.int32, (SLOTS, 128), 1)
    mass_ref[...] = jnp.sum(jnp.where(row == lane, mass, 0.0), axis=0)[0:SLOTS]


def in_hbm(x):
    return pltpu.with_memory_space_constraint(x, pltpu.HBM)


def swap(x, axis):
    return lax.ppermute(x, axis, [(0, 1), (1, 0)])


def turn(x, step):
    return lax.ppermute(x, "z", [(i, (i + step) % DEPTH) for i in range(DEPTH)])


def trade(parts, axes):
    own, near, far, cross = parts
    return (
        own,
        swap(near, axes[1]),
        swap(far, axes[0]),
        lax.ppermute(cross, axes, [(i, 3 - i) for i in range(4)]),
    )


def on_device(particles, references, noise_weight, offsets, candidates, class_owner):
    pool_index = (lax.axis_index("yl") * 2 + lax.axis_index("core")).astype(jnp.int32)
    q = pool_index.reshape(1)

    zi, xi = lax.axis_index("z").astype(jnp.int32), lax.axis_index("xl").astype(jnp.int32)
    place = jnp.stack([pool_index, zi, xi])
    weight = noise_weight.reshape(16, 128)
    packed, particles = pl.pallas_call(
        pack_kernel,
        out_shape=(
            jax.ShapeDtypeStruct((BLOCK, 128), BF16),
            jax.ShapeDtypeStruct((ROWS, EXTENDED), BF16),
        ),
        in_specs=[SMEM_SPEC, VMEM_SPEC, VMEM_SPEC, HBM_SPEC],
        out_specs=(VMEM_SPEC, VMEM_SPEC),
        scratch_shapes=[
            VMEM((LOCAL, ROT, 2 * K), F32),
            VMEM((BLOCK, 128), F32),
            pltpu.SemaphoreType.DMA,
        ],
        compiler_params=params(8),
        name="pack",
    )(q, in_hbm(candidates.T), in_hbm(references), in_hbm(particles))
    far = swap(particles, "yl")
    ring = [None] * DEPTH
    near, beside = lax.optimization_barrier((swap(particles, "core"), swap(packed, "xl")))
    ring[0] = up = down = jnp.stack([packed, beside])
    for k in range(1, DEPTH // 2):
        ring[k] = up = turn(up, 1)
        ring[DEPTH - k] = down = turn(down, -1)
    ring[DEPTH // 2] = turn(up, 1)
    flat = jax.ShapeDtypeStruct((NSHIFT * 16, 128), F32)
    cosine, sine, wc, ws = pl.pallas_call(
        tables_kernel,
        out_shape=(flat, flat, flat, flat),
        in_specs=[SMEM_SPEC, VMEM_SPEC],
        out_specs=(VMEM_SPEC,) * 4,
        compiler_params=params(4),
        cost_estimate=pl.CostEstimate(flops=1 * 10**9, bytes_accessed=3 * 10**6, transcendentals=0),
        name="tables",
    )(offsets, weight)
    far, wc, ring = lax.optimization_barrier((far, wc, ring))
    parts = (particles, near, far, swap(far, "core"))
    table_rows = NSHIFT * QROT * CLASSES
    *terms, pool = pl.pallas_call(
        score_kernel,
        out_shape=[
            jax.ShapeDtypeStruct((56, NPOOL * ROWS), F32 if j == 0 else BF16) for j in range(NPOOL)
        ]
        + [jax.ShapeDtypeStruct((NPOOL * ROWS, 2 * K), BF16)],
        in_specs=[SMEM_SPEC] + [HBM_SPEC] * DEPTH + [ANY_SPEC] * 4 + [VMEM_SPEC] * 3,
        out_specs=[VMEM_SPEC] * (NPOOL + 1),
        scratch_shapes=[
            VMEM((DEPTH, 2, BLOCK, 128), BF16),
            VMEM((NBLK * BLOCK, 128), F32),
            VMEM((table_rows, 256 * STEP_TILES), BF16),
            VMEM((table_rows, 256 * STEP_TILES), BF16),
            VMEM((table_rows, NPOOL * ROWS), F32),
            VMEM((NPOOL, 56, NPOOL * ROWS), F32),
            VMEM((8, NPOOL * ROWS), jnp.int32),
            VMEM((NPOOL, 8, ROWS), BF16),
            pltpu.SemaphoreType.DMA((2, NPOOL)),
            pltpu.SemaphoreType.DMA((DEPTH,)),
        ],
        compiler_params=params(20),
        name="score",
    )(
        place, *[in_hbm(x) for x in ring], *parts,
        wc, ws, weight,
    )
    terms = trade(terms, POOL)

    sums, log_evidence = pl.pallas_call(
        class_kernel,
        out_shape=(
            jax.ShapeDtypeStruct((NBLK, 16, COLS), BF16),
            jax.ShapeDtypeStruct((1, ROWS), F32),
        ),
        in_specs=[SMEM_SPEC] + [VMEM_SPEC] * 7,
        out_specs=(VMEM_SPEC, VMEM_SPEC),
        scratch_shapes=[
            VMEM((NSHIFT * 16, NPOOL * ROWS), F32),
            VMEM((1, NPOOL * ROWS), F32),
        ],
        compiler_params=params(16),
        name="classes",
    )(q, *terms, pool, cosine, sine)
    sums = lax.all_to_all(sums, BLK, 0, 0, tiled=True)

    class_ids = jnp.arange(CLASSES, dtype=jnp.int32)
    shared_owner = class_owner[:, None] == class_owner[None, :]
    earlier = class_ids[:, None] < class_ids[None, :]
    position = jnp.sum((shared_owner & earlier).astype(jnp.int32), axis=0)
    target = class_owner * SLOTS + position
    mine = lax.dynamic_slice(target, (pool_index * QCLS,), (QCLS,))
    mine = jnp.pad(mine, (0, 128 - QCLS), constant_values=-1).reshape(1, 128)
    placed = pl.pallas_call(
        place_kernel,
        out_shape=pltpu.HBM((NDOM, SLOTS, COLS + 128), BF16),
        in_specs=[VMEM_SPEC, VMEM_SPEC],
        out_specs=pl.BlockSpec(memory_space=pltpu.HBM),
        scratch_shapes=[VMEM((NDOM, SLOTS, COLS + 128), BF16), pltpu.SemaphoreType.DMA],
        compiler_params=params(4),
        name="place",
    )(mine, sums)
    placed = lax.all_to_all(placed, DOM, 0, 0, tiled=True)
    means, mass = pl.pallas_call(
        mean_kernel,
        out_shape=(
            jax.ShapeDtypeStruct((SLOTS, COLS), F32),
            jax.ShapeDtypeStruct((SLOTS,), F32),
        ),
        in_specs=[VMEM_SPEC],
        out_specs=(VMEM_SPEC, VMEM_SPEC),
        compiler_params=params(4),
        name="means",
    )(placed)
    return (means, mass, log_evidence.reshape(ROWS))


def solution(mesh):
    fine = Mesh(
        np.asarray(mesh.devices).reshape([size for _, size in FINE]), [name for name, _ in FINE]
    )
    every = DOM + BLK
    return jax.shard_map(
        on_device,
        mesh=fine,
        in_specs=(P(every, None), P(BLK, None, None), P(), P(), P(every, None), P()),
        out_specs=(P(DOM, BLK), P(DOM), P(every)),
        check_vma=False,
    )
```
